128 devices in a mesh: theta: 16 (over z, x_hi, core), gz: 8 (over x_lo, y).
Axes of the slice: x: 4 (x_hi: 2, x_lo: 2; x = x_hi * 2 + x_lo), y: 4, z: 4, core: 2. Of those that a mesh axis runs over, the one named last changes fastest.
Arguments:
- velocity: float32 [3, 512, 256, 128], P(None, 'theta', 'gz'), may hold values from -3 to 3
Outputs:
- viscosity_ratio: float32 [512, 256, 128], P('theta', 'gz')
- pressure_modes: float32 [2, 512, 256, 128], P(None, 'gz', 'theta')
The draws below stay inside these ranges and needn't reach their ends.
All inputs are finite; a program needn't handle non-finite values.
Results may differ from the reference program's by a relative error of at most 0.0003.
Values sent between devices are 32-bit elements; how exact they have to be, the bound alone decides.
A program may use at most 128 MiB of HBM per device.

```python
import math
import jax
import jax.numpy as jnp
from jax import lax

NTH = 512
NZ = 256
NR = 128


def draw_velocity(key, part):
    keys = jax.random.split(jax.random.fold_in(key, 11), 3)
    shape = (3, NTH, NZ, NR)
    theta_pos = (jnp.arange(NTH, dtype=jnp.float32) / NTH)[:, None, None]
    axial_pos = (jnp.arange(NZ, dtype=jnp.float32) / NZ)[None, :, None]
    radius = ((jnp.arange(NR, dtype=jnp.float32) + 0.5) / NR)[None, None, :]
    noise = jnp.clip(jax.random.normal(keys[0], shape, jnp.float32), -5.0, 5.0)
    swirl = 0.0
    rough = jnp.exp(jax.random.uniform(keys[1], shape, jnp.float32, -0.45, 0.45))
    phase = jax.random.uniform(keys[2], (3, 1, 1, 1), jnp.float32, 0.0, 2.0 * math.pi)
    wave = jnp.cos(2.0 * math.pi * (3.0 * theta_pos + 2.0 * axial_pos) + phase) * jnp.sin(math.pi * radius)
    amplitude = 0.02 * (1.0 + 2.0 * theta_pos) * (1.0 + 2.0 * axial_pos) * radius
    fluctuation = amplitude * (noise * rough + 2.0 * theta_pos * wave)
    ones = jnp.ones((1, NTH, NZ, NR), jnp.float32)
    mean = jnp.concatenate([0.0 * ones, swirl * radius * ones, (1.0 - radius ** 2) * ones], axis=0)
    return fluctuation + mean


def setup_inputs(seed: int = 0) -> dict:
    key_list = jax.random.split(jax.random.key(seed), 2)
    return {
        "velocity": draw_velocity(jax.random.fold_in(key_list[1], 71), 0),
    }


pipe_length = 4.0 * math.pi
nu_molecular = 5e-05
time_step = 2.0
filter_ratio = 4.0
epsilon_den = 1e-06
pair_first = (0, 1, 2, 0, 0, 1)
pair_second = (0, 1, 2, 1, 2, 2)

def grid_terms():
    radial_step = 1.0 / NR
    radius = (jnp.arange(NR, dtype=jnp.float32) + 0.5) * radial_step
    theta_step = 2.0 * math.pi / NTH
    axial_step = pipe_length / NZ
    width_sq = jnp.cbrt(radial_step * radius * theta_step * axial_step) ** 2
    return (radius, width_sq)

def along_theta(padded):
    return (padded[..., 2:, 1:-1, :] - padded[..., :-2, 1:-1, :]) * (0.5 * NTH / (2.0 * math.pi))

def along_axis(padded):
    return (padded[..., 1:-1, 2:, :] - padded[..., 1:-1, :-2, :]) * (0.5 * NZ / pipe_length)

def along_radius(field):
    zeros = jnp.zeros(field.shape[:-1] + (1,), field.dtype)
    extended = jnp.concatenate([zeros, field, zeros], axis=-1)
    return (extended[..., 2:] - extended[..., :-2]) * (0.5 * NR)

def interior(padded):
    return padded[..., 1:-1, 1:-1, :]

def strain(padded, radius):
    centre = interior(padded)
    radial = along_radius(centre)
    azimuthal = along_theta(padded) / radius
    axial = along_axis(padded)
    return jnp.stack([radial[0], azimuthal[1] + centre[0] / radius, axial[2], 0.5 * (radial[1] - centre[1] / radius + azimuthal[0]), 0.5 * (axial[0] + radial[2]), 0.5 * (azimuthal[2] + axial[1])])

def magnitude(tensor):
    return jnp.sqrt(2.0 * (tensor[0] ** 2 + tensor[1] ** 2 + tensor[2] ** 2) + 4.0 * (tensor[3] ** 2 + tensor[4] ** 2 + tensor[5] ** 2))

def test_filter(padded):
    across = 0.25 * padded[..., :-2, :, :] + 0.5 * padded[..., 1:-1, :, :] + 0.25 * padded[..., 2:, :, :]
    return 0.25 * across[..., :, :-2, :] + 0.5 * across[..., :, 1:-1, :] + 0.25 * across[..., :, 2:, :]

def products(flow, tensor):
    pairs = jnp.stack([flow[first_comp] * flow[second_comp] for first_comp, second_comp in zip(pair_first, pair_second)])
    return jnp.concatenate([flow, pairs, tensor, magnitude(tensor) * tensor], axis=0)

def germano(filtered, width_sq):
    means = filtered[0:3]
    pairs = jnp.stack([means[first_comp] * means[second_comp] for first_comp, second_comp in zip(pair_first, pair_second)])
    leonard = filtered[3:9] - pairs
    smooth = filtered[9:15]
    model = 2.0 * width_sq * (filter_ratio * magnitude(smooth) * smooth - filtered[15:21])
    weights = jnp.array([1.0, 1.0, 1.0, 2.0, 2.0, 2.0], dtype=jnp.float32)[:, None, None, None]
    return (lax.optimization_barrier(jnp.sum(weights * leonard * model, axis=(0, 1, 2))), lax.optimization_barrier(jnp.sum(weights * model * model, axis=(0, 1, 2))))

def divergence(stress, radius):
    centre = interior(stress)
    radial = along_radius(centre)
    azimuthal = along_theta(stress) / radius
    axial = along_axis(stress)
    return jnp.stack([radial[0] + azimuthal[3] + axial[4] + (centre[0] - centre[1]) / radius, radial[3] + azimuthal[1] + axial[5] + 2.0 * centre[3] / radius, radial[4] + azimuthal[5] + axial[2] + centre[4] / radius])

def continuity(padded, radius):
    centre = interior(padded)
    return along_radius(radius * centre[0]) / radius + along_theta(padded[1]) / radius + along_axis(padded[2])

def mode_solve(real_part, imag_part, theta_modes, axial_modes, radius):
    radial_step = 1.0 / NR
    lower = (radius - 0.5 * radial_step) / radius * (NR * NR)
    upper = (radius + 0.5 * radial_step) / radius * (NR * NR)
    last = jnp.arange(NR, dtype=jnp.int32) == NR - 1
    centre = -(lower + upper) - jnp.where(last, upper, 0.0)
    upper = jnp.where(last, 0.0, upper)
    theta_wave = jnp.minimum(theta_modes, NTH - theta_modes).astype(jnp.float32)
    axial_wave = jnp.minimum(axial_modes, NZ - axial_modes).astype(jnp.float32) * (2.0 * math.pi / pipe_length)
    diagonal = centre - (theta_wave[:, None, None] / radius) ** 2 - axial_wave[None, :, None] ** 2
    shape = diagonal.shape
    solved = lax.linalg.tridiagonal_solve(jnp.broadcast_to(lower, shape), diagonal, jnp.broadcast_to(upper, shape), jnp.stack([real_part, imag_part], axis=-1))
    return jnp.moveaxis(solved, -1, 0)

def reference(velocity):
    radius, width_sq = grid_terms()
    slab_count = 8
    slab_len = NZ // slab_count
    padded = jnp.pad(velocity, ((0, 0), (3, 3), (3, 3), (0, 0)), mode='wrap')
    starts = jnp.arange(slab_count, dtype=jnp.int32) * slab_len

    def shell_terms(start):
        piece = lax.dynamic_slice_in_dim(padded, start + 1, slab_len + 4, axis=2)[:, 1:-1]
        tensor = strain(piece, radius)
        filtered = test_filter(products(interior(piece), tensor))
        return germano(filtered, width_sq)
    numer, denom = lax.map(shell_terms, starts)
    coefficient = lax.optimization_barrier(jnp.sum(numer, axis=0)) / (lax.optimization_barrier(jnp.sum(denom, axis=0)) + epsilon_den)

    def source_terms(start):
        piece = lax.dynamic_slice_in_dim(padded, start, slab_len + 6, axis=2)
        tensor = strain(piece, radius)
        eddy = coefficient * width_sq * magnitude(tensor)
        stress = 2.0 * (nu_molecular + eddy) * tensor
        star = interior(interior(piece)) + time_step * divergence(stress, radius)
        return (continuity(star, radius), interior(interior(eddy)) / nu_molecular)
    sources, ratios = lax.map(source_terms, starts)
    source = jnp.moveaxis(sources, 0, 1).reshape(NTH, NZ, NR)
    ratio = jnp.moveaxis(ratios, 0, 1).reshape(NTH, NZ, NR)
    spectrum = jnp.fft.fft2(source, axes=(0, 1)) / math.sqrt(NTH * NZ)
    pressure = mode_solve(jnp.real(spectrum).astype(jnp.float32), jnp.imag(spectrum).astype(jnp.float32), jnp.arange(NTH, dtype=jnp.int32), jnp.arange(NZ, dtype=jnp.int32), radius)
    return (ratio, pressure)
```

```python
import functools
import math

import jax
import jax.numpy as jnp
import ml_dtypes
import numpy as np
from jax import lax
from jax.experimental import pallas as pl
from jax.experimental.pallas import tpu as pltpu
from jax.sharding import PartitionSpec as P

NTH = 512
NZ = 256
NR = 128


pipe_length = 4.0 * math.pi
nu_molecular = 5e-05
time_step = 2.0
filter_ratio = 4.0
epsilon_den = 1e-06
pair_first = (0, 1, 2, 0, 0, 1)
pair_second = (0, 1, 2, 1, 2, 2)


def with_halo(block, sides, width):
    for axis, dim in sides:
        count = lax.axis_size(axis)
        forward = [(i, i + 1) for i in range(count - 1)]
        forward.append((count - 1, 0))
        backward = [(target, source) for source, target in forward]
        low = lax.ppermute(
            lax.slice_in_dim(block, block.shape[dim] - width, None, axis=dim), axis, forward
        )
        high = lax.ppermute(lax.slice_in_dim(block, 0, width, axis=dim), axis, backward)
        block = jnp.concatenate([low, block, high], axis=dim)
    return block


def grid_terms():
    radial_step = 1.0 / NR
    radius = (jnp.arange(NR, dtype=jnp.float32) + 0.5) * radial_step
    theta_step = 2.0 * math.pi / NTH
    axial_step = pipe_length / NZ
    width_sq = jnp.cbrt(radial_step * radius * theta_step * axial_step) ** 2
    return (radius, width_sq)


def along_theta(padded):
    return (padded[..., 2:, 1:-1, :] - padded[..., :-2, 1:-1, :]) * (0.5 * NTH / (2.0 * math.pi))


def along_axis(padded):
    return (padded[..., 1:-1, 2:, :] - padded[..., 1:-1, :-2, :]) * (0.5 * NZ / pipe_length)


def along_radius(field):
    zeros = jnp.zeros(field.shape[:-1] + (1,), field.dtype)
    extended = jnp.concatenate([zeros, field, zeros], axis=-1)
    return (extended[..., 2:] - extended[..., :-2]) * (0.5 * NR)


def interior(padded):
    return padded[..., 1:-1, 1:-1, :]


def strain(padded, radius):
    centre = interior(padded)
    radial = along_radius(centre)
    azimuthal = along_theta(padded) / radius
    axial = along_axis(padded)
    return jnp.stack(
        [
            radial[0],
            azimuthal[1] + centre[0] / radius,
            axial[2],
            0.5 * (radial[1] - centre[1] / radius + azimuthal[0]),
            0.5 * (axial[0] + radial[2]),
            0.5 * (azimuthal[2] + axial[1]),
        ]
    )


def magnitude(tensor):
    return jnp.sqrt(
        2.0 * (tensor[0] ** 2 + tensor[1] ** 2 + tensor[2] ** 2)
        + 4.0 * (tensor[3] ** 2 + tensor[4] ** 2 + tensor[5] ** 2)
    )


def test_filter(padded):
    across = (
        0.25 * padded[..., :-2, :, :] + 0.5 * padded[..., 1:-1, :, :] + 0.25 * padded[..., 2:, :, :]
    )
    return (
        0.25 * across[..., :, :-2, :] + 0.5 * across[..., :, 1:-1, :] + 0.25 * across[..., :, 2:, :]
    )


def products(flow, tensor):
    pairs = jnp.stack(
        [
            flow[first_comp] * flow[second_comp]
            for first_comp, second_comp in zip(pair_first, pair_second)
        ]
    )
    return jnp.concatenate([flow, pairs, tensor, magnitude(tensor) * tensor], axis=0)


def germano(filtered, width_sq):
    means = filtered[0:3]
    pairs = jnp.stack(
        [
            means[first_comp] * means[second_comp]
            for first_comp, second_comp in zip(pair_first, pair_second)
        ]
    )
    leonard = filtered[3:9] - pairs
    smooth = filtered[9:15]
    model = 2.0 * width_sq * (filter_ratio * magnitude(smooth) * smooth - filtered[15:21])
    weights = jnp.array([1.0, 1.0, 1.0, 2.0, 2.0, 2.0], dtype=jnp.float32)[:, None, None, None]
    return (
        jnp.sum(weights * leonard * model, axis=(0, 1, 2)),
        jnp.sum(weights * model * model, axis=(0, 1, 2)),
    )


def divergence(stress, radius):
    centre = interior(stress)
    radial = along_radius(centre)
    azimuthal = along_theta(stress) / radius
    axial = along_axis(stress)
    return jnp.stack(
        [
            radial[0] + azimuthal[3] + axial[4] + (centre[0] - centre[1]) / radius,
            radial[3] + azimuthal[1] + axial[5] + 2.0 * centre[3] / radius,
            radial[4] + azimuthal[5] + axial[2] + centre[4] / radius,
        ]
    )


def continuity(padded, radius):
    centre = interior(padded)
    return (
        along_radius(radius * centre[0]) / radius
        + along_theta(padded[1]) / radius
        + along_axis(padded[2])
    )


THETA_COUNT = 16
GZ_COUNT = 8
DEVICES = THETA_COUNT * GZ_COUNT
LOCAL_T = NTH // THETA_COUNT
LOCAL_Z = NZ // GZ_COUNT
LOCAL_M = NTH // GZ_COUNT
LOCAL_K = NZ // THETA_COUNT
MESH_ID = pl.DeviceIdType.MESH
HALF = NR // 2


def split_table(table):
    parts, rest = [], table
    for _ in range(3):
        part = rest.astype(np.float32).astype(ml_dtypes.bfloat16)
        parts.append(part)
        rest = rest - part.astype(np.float64)
    return np.stack(parts)


def axial_table():
    order = np.arange(NZ)
    block, rest = order // LOCAL_Z, order % LOCAL_Z
    cells = block * LOCAL_Z + 4 * (rest % 8) + rest // 8
    angle = 2.0 * np.pi * ((np.arange(NZ)[:, None] * cells[None, :]) % NZ) / NZ
    return split_table(np.concatenate([np.cos(angle), np.sin(angle)], axis=0))


def cycle_table():
    angle = 2.0 * np.pi * ((np.arange(NTH)[:, None] * np.arange(NTH)[None, :]) % NTH) / NTH
    scale = 1.0 / math.sqrt(NTH * NZ)
    cosine = (np.cos(angle) * scale).reshape(NTH, GZ_COUNT, LOCAL_M)
    sine = (np.sin(angle) * scale).reshape(NTH, GZ_COUNT, LOCAL_M)
    upper = np.stack([cosine, -sine], axis=2)
    lower = np.stack([-sine, -cosine], axis=2)
    both = np.concatenate([upper, lower], axis=0).reshape(2 * NTH, GZ_COUNT // 2, 4 * LOCAL_M)
    return split_table(np.moveaxis(both, 1, 0))


def split_value(value):
    parts = []
    for _ in range(3):
        part = value.astype(jnp.bfloat16)
        parts.append(part)
        value = value - part.astype(jnp.float32)
    return parts


def product(left, right):
    total = None
    for i, j in ((0, 2), (2, 0), (1, 1), (0, 1), (1, 0), (0, 0)):
        term = jnp.dot(left[i], right[j], preferred_element_type=jnp.float32)
        total = term if total is None else total + term
    return total


def wait_bytes(ref, sem):
    pltpu.make_async_copy(ref, ref, sem).wait()


def meet_all(row, column, barrier, second):
    def greet_row(i, carry):
        pl.semaphore_signal(
            barrier,
            inc=1,
            device_id={"theta": lax.rem(row + i, THETA_COUNT), "gz": column},
            device_id_type=MESH_ID,
        )
        return carry

    def greet_column(sem):
        def greet(i, carry):
            pl.semaphore_signal(
                sem,
                inc=1,
                device_id={"theta": row, "gz": lax.rem(column + i, GZ_COUNT)},
                device_id_type=MESH_ID,
            )
            return carry

        return greet

    lax.fori_loop(1, THETA_COUNT, greet_row, 0)
    lax.fori_loop(1, GZ_COUNT, greet_column(barrier), 0)
    pl.semaphore_wait(barrier, THETA_COUNT + GZ_COUNT - 2)
    lax.fori_loop(1, GZ_COUNT, greet_column(second), 0)
    pl.semaphore_wait(second, GZ_COUNT - 1)


def spectral_kernel(
    tiles_ref,
    axial_hbm,
    cycle_hbm,
    modes_ref,
    planes,
    plane,
    axial,
    cycle,
    left,
    spectrum,
    second,
    table_sem,
    send_sem,
    recv_sem,
    out_send_sem,
    out_recv_sem,
    own_sem,
):
    row, column = lax.axis_index("theta"), lax.axis_index("gz")
    me = row * GZ_COUNT + column
    fetch_axial = pltpu.make_async_copy(axial_hbm, axial, table_sem.at[0])
    fetch_cycle = pltpu.make_async_copy(cycle_hbm, cycle, table_sem.at[1])
    fetch_axial.start()
    fetch_cycle.start()
    meet_all(row, column, pltpu.get_barrier_semaphore(), second)

    def send_tile(i, carry):
        target = lax.rem(me + i, DEVICES)
        pltpu.make_async_remote_copy(
            src_ref=tiles_ref.at[target],
            dst_ref=planes.at[me],
            send_sem=send_sem,
            recv_sem=recv_sem,
            device_id={"theta": target // GZ_COUNT, "gz": lax.rem(target, GZ_COUNT)},
            device_id_type=MESH_ID,
        ).start()
        return carry

    lax.fori_loop(1, DEVICES, send_tile, 0)
    planes[me] = tiles_ref[me]
    wait_bytes(planes.at[pl.ds(0, DEVICES - 1)], recv_sem)
    wait_bytes(planes.at[pl.ds(0, DEVICES - 1)], send_sem)

    group = lax.broadcasted_iota(jnp.int32, (8, 128), 1) // LOCAL_T

    def gather_lines(c, carry):
        for quad in range(THETA_COUNT // 4):
            parts = [planes[(4 * quad + b) * GZ_COUNT + c] for b in range(4)]
            for z in range(4):
                turned = [
                    parts[b] if b == z else pltpu.roll(parts[b], ((b - z) * LOCAL_T) % 128, 1)
                    for b in range(4)
                ]
                value = jnp.where(
                    group < 2,
                    jnp.where(group == 0, turned[0], turned[1]),
                    jnp.where(group == 2, turned[2], turned[3]),
                )
                start = pl.multiple_of(c * LOCAL_Z + 8 * z, 8)
                plane[pl.ds(start, 8), 128 * quad : 128 * quad + 128] = value
        return carry

    lax.fori_loop(0, GZ_COUNT, gather_lines, 0)
    fetch_axial.wait()
    lines = product(axial, split_value(plane[...]))
    for n, part in enumerate(split_value(lines)):
        left[n, :, :NTH] = part[:NZ]
        left[n, :, NTH:] = part[NZ:]
    fetch_cycle.wait()

    def transform(step, carry):
        pair = lax.rem(column // 2 + step, GZ_COUNT // 2)
        both = product(left, cycle.at[:, pair])
        spectrum[2 * pair] = both[:, :128]
        spectrum[2 * pair + 1] = both[:, 128:]

        def send_modes(i, inner):
            target_column = 2 * pair + lax.rem(column + i // THETA_COUNT, 2)
            target_row = lax.rem(row + i, THETA_COUNT)
            rows = pl.ds(pl.multiple_of(target_row * LOCAL_K, LOCAL_K), LOCAL_K)

            @pl.when(jnp.logical_or(target_row != row, target_column != column))
            def _():
                pltpu.make_async_remote_copy(
                    src_ref=spectrum.at[target_column, rows],
                    dst_ref=modes_ref.at[me],
                    send_sem=out_send_sem,
                    recv_sem=out_recv_sem,
                    device_id={"theta": target_row, "gz": target_column},
                    device_id_type=MESH_ID,
                ).start()

            return inner

        lax.fori_loop(0, 2 * THETA_COUNT, send_modes, 0)
        return carry

    lax.fori_loop(0, GZ_COUNT // 2, transform, 0)
    own_rows = pl.ds(pl.multiple_of(row * LOCAL_K, LOCAL_K), LOCAL_K)
    keep = pltpu.make_async_copy(spectrum.at[column, own_rows], modes_ref.at[me], own_sem)
    keep.start()
    keep.wait()
    wait_bytes(modes_ref.at[pl.ds(0, DEVICES - 1)], out_send_sem)
    wait_bytes(modes_ref.at[pl.ds(0, DEVICES - 1)], out_recv_sem)


def spectral(tiles):
    any_space = pl.BlockSpec(memory_space=pl.ANY)
    return pl.pallas_call(
        spectral_kernel,
        out_shape=jax.ShapeDtypeStruct((DEVICES, LOCAL_K, 128), jnp.float32),
        in_specs=[pl.BlockSpec(memory_space=pltpu.VMEM), any_space, any_space],
        out_specs=any_space,
        scratch_shapes=[
            pltpu.VMEM((DEVICES, 8, 128), jnp.float32),
            pltpu.VMEM((NZ, NTH), jnp.float32),
            pltpu.VMEM((3, 2 * NZ, NZ), jnp.bfloat16),
            pltpu.VMEM((3, GZ_COUNT // 2, 2 * NTH, 4 * LOCAL_M), jnp.bfloat16),
            pltpu.VMEM((3, NZ, 2 * NTH), jnp.bfloat16),
            pltpu.VMEM((GZ_COUNT, NZ, 128), jnp.float32),
            pltpu.SemaphoreType.REGULAR,
            pltpu.SemaphoreType.DMA((2,)),
            pltpu.SemaphoreType.DMA,
            pltpu.SemaphoreType.DMA,
            pltpu.SemaphoreType.DMA,
            pltpu.SemaphoreType.DMA,
            pltpu.SemaphoreType.DMA,
        ],
        compiler_params=pltpu.CompilerParams(
            collective_id=0, has_side_effects=True, vmem_limit_bytes=48 << 20
        ),
        name="spectral",
    )(tiles, jnp.asarray(axial_table()), jnp.asarray(cycle_table()))


def solve_kernel(modes_ref, out_ref, inverse, partial, pressure):
    row, column = lax.axis_index("theta"), lax.axis_index("gz")
    shape = (LOCAL_K, 128)
    theta_mode = column * LOCAL_M + lax.broadcasted_iota(jnp.int32, shape, 1) % LOCAL_M
    axial_mode = row * LOCAL_K + lax.broadcasted_iota(jnp.int32, shape, 0)
    theta_wave = jnp.minimum(theta_mode, NTH - theta_mode).astype(jnp.float32)
    axial_wave = jnp.minimum(axial_mode, NZ - axial_mode).astype(jnp.float32) * (
        2.0 * math.pi / pipe_length
    )
    theta_sq = theta_wave * theta_wave
    axial_sq = axial_wave * axial_wave * (1.0 / (NR * NR))

    def diagonal(i):
        middle = i + 0.5
        extra = float(NR) if i == NR - 1 else 0.0
        return theta_sq * (1.0 / middle) + (axial_sq * middle + (2.0 * i + 1.0 + extra))

    def load(i):
        return modes_ref[i] * (-(i + 0.5) / (NR * NR))

    low_diag, low_value = diagonal(0), load(0)
    high_diag, high_value = diagonal(NR - 1), load(NR - 1)
    for step in range(1, HALF):
        i = step
        low_inverse = 1.0 / low_diag
        inverse[i - 1] = low_inverse
        partial[i - 1] = low_value
        low_value = load(i) + (low_inverse * float(i)) * low_value
        low_diag = diagonal(i) - low_inverse * float(i * i)
        j = NR - 1 - step
        high_inverse = 1.0 / high_diag
        inverse[j + 1] = high_inverse
        partial[j + 1] = high_value
        high_value = load(j) + (high_inverse * float(j + 1)) * high_value
        high_diag = diagonal(j) - high_inverse * float((j + 1) * (j + 1))
    scale = 1.0 / (low_diag * high_diag - float(HALF * HALF))
    low = (low_value * high_diag + float(HALF) * high_value) * scale
    high = (high_value * low_diag + float(HALF) * low_value) * scale
    pressure[HALF - 1] = low
    pressure[HALF] = high
    for step in range(1, HALF):
        i = HALF - 1 - step
        low = (partial[i] + float(i + 1) * low) * inverse[i]
        pressure[i] = low
        j = HALF + step
        high = (partial[j] + float(j) * high) * inverse[j]
        pressure[j] = high
    for k in range(LOCAL_K):
        out_ref[:, k, :] = pressure[:, k, :].T


def solve(modes):
    vmem = pl.BlockSpec(memory_space=pltpu.VMEM)
    out = pl.pallas_call(
        solve_kernel,
        out_shape=jax.ShapeDtypeStruct((2 * LOCAL_M, LOCAL_K, NR), jnp.float32),
        in_specs=[vmem],
        out_specs=vmem,
        scratch_shapes=[pltpu.VMEM((NR, LOCAL_K, 128), jnp.float32)] * 3,
        compiler_params=pltpu.CompilerParams(vmem_limit_bytes=32 << 20),
        name="solve",
    )(modes)
    return out.reshape(2, LOCAL_M, LOCAL_K, NR)


def body(velocity):
    radius, width_sq = grid_terms()
    wide_faces = None
    wide_faces = with_halo(velocity, (("theta", 1), ("gz", 2)), 3)
    tensor_wide = strain(wide_faces, radius)
    tensor_cycle = interior(tensor_wide)
    filtered = test_filter(products(interior(interior(wide_faces)), tensor_cycle))
    tensor = interior(tensor_cycle)
    numer, denom = germano(filtered, width_sq)
    numer, denom = lax.psum((numer, denom), ("theta", "gz"))
    coefficient = numer / (denom + epsilon_den)
    eddy = coefficient * width_sq * magnitude(tensor)
    stress = 2.0 * (nu_molecular + coefficient * width_sq * magnitude(tensor_wide)) * tensor_wide
    predicted_cycle = interior(interior(wide_faces)) + time_step * divergence(stress, radius)
    source = continuity(predicted_cycle, radius)
    tiles = source.reshape(LOCAL_T, 8, 4, NR).transpose(3, 1, 2, 0).reshape(NR, 8, 128)
    pressure = solve(spectral(tiles))
    return (eddy / nu_molecular, pressure)


def solution(mesh):
    return jax.shard_map(
        body,
        mesh=mesh,
        in_specs=(P(None, "theta", "gz", None),),
        out_specs=(P("theta", "gz", None), P(None, "gz", "theta", None)),
        check_vma=False,
    )
```

```python
import functools
import math

import jax
import jax.numpy as jnp
import ml_dtypes
import numpy as np
from jax import lax
from jax.experimental import pallas as pl
from jax.experimental.pallas import tpu as pltpu
from jax.sharding import PartitionSpec as P

NTH = 512
NZ = 256
NR = 128


pipe_length = 4.0 * math.pi
nu_molecular = 5e-05
time_step = 2.0
filter_ratio = 4.0
epsilon_den = 1e-06
pair_first = (0, 1, 2, 0, 0, 1)
pair_second = (0, 1, 2, 1, 2, 2)


THETA_COUNT = 16
GZ_COUNT = 8
DEVICES = THETA_COUNT * GZ_COUNT
LOCAL_T = NTH // THETA_COUNT
LOCAL_Z = NZ // GZ_COUNT
LOCAL_M = NTH // GZ_COUNT
LOCAL_K = NZ // THETA_COUNT
MESH_ID = pl.DeviceIdType.MESH
HALF = NR // 2


def wait_bytes(ref, sem):
    pltpu.make_async_copy(ref, ref, sem).wait()


T_ROWS = LOCAL_T + 6
Z_BASE = 8
Z_ROWS = LOCAL_Z + 2 * Z_BASE
Z_STEP = LOCAL_Z // 8
S_ROWS = LOCAL_T + 4
S_COLS = Z_STEP + 4
DT = 0.5 * NTH / (2.0 * math.pi)
DZ = 0.5 * NZ / pipe_length


def radial_table():
    radius = (np.arange(NR) + 0.5) / NR
    width = np.cbrt((1.0 / NR) * radius * (2.0 * np.pi / NTH) * (pipe_length / NZ)) ** 2
    upper = np.full(NR, 0.5 * NR)
    lower = upper.copy()
    upper[-1] = 0.0
    lower[0] = 0.0
    rows = np.stack([1.0 / radius, DT / radius, upper, lower, width, radius])
    return np.broadcast_to(rows[:, None, :], (6, 8, NR)).astype(np.float32)


def along_radius(field, radial):
    return pltpu.roll(field, NR - 1, 1) * radial[2] - pltpu.roll(field, 1, 1) * radial[3]


def tensor_magnitude(t):
    diagonal = t[0] * t[0] + t[1] * t[1] + t[2] * t[2]
    mixed = t[3] * t[3] + t[4] * t[4] + t[5] * t[5]
    return jnp.sqrt(2.0 * diagonal + 4.0 * mixed)


def neighbours(row, column):
    below, above = lax.rem(row + THETA_COUNT - 1, THETA_COUNT), lax.rem(row + 1, THETA_COUNT)
    left, right = lax.rem(column + GZ_COUNT - 1, GZ_COUNT), lax.rem(column + 1, GZ_COUNT)
    return below, above, left, right


def device(row, column):
    return {"theta": row, "gz": column}


def exchange(velocity, flow, packed, landed, load_sem, send_sem, recv_sem, barrier):
    row, column = lax.axis_index("theta"), lax.axis_index("gz")
    below, above, left, right = neighbours(row, column)
    load = pltpu.make_async_copy(
        velocity, flow.at[:, pl.ds(3, LOCAL_T), pl.ds(Z_BASE, LOCAL_Z), :], load_sem
    )
    load.start()

    def greet_row(i, carry):
        target = lax.rem(row + i, THETA_COUNT)
        pl.semaphore_signal(barrier, inc=1, device_id=device(target, column), device_id_type=MESH_ID)
        return carry

    def greet_column(i, carry):
        target = lax.rem(column + i, GZ_COUNT)
        pl.semaphore_signal(barrier, inc=1, device_id=device(row, target), device_id_type=MESH_ID)
        return carry

    lax.fori_loop(1, THETA_COUNT, greet_row, 0)
    lax.fori_loop(1, GZ_COUNT, greet_column, 0)
    for r in (below, above):
        for c in (left, right):
            pl.semaphore_signal(barrier, inc=1, device_id=device(r, c), device_id_type=MESH_ID)
    pl.semaphore_wait(barrier, THETA_COUNT + GZ_COUNT + 2)

    def copy(n, source, target, r, c):
        return pltpu.make_async_remote_copy(
            src_ref=source,
            dst_ref=target,
            send_sem=send_sem.at[n],
            recv_sem=recv_sem.at[n],
            device_id=device(r, c),
            device_id_type=MESH_ID,
        )

    inner = pl.ds(Z_BASE, LOCAL_Z)
    copies = [
        copy(0, velocity.at[:, pl.ds(LOCAL_T - 3, 3)], flow.at[:, pl.ds(0, 3), inner], above, column),
        copy(1, velocity.at[:, pl.ds(0, 3)], flow.at[:, pl.ds(LOCAL_T + 3, 3), inner], below, column),
    ]
    for item in copies:
        item.start()
    load.wait()
    for side, first in ((0, Z_BASE + LOCAL_Z - 3), (1, Z_BASE)):
        for comp in range(3):
            for z in range(3):
                packed[side, 3 * comp + z] = flow[comp, pl.ds(3, LOCAL_T), first + z, :]
    for side, target in ((0, right), (1, left)):
        main, low, high = pl.ds(8, LOCAL_T), pl.ds(0, 8), pl.ds(LOCAL_T + 8, 8)
        sides = [
            copy(2 + 3 * side, packed.at[side], landed.at[side, :, main], row, target),
            copy(3 + 3 * side, packed.at[side, :, pl.ds(LOCAL_T - 8, 8)], landed.at[side, :, low], above, target),
            copy(4 + 3 * side, packed.at[side, :, pl.ds(0, 8)], landed.at[side, :, high], below, target),
        ]
        for item in sides:
            item.start()
        copies += sides
    for item in copies:
        item.wait()
    for side, first in ((0, Z_BASE - 3), (1, Z_BASE + LOCAL_Z)):
        for comp in range(3):
            for z in range(3):
                flow[comp, :, first + z, :] = landed[side, 3 * comp + z, pl.ds(5, T_ROWS), :]


def read_flow(flow, comp, t, q):
    return flow[comp, t, pl.ds(Z_BASE + q, 8, stride=Z_STEP), :]


def strain_rows(flow, tensor, radial):
    def strain_row(n, carry):
        centre = [[read_flow(flow, c, n + 1, q) for q in range(-3, Z_STEP + 3)] for c in range(3)]
        for i in range(S_COLS):
            u = [centre[c][i + 1] for c in range(3)]
            dz = [(centre[c][i + 2] - centre[c][i]) * DZ for c in range(3)]
            dt = [
                (read_flow(flow, c, n + 2, i - 2) - read_flow(flow, c, n, i - 2)) * radial[1]
                for c in range(3)
            ]
            dr = [along_radius(u[c], radial) for c in range(3)]
            parts = [
                dr[0],
                dt[1] + u[0] * radial[0],
                dz[2],
                0.5 * (dr[1] - u[1] * radial[0] + dt[0]),
                0.5 * (dz[0] + dr[2]),
                0.5 * (dt[2] + dz[1]),
            ]
            for k in range(6):
                tensor[k, n, i] = parts[k]
            tensor[6, n, i] = tensor_magnitude(parts)
        return carry

    lax.fori_loop(0, S_ROWS, strain_row, 0)


def filter_rows(flow, tensor, state, filtered):
    span = range(-1, Z_STEP + 1)

    def across(n):
        flows = [[read_flow(flow, c, n + 1, q) for q in span] for c in range(3)]
        for c in range(3):
            yield flows[c]
        for a, b in zip(pair_first, pair_second):
            yield [x * y for x, y in zip(flows[a], flows[b])]
        for k in range(6):
            yield [tensor[k, n, q + 2] for q in span]
        for k in range(6):
            yield [tensor[k, n, q + 2] * tensor[6, n, q + 2] for q in span]

    def axial(values):
        pairs = [x + y for x, y in zip(values[:-1], values[1:])]
        return [x + y for x, y in zip(pairs[:-1], pairs[1:])]

    def first_rows():
        for f, (one, two) in enumerate(zip(across(1), across(2))):
            one, two = axial(one), axial(two)
            for q in range(Z_STEP):
                state[0, f, q] = two[q]
                state[1, f, q] = one[q] + two[q]

    def pair_rows(step, carry):
        n = 3 + 2 * step
        for f, (one, two) in enumerate(zip(across(n), across(n + 1))):
            one, two = axial(one), axial(two)
            for q in range(Z_STEP):
                before = state[0, f, q] + one[q]
                after = one[q] + two[q]
                filtered[f, q] = state[1, f, q] + before
                filtered[f, Z_STEP + q] = before + after
                state[0, f, q] = two[q]
                state[1, f, q] = after
        numer, denom = carry
        for q in range(2 * Z_STEP):
            means = [filtered[c, q] for c in range(3)]
            smooth = [filtered[9 + k, q] for k in range(6)]
            size = tensor_magnitude(smooth) * (filter_ratio / 16.0)
            lm, mm = [], []
            for k in range(6):
                leonard = filtered[3 + k, q] - means[pair_first[k]] * means[pair_second[k]] * (1.0 / 16.0)
                model = size * smooth[k] - filtered[15 + k, q]
                lm.append(leonard * model)
                mm.append(model * model)
            numer = numer + (lm[0] + lm[1] + lm[2]) + 2.0 * (lm[3] + lm[4] + lm[5])
            denom = denom + (mm[0] + mm[1] + mm[2]) + 2.0 * (mm[3] + mm[4] + mm[5])
        return numer, denom

    first_rows()
    zero = jnp.zeros((8, NR), jnp.float32)
    return lax.fori_loop(0, LOCAL_T // 2, pair_rows, (zero, zero))


def sum_everywhere(numer, denom, row_sums, all_sums, send_sem, recv_sem):
    row, column = lax.axis_index("theta"), lax.axis_index("gz")
    first = lax.broadcasted_iota(jnp.int32, (8, NR), 0) == 0
    tile = jnp.where(
        first, jnp.sum(numer, axis=0, keepdims=True), jnp.sum(denom, axis=0, keepdims=True)
    )

    def share(buffer, tile, place, count, target, step):
        buffer[place] = tile

        def send(i, carry):
            pltpu.make_async_remote_copy(
                src_ref=buffer.at[place],
                dst_ref=buffer.at[place],
                send_sem=send_sem.at[step],
                recv_sem=recv_sem.at[step],
                device_id=target(lax.rem(place + i, count)),
                device_id_type=MESH_ID,
            ).start()
            return carry

        lax.fori_loop(1, count, send, 0)
        others = buffer.at[pl.ds(0, count - 1)]
        wait_bytes(others, recv_sem.at[step])
        wait_bytes(others, send_sem.at[step])
        total = buffer[0]
        for i in range(1, count):
            total = total + buffer[i]
        return total

    tile = share(row_sums, tile, row, THETA_COUNT, lambda i: device(i, column), 0)
    tile = share(all_sums, tile, column, GZ_COUNT, lambda i: device(row, i), 1)
    return tile[0:1], tile[1:2]


def stress_rows(tensor, ratio, eddy):
    def stress_row(n, carry):
        for i in range(S_COLS):
            viscosity = eddy * tensor[6, n, i]
            scale = 2.0 * viscosity + 2.0 * nu_molecular
            for k in range(6):
                tensor[k, n, i] = tensor[k, n, i] * scale
        return carry

    def ratio_row(t, carry):
        for q in range(Z_STEP):
            value = eddy * tensor[6, t + 2, q + 2] * (1.0 / nu_molecular)
            ratio[t, pl.ds(q, 8, stride=Z_STEP), :] = value
        return carry

    lax.fori_loop(0, LOCAL_T, ratio_row, 0)
    lax.fori_loop(0, S_ROWS, stress_row, 0)


def source_rows(flow, tensor, swirl, partial, source, radial):
    def swirl_row(n, carry):
        for q in range(Z_STEP):
            i = q + 2
            shear = tensor[3, n, i]
            force = (
                along_radius(shear, radial)
                + (tensor[1, n + 1, i] - tensor[1, n - 1, i]) * radial[1]
                + (tensor[5, n, i + 1] - tensor[5, n, i - 1]) * DZ
                + 2.0 * shear * radial[0]
            )
            swirl[n - 1, q] = read_flow(flow, 1, n + 1, q) + time_step * force
        return carry

    def other_row(t, carry):
        n = t + 2
        axial = []
        for q in range(-1, Z_STEP + 1):
            i = q + 2
            shear = tensor[4, n, i]
            force = (
                along_radius(shear, radial)
                + (tensor[5, n + 1, i] - tensor[5, n - 1, i]) * radial[1]
                + (tensor[2, n, i + 1] - tensor[2, n, i - 1]) * DZ
                + shear * radial[0]
            )
            axial.append(read_flow(flow, 2, n + 1, q) + time_step * force)
        for q in range(Z_STEP):
            i = q + 2
            normal = tensor[0, n, i]
            force = (
                along_radius(normal, radial)
                + (tensor[3, n + 1, i] - tensor[3, n - 1, i]) * radial[1]
                + (tensor[4, n, i + 1] - tensor[4, n, i - 1]) * DZ
                + (normal - tensor[1, n, i]) * radial[0]
            )
            outward = (read_flow(flow, 0, n + 1, q) + time_step * force) * radial[5]
            partial[t, q] = along_radius(outward, radial) * radial[0] + (axial[q + 2] - axial[q]) * DZ
        return carry

    def join_row(t, carry):
        for q in range(Z_STEP):
            value = partial[t, q] + (swirl[t + 2, q] - swirl[t, q]) * radial[1]
            source[:, q * LOCAL_T + t, :] = value
        return carry

    lax.fori_loop(1, S_ROWS - 1, swirl_row, 0)
    lax.fori_loop(0, LOCAL_T, other_row, 0)
    lax.fori_loop(0, LOCAL_T, join_row, 0)


def front_kernel(
    velocity,
    radial,
    ratio,
    tiles,
    flow,
    packed,
    landed,
    tensor,
    state,
    filtered,
    row_sums,
    all_sums,
    swirl,
    partial,
    source,
    load_sem,
    send_sem,
    recv_sem,
    sum_send_sem,
    sum_recv_sem,
):
    barrier = pltpu.get_barrier_semaphore()
    exchange(velocity, flow, packed, landed, load_sem, send_sem, recv_sem, barrier)
    strain_rows(flow, tensor, radial)
    numer, denom = filter_rows(flow, tensor, state, filtered)
    numer, denom = sum_everywhere(numer, denom, row_sums, all_sums, sum_send_sem, sum_recv_sem)
    width = radial[4][0:1]
    numer = numer * (width * (2.0 / 256.0))
    denom = denom * (width * width * (4.0 / 256.0))
    coefficient = numer / (denom + epsilon_den)
    eddy = jnp.broadcast_to(coefficient * width, (8, NR))
    stress_rows(tensor, ratio, eddy)
    source_rows(flow, tensor, swirl, partial, source, radial)
    for s in range(8):
        tiles[:, s, :] = source[s].T


def front(velocity):
    vmem = pl.BlockSpec(memory_space=pltpu.VMEM)
    return pl.pallas_call(
        front_kernel,
        out_shape=(
            jax.ShapeDtypeStruct((LOCAL_T, LOCAL_Z, NR), jnp.float32),
            jax.ShapeDtypeStruct((NR, 8, 4 * LOCAL_T), jnp.float32),
        ),
        in_specs=[pl.BlockSpec(memory_space=pl.ANY), vmem],
        out_specs=(vmem, vmem),
        scratch_shapes=[
            pltpu.VMEM((3, T_ROWS, Z_ROWS, NR), jnp.float32),
            pltpu.VMEM((2, 9, LOCAL_T, NR), jnp.float32),
            pltpu.VMEM((2, 9, LOCAL_T + 16, NR), jnp.float32),
            pltpu.VMEM((7, S_ROWS, S_COLS, 8, NR), jnp.float32),
            pltpu.VMEM((2, 21, Z_STEP, 8, NR), jnp.float32),
            pltpu.VMEM((21, 2 * Z_STEP, 8, NR), jnp.float32),
            pltpu.VMEM((THETA_COUNT, 8, NR), jnp.float32),
            pltpu.VMEM((GZ_COUNT, 8, NR), jnp.float32),
            pltpu.VMEM((LOCAL_T + 2, Z_STEP, 8, NR), jnp.float32),
            pltpu.VMEM((LOCAL_T, Z_STEP, 8, NR), jnp.float32),
            pltpu.VMEM((8, 4 * LOCAL_T, NR), jnp.float32),
            pltpu.SemaphoreType.DMA,
            pltpu.SemaphoreType.DMA((8,)),
            pltpu.SemaphoreType.DMA((8,)),
            pltpu.SemaphoreType.DMA((2,)),
            pltpu.SemaphoreType.DMA((2,)),
        ],
        compiler_params=pltpu.CompilerParams(
            collective_id=1, has_side_effects=True, vmem_limit_bytes=48 << 20
        ),
        name="front",
    )(velocity, jnp.asarray(radial_table()))


def split_table(table):
    parts, rest = [], table
    for _ in range(3):
        part = rest.astype(np.float32).astype(ml_dtypes.bfloat16)
        parts.append(part)
        rest = rest - part.astype(np.float64)
    return np.stack(parts)


def axial_table():
    order = np.arange(NZ)
    block, rest = order // LOCAL_Z, order % LOCAL_Z
    cells = block * LOCAL_Z + 4 * (rest % 8) + rest // 8
    angle = 2.0 * np.pi * ((np.arange(NZ)[:, None] * cells[None, :]) % NZ) / NZ
    return split_table(np.concatenate([np.cos(angle), np.sin(angle)], axis=0))


def cycle_table():
    angle = 2.0 * np.pi * ((np.arange(NTH)[:, None] * np.arange(NTH)[None, :]) % NTH) / NTH
    scale = 1.0 / math.sqrt(NTH * NZ)
    cosine = (np.cos(angle) * scale).reshape(NTH, GZ_COUNT, LOCAL_M)
    sine = (np.sin(angle) * scale).reshape(NTH, GZ_COUNT, LOCAL_M)
    upper = np.stack([cosine, -sine], axis=2)
    lower = np.stack([-sine, -cosine], axis=2)
    both = np.concatenate([upper, lower], axis=0).reshape(2 * NTH, GZ_COUNT // 2, 4 * LOCAL_M)
    return split_table(np.moveaxis(both, 1, 0))


def split_value(value):
    parts = []
    for _ in range(3):
        part = value.astype(jnp.bfloat16)
        parts.append(part)
        value = value - part.astype(jnp.float32)
    return parts


def product(left, right):
    total = None
    for i, j in ((0, 2), (2, 0), (1, 1), (0, 1), (1, 0), (0, 0)):
        term = jnp.dot(left[i], right[j], preferred_element_type=jnp.float32)
        total = term if total is None else total + term
    return total


def meet_all(row, column, barrier, second):
    def greet_row(i, carry):
        pl.semaphore_signal(
            barrier,
            inc=1,
            device_id={"theta": lax.rem(row + i, THETA_COUNT), "gz": column},
            device_id_type=MESH_ID,
        )
        return carry

    def greet_column(sem):
        def greet(i, carry):
            pl.semaphore_signal(
                sem,
                inc=1,
                device_id={"theta": row, "gz": lax.rem(column + i, GZ_COUNT)},
                device_id_type=MESH_ID,
            )
            return carry

        return greet

    lax.fori_loop(1, THETA_COUNT, greet_row, 0)
    lax.fori_loop(1, GZ_COUNT, greet_column(barrier), 0)
    pl.semaphore_wait(barrier, THETA_COUNT + GZ_COUNT - 2)
    lax.fori_loop(1, GZ_COUNT, greet_column(second), 0)
    pl.semaphore_wait(second, GZ_COUNT - 1)


def spectral_kernel(
    tiles_ref,
    axial_hbm,
    cycle_hbm,
    modes_ref,
    planes,
    plane,
    axial,
    cycle,
    left,
    spectrum,
    second,
    table_sem,
    send_sem,
    recv_sem,
    out_send_sem,
    out_recv_sem,
    own_sem,
):
    row, column = lax.axis_index("theta"), lax.axis_index("gz")
    me = row * GZ_COUNT + column
    fetch_axial = pltpu.make_async_copy(axial_hbm, axial, table_sem.at[0])
    fetch_cycle = pltpu.make_async_copy(cycle_hbm, cycle, table_sem.at[1])
    fetch_axial.start()
    fetch_cycle.start()
    meet_all(row, column, pltpu.get_barrier_semaphore(), second)

    def send_tile(i, carry):
        target = lax.rem(me + i, DEVICES)
        pltpu.make_async_remote_copy(
            src_ref=tiles_ref.at[target],
            dst_ref=planes.at[me],
            send_sem=send_sem,
            recv_sem=recv_sem,
            device_id={"theta": target // GZ_COUNT, "gz": lax.rem(target, GZ_COUNT)},
            device_id_type=MESH_ID,
        ).start()
        return carry

    lax.fori_loop(1, DEVICES, send_tile, 0)
    planes[me] = tiles_ref[me]
    wait_bytes(planes.at[pl.ds(0, DEVICES - 1)], recv_sem)
    wait_bytes(planes.at[pl.ds(0, DEVICES - 1)], send_sem)

    group = lax.broadcasted_iota(jnp.int32, (8, 128), 1) // LOCAL_T

    def gather_lines(c, carry):
        for quad in range(THETA_COUNT // 4):
            parts = [planes[(4 * quad + b) * GZ_COUNT + c] for b in range(4)]
            for z in range(4):
                turned = [
                    parts[b] if b == z else pltpu.roll(parts[b], ((b - z) * LOCAL_T) % 128, 1)
                    for b in range(4)
                ]
                value = jnp.where(
                    group < 2,
                    jnp.where(group == 0, turned[0], turned[1]),
                    jnp.where(group == 2, turned[2], turned[3]),
                )
                start = pl.multiple_of(c * LOCAL_Z + 8 * z, 8)
                plane[pl.ds(start, 8), 128 * quad : 128 * quad + 128] = value
        return carry

    lax.fori_loop(0, GZ_COUNT, gather_lines, 0)
    fetch_axial.wait()
    lines = product(axial, split_value(plane[...]))
    for n, part in enumerate(split_value(lines)):
        left[n, :, :NTH] = part[:NZ]
        left[n, :, NTH:] = part[NZ:]
    fetch_cycle.wait()

    def transform(step, carry):
        pair = lax.rem(column // 2 + step, GZ_COUNT // 2)
        both = product(left, cycle.at[:, pair])
        spectrum[2 * pair] = both[:, :128]
        spectrum[2 * pair + 1] = both[:, 128:]

        def send_modes(i, inner):
            target_column = 2 * pair + lax.rem(column + i // THETA_COUNT, 2)
            target_row = lax.rem(row + i, THETA_COUNT)
            rows = pl.ds(pl.multiple_of(target_row * LOCAL_K, LOCAL_K), LOCAL_K)

            @pl.when(jnp.logical_or(target_row != row, target_column != column))
            def _():
                pltpu.make_async_remote_copy(
                    src_ref=spectrum.at[target_column, rows],
                    dst_ref=modes_ref.at[me],
                    send_sem=out_send_sem,
                    recv_sem=out_recv_sem,
                    device_id={"theta": target_row, "gz": target_column},
                    device_id_type=MESH_ID,
                ).start()

            return inner

        lax.fori_loop(0, 2 * THETA_COUNT, send_modes, 0)
        return carry

    lax.fori_loop(0, GZ_COUNT // 2, transform, 0)
    own_rows = pl.ds(pl.multiple_of(row * LOCAL_K, LOCAL_K), LOCAL_K)
    keep = pltpu.make_async_copy(spectrum.at[column, own_rows], modes_ref.at[me], own_sem)
    keep.start()
    keep.wait()
    wait_bytes(modes_ref.at[pl.ds(0, DEVICES - 1)], out_send_sem)
    wait_bytes(modes_ref.at[pl.ds(0, DEVICES - 1)], out_recv_sem)


def spectral(tiles):
    any_space = pl.BlockSpec(memory_space=pl.ANY)
    return pl.pallas_call(
        spectral_kernel,
        out_shape=jax.ShapeDtypeStruct((DEVICES, LOCAL_K, 128), jnp.float32),
        in_specs=[pl.BlockSpec(memory_space=pltpu.VMEM), any_space, any_space],
        out_specs=any_space,
        scratch_shapes=[
            pltpu.VMEM((DEVICES, 8, 128), jnp.float32),
            pltpu.VMEM((NZ, NTH), jnp.float32),
            pltpu.VMEM((3, 2 * NZ, NZ), jnp.bfloat16),
            pltpu.VMEM((3, GZ_COUNT // 2, 2 * NTH, 4 * LOCAL_M), jnp.bfloat16),
            pltpu.VMEM((3, NZ, 2 * NTH), jnp.bfloat16),
            pltpu.VMEM((GZ_COUNT, NZ, 128), jnp.float32),
            pltpu.SemaphoreType.REGULAR,
            pltpu.SemaphoreType.DMA((2,)),
            pltpu.SemaphoreType.DMA,
            pltpu.SemaphoreType.DMA,
            pltpu.SemaphoreType.DMA,
            pltpu.SemaphoreType.DMA,
            pltpu.SemaphoreType.DMA,
        ],
        compiler_params=pltpu.CompilerParams(
            collective_id=0, has_side_effects=True, vmem_limit_bytes=48 << 20
        ),
        name="spectral",
    )(tiles, jnp.asarray(axial_table()), jnp.asarray(cycle_table()))


def solve_kernel(modes_ref, out_ref, inverse, partial, pressure):
    row, column = lax.axis_index("theta"), lax.axis_index("gz")
    shape = (LOCAL_K, 128)
    theta_mode = column * LOCAL_M + lax.broadcasted_iota(jnp.int32, shape, 1) % LOCAL_M
    axial_mode = row * LOCAL_K + lax.broadcasted_iota(jnp.int32, shape, 0)
    theta_wave = jnp.minimum(theta_mode, NTH - theta_mode).astype(jnp.float32)
    axial_wave = jnp.minimum(axial_mode, NZ - axial_mode).astype(jnp.float32) * (
        2.0 * math.pi / pipe_length
    )
    theta_sq = theta_wave * theta_wave
    axial_sq = axial_wave * axial_wave * (1.0 / (NR * NR))

    def diagonal(i):
        middle = i + 0.5
        extra = float(NR) if i == NR - 1 else 0.0
        return theta_sq * (1.0 / middle) + (axial_sq * middle + (2.0 * i + 1.0 + extra))

    def load(i):
        return modes_ref[i] * (-(i + 0.5) / (NR * NR))

    low_diag, low_value = diagonal(0), load(0)
    high_diag, high_value = diagonal(NR - 1), load(NR - 1)
    for step in range(1, HALF):
        i = step
        low_inverse = 1.0 / low_diag
        inverse[i - 1] = low_inverse
        partial[i - 1] = low_value
        low_value = load(i) + (low_inverse * float(i)) * low_value
        low_diag = diagonal(i) - low_inverse * float(i * i)
        j = NR - 1 - step
        high_inverse = 1.0 / high_diag
        inverse[j + 1] = high_inverse
        partial[j + 1] = high_value
        high_value = load(j) + (high_inverse * float(j + 1)) * high_value
        high_diag = diagonal(j) - high_inverse * float((j + 1) * (j + 1))
    scale = 1.0 / (low_diag * high_diag - float(HALF * HALF))
    low = (low_value * high_diag + float(HALF) * high_value) * scale
    high = (high_value * low_diag + float(HALF) * low_value) * scale
    pressure[HALF - 1] = low
    pressure[HALF] = high
    for step in range(1, HALF):
        i = HALF - 1 - step
        low = (partial[i] + float(i + 1) * low) * inverse[i]
        pressure[i] = low
        j = HALF + step
        high = (partial[j] + float(j) * high) * inverse[j]
        pressure[j] = high
    for k in range(LOCAL_K):
        out_ref[:, k, :] = pressure[:, k, :].T


def solve(modes):
    vmem = pl.BlockSpec(memory_space=pltpu.VMEM)
    out = pl.pallas_call(
        solve_kernel,
        out_shape=jax.ShapeDtypeStruct((2 * LOCAL_M, LOCAL_K, NR), jnp.float32),
        in_specs=[vmem],
        out_specs=vmem,
        scratch_shapes=[pltpu.VMEM((NR, LOCAL_K, 128), jnp.float32)] * 3,
        compiler_params=pltpu.CompilerParams(vmem_limit_bytes=32 << 20),
        name="solve",
    )(modes)
    return out.reshape(2, LOCAL_M, LOCAL_K, NR)


def body(velocity):
    ratio, tiles = front(velocity)
    return (ratio, solve(spectral(tiles)))


def solution(mesh):
    return jax.shard_map(
        body,
        mesh=mesh,
        in_specs=(P(None, "theta", "gz", None),),
        out_specs=(P("theta", "gz", None), P(None, "gz", "theta", None)),
        check_vma=False,
    )
```

```python
import functools
import math

import jax
import jax.numpy as jnp
import ml_dtypes
import numpy as np
from jax import lax
from jax.experimental import pallas as pl
from jax.experimental.pallas import tpu as pltpu
from jax.sharding import PartitionSpec as P

NTH = 512
NZ = 256
NR = 128


pipe_length = 4.0 * math.pi
nu_molecular = 5e-05
time_step = 2.0
filter_ratio = 4.0
epsilon_den = 1e-06
pair_first = (0, 1, 2, 0, 0, 1)
pair_second = (0, 1, 2, 1, 2, 2)


THETA_COUNT = 16
GZ_COUNT = 8
DEVICES = THETA_COUNT * GZ_COUNT
LOCAL_T = NTH // THETA_COUNT
LOCAL_Z = NZ // GZ_COUNT
LOCAL_M = NTH // GZ_COUNT
LOCAL_K = NZ // THETA_COUNT
MESH_ID = pl.DeviceIdType.MESH
HALF = NR // 2


def wait_bytes(ref, sem):
    pltpu.make_async_copy(ref, ref, sem).wait()


T_ROWS = LOCAL_T + 6
Z_BASE = 8
Z_ROWS = LOCAL_Z + 2 * Z_BASE
Z_STEP = LOCAL_Z // 8
S_ROWS = LOCAL_T + 4
S_COLS = Z_STEP + 4
DT = 0.5 * NTH / (2.0 * math.pi)
DZ = 0.5 * NZ / pipe_length


def radial_table():
    radius = (np.arange(NR) + 0.5) / NR
    width = np.cbrt((1.0 / NR) * radius * (2.0 * np.pi / NTH) * (pipe_length / NZ)) ** 2
    upper = np.full(NR, 0.5 * NR)
    lower = upper.copy()
    upper[-1] = 0.0
    lower[0] = 0.0
    rows = np.stack([1.0 / radius, DT / radius, upper, lower, width, radius])
    return np.broadcast_to(rows[:, None, :], (6, 8, NR)).astype(np.float32)


def along_radius(field, radial):
    return pltpu.roll(field, NR - 1, 1) * radial[2] - pltpu.roll(field, 1, 1) * radial[3]


def tensor_magnitude(t):
    diagonal = t[0] * t[0] + t[1] * t[1] + t[2] * t[2]
    mixed = t[3] * t[3] + t[4] * t[4] + t[5] * t[5]
    return jnp.sqrt(2.0 * diagonal + 4.0 * mixed)


def neighbours(row, column):
    below, above = lax.rem(row + THETA_COUNT - 1, THETA_COUNT), lax.rem(row + 1, THETA_COUNT)
    left, right = lax.rem(column + GZ_COUNT - 1, GZ_COUNT), lax.rem(column + 1, GZ_COUNT)
    return below, above, left, right


def device(row, column):
    return {"theta": row, "gz": column}


def exchange(velocity, flow, packed, landed, load_sem, send_sem, recv_sem, barrier, fetches):
    row, column = lax.axis_index("theta"), lax.axis_index("gz")
    below, above, left, right = neighbours(row, column)
    load = pltpu.make_async_copy(
        velocity, flow.at[:, pl.ds(3, LOCAL_T), pl.ds(Z_BASE, LOCAL_Z), :], load_sem
    )
    load.start()
    for item in fetches:
        item.start()

    def greet_row(i, carry):
        target = lax.rem(row + i, THETA_COUNT)
        pl.semaphore_signal(barrier, inc=1, device_id=device(target, column), device_id_type=MESH_ID)
        return carry

    def greet_column(i, carry):
        target = lax.rem(column + i, GZ_COUNT)
        pl.semaphore_signal(barrier, inc=1, device_id=device(row, target), device_id_type=MESH_ID)
        return carry

    lax.fori_loop(1, THETA_COUNT, greet_row, 0)
    lax.fori_loop(1, GZ_COUNT, greet_column, 0)
    for r in (below, above):
        for c in (left, right):
            pl.semaphore_signal(barrier, inc=1, device_id=device(r, c), device_id_type=MESH_ID)
    pl.semaphore_wait(barrier, THETA_COUNT + GZ_COUNT + 2)

    def copy(n, source, target, r, c):
        return pltpu.make_async_remote_copy(
            src_ref=source,
            dst_ref=target,
            send_sem=send_sem.at[n],
            recv_sem=recv_sem.at[n],
            device_id=device(r, c),
            device_id_type=MESH_ID,
        )

    inner = pl.ds(Z_BASE, LOCAL_Z)
    copies = [
        copy(0, velocity.at[:, pl.ds(LOCAL_T - 3, 3)], flow.at[:, pl.ds(0, 3), inner], above, column),
        copy(1, velocity.at[:, pl.ds(0, 3)], flow.at[:, pl.ds(LOCAL_T + 3, 3), inner], below, column),
    ]
    for item in copies:
        item.start()
    load.wait()
    fetches[0].wait()
    for side, first in ((0, Z_BASE + LOCAL_Z - 3), (1, Z_BASE)):
        for comp in range(3):
            for z in range(3):
                packed[side, 3 * comp + z] = flow[comp, pl.ds(3, LOCAL_T), first + z, :]
    for side, target in ((0, right), (1, left)):
        main, low, high = pl.ds(8, LOCAL_T), pl.ds(0, 8), pl.ds(LOCAL_T + 8, 8)
        sides = [
            copy(2 + 3 * side, packed.at[side], landed.at[side, :, main], row, target),
            copy(3 + 3 * side, packed.at[side, :, pl.ds(LOCAL_T - 8, 8)], landed.at[side, :, low], above, target),
            copy(4 + 3 * side, packed.at[side, :, pl.ds(0, 8)], landed.at[side, :, high], below, target),
        ]
        for item in sides:
            item.start()
        copies += sides
    for item in copies:
        item.wait()
    for side, first in ((0, Z_BASE - 3), (1, Z_BASE + LOCAL_Z)):
        for comp in range(3):
            for z in range(3):
                flow[comp, :, first + z, :] = landed[side, 3 * comp + z, pl.ds(5, T_ROWS), :]


def read_flow(flow, comp, t, q):
    return flow[comp, t, pl.ds(Z_BASE + q, 8, stride=Z_STEP), :]


def strain_rows(flow, tensor, radial):
    def strain_row(n, carry):
        centre = [[read_flow(flow, c, n + 1, q) for q in range(-3, Z_STEP + 3)] for c in range(3)]
        for i in range(S_COLS):
            u = [centre[c][i + 1] for c in range(3)]
            dz = [(centre[c][i + 2] - centre[c][i]) * DZ for c in range(3)]
            dt = [
                (read_flow(flow, c, n + 2, i - 2) - read_flow(flow, c, n, i - 2)) * radial[1]
                for c in range(3)
            ]
            dr = [along_radius(u[c], radial) for c in range(3)]
            parts = [
                dr[0],
                dt[1] + u[0] * radial[0],
                dz[2],
                0.5 * (dr[1] - u[1] * radial[0] + dt[0]),
                0.5 * (dz[0] + dr[2]),
                0.5 * (dt[2] + dz[1]),
            ]
            for k in range(6):
                tensor[k, n, i] = parts[k]
            tensor[6, n, i] = tensor_magnitude(parts)
        return carry

    lax.fori_loop(0, S_ROWS, strain_row, 0, unroll=2)


def filter_rows(flow, tensor, state, filtered):
    span = range(-1, Z_STEP + 1)

    def across(n):
        flows = [[read_flow(flow, c, n + 1, q) for q in span] for c in range(3)]
        for c in range(3):
            yield flows[c]
        for a, b in zip(pair_first, pair_second):
            yield [x * y for x, y in zip(flows[a], flows[b])]
        for k in range(6):
            yield [tensor[k, n, q + 2] for q in span]
        for k in range(6):
            yield [tensor[k, n, q + 2] * tensor[6, n, q + 2] for q in span]

    def axial(values):
        pairs = [x + y for x, y in zip(values[:-1], values[1:])]
        return [x + y for x, y in zip(pairs[:-1], pairs[1:])]

    def first_rows():
        for f, (one, two) in enumerate(zip(across(1), across(2))):
            one, two = axial(one), axial(two)
            for q in range(Z_STEP):
                state[0, f, q] = two[q]
                state[1, f, q] = one[q] + two[q]

    def pair_rows(step, carry):
        n = 3 + 2 * step
        for f, (one, two) in enumerate(zip(across(n), across(n + 1))):
            one, two = axial(one), axial(two)
            for q in range(Z_STEP):
                before = state[0, f, q] + one[q]
                after = one[q] + two[q]
                filtered[f, q] = state[1, f, q] + before
                filtered[f, Z_STEP + q] = before + after
                state[0, f, q] = two[q]
                state[1, f, q] = after
        numer, denom = carry
        for q in range(2 * Z_STEP):
            means = [filtered[c, q] for c in range(3)]
            smooth = [filtered[9 + k, q] for k in range(6)]
            size = tensor_magnitude(smooth) * (filter_ratio / 16.0)
            lm, mm = [], []
            for k in range(6):
                leonard = filtered[3 + k, q] - means[pair_first[k]] * means[pair_second[k]] * (1.0 / 16.0)
                model = size * smooth[k] - filtered[15 + k, q]
                lm.append(leonard * model)
                mm.append(model * model)
            numer = numer + (lm[0] + lm[1] + lm[2]) + 2.0 * (lm[3] + lm[4] + lm[5])
            denom = denom + (mm[0] + mm[1] + mm[2]) + 2.0 * (mm[3] + mm[4] + mm[5])
        return numer, denom

    first_rows()
    zero = jnp.zeros((8, NR), jnp.float32)
    return lax.fori_loop(0, LOCAL_T // 2, pair_rows, (zero, zero))


def sum_everywhere(numer, denom, row_sums, all_sums, send_sem, recv_sem):
    row, column = lax.axis_index("theta"), lax.axis_index("gz")
    first = lax.broadcasted_iota(jnp.int32, (8, NR), 0) == 0
    tile = jnp.where(
        first, jnp.sum(numer, axis=0, keepdims=True), jnp.sum(denom, axis=0, keepdims=True)
    )

    def share(buffer, tile, place, count, target, step):
        buffer[place] = tile

        def send(i, carry):
            pltpu.make_async_remote_copy(
                src_ref=buffer.at[place],
                dst_ref=buffer.at[place],
                send_sem=send_sem.at[step],
                recv_sem=recv_sem.at[step],
                device_id=target(lax.rem(place + i, count)),
                device_id_type=MESH_ID,
            ).start()
            return carry

        lax.fori_loop(1, count, send, 0)
        others = buffer.at[pl.ds(0, count - 1)]
        wait_bytes(others, recv_sem.at[step])
        wait_bytes(others, send_sem.at[step])
        total = buffer[0]
        for i in range(1, count):
            total = total + buffer[i]
        return total

    tile = share(row_sums, tile, row, THETA_COUNT, lambda i: device(i, column), 0)
    tile = share(all_sums, tile, column, GZ_COUNT, lambda i: device(row, i), 1)
    return tile[0:1], tile[1:2]


def stress_rows(tensor, ratio, eddy):
    def stress_row(n, carry):
        for i in range(S_COLS):
            viscosity = eddy * tensor[6, n, i]
            scale = 2.0 * viscosity + 2.0 * nu_molecular
            for k in range(6):
                tensor[k, n, i] = tensor[k, n, i] * scale
        return carry

    def ratio_row(t, carry):
        for q in range(Z_STEP):
            value = eddy * tensor[6, t + 2, q + 2] * (1.0 / nu_molecular)
            ratio[t, pl.ds(q, 8, stride=Z_STEP), :] = value
        return carry

    lax.fori_loop(0, LOCAL_T, ratio_row, 0)
    lax.fori_loop(0, S_ROWS, stress_row, 0, unroll=2)


def source_rows(flow, tensor, swirl, partial, source, radial):
    def swirl_row(n, carry):
        for q in range(Z_STEP):
            i = q + 2
            shear = tensor[3, n, i]
            force = (
                along_radius(shear, radial)
                + (tensor[1, n + 1, i] - tensor[1, n - 1, i]) * radial[1]
                + (tensor[5, n, i + 1] - tensor[5, n, i - 1]) * DZ
                + 2.0 * shear * radial[0]
            )
            swirl[n - 1, q] = read_flow(flow, 1, n + 1, q) + time_step * force
        return carry

    def other_row(t, carry):
        n = t + 2
        axial = []
        for q in range(-1, Z_STEP + 1):
            i = q + 2
            shear = tensor[4, n, i]
            force = (
                along_radius(shear, radial)
                + (tensor[5, n + 1, i] - tensor[5, n - 1, i]) * radial[1]
                + (tensor[2, n, i + 1] - tensor[2, n, i - 1]) * DZ
                + shear * radial[0]
            )
            axial.append(read_flow(flow, 2, n + 1, q) + time_step * force)
        for q in range(Z_STEP):
            i = q + 2
            normal = tensor[0, n, i]
            force = (
                along_radius(normal, radial)
                + (tensor[3, n + 1, i] - tensor[3, n - 1, i]) * radial[1]
                + (tensor[4, n, i + 1] - tensor[4, n, i - 1]) * DZ
                + (normal - tensor[1, n, i]) * radial[0]
            )
            outward = (read_flow(flow, 0, n + 1, q) + time_step * force) * radial[5]
            partial[t, q] = along_radius(outward, radial) * radial[0] + (axial[q + 2] - axial[q]) * DZ
        return carry

    def join_row(t, carry):
        for q in range(Z_STEP):
            value = partial[t, q] + (swirl[t + 2, q] - swirl[t, q]) * radial[1]
            source[:, q * LOCAL_T + t, :] = value
        return carry

    lax.fori_loop(1, S_ROWS - 1, swirl_row, 0, unroll=2)
    lax.fori_loop(0, LOCAL_T, other_row, 0, unroll=4)
    lax.fori_loop(0, LOCAL_T, join_row, 0, unroll=2)


def split_table(table):
    parts, rest = [], table
    for _ in range(3):
        part = rest.astype(np.float32).astype(ml_dtypes.bfloat16)
        parts.append(part)
        rest = rest - part.astype(np.float64)
    return np.stack(parts)


def axial_table():
    order = np.arange(NZ)
    block, rest = order // LOCAL_Z, order % LOCAL_Z
    cells = block * LOCAL_Z + 4 * (rest % 8) + rest // 8
    angle = 2.0 * np.pi * ((np.arange(NZ)[:, None] * cells[None, :]) % NZ) / NZ
    return split_table(np.concatenate([np.cos(angle), np.sin(angle)], axis=0))


def cycle_table():
    angle = 2.0 * np.pi * ((np.arange(NTH)[:, None] * np.arange(NTH)[None, :]) % NTH) / NTH
    scale = 1.0 / math.sqrt(NTH * NZ)
    cosine = (np.cos(angle) * scale).reshape(NTH, GZ_COUNT, LOCAL_M)
    sine = (np.sin(angle) * scale).reshape(NTH, GZ_COUNT, LOCAL_M)
    upper = np.stack([cosine, -sine], axis=2)
    lower = np.stack([-sine, -cosine], axis=2)
    both = np.concatenate([upper, lower], axis=0).reshape(2 * NTH, GZ_COUNT // 2, 4 * LOCAL_M)
    return split_table(np.moveaxis(both, 1, 0))


def split_value(value):
    parts = []
    for _ in range(3):
        part = value.astype(jnp.bfloat16)
        parts.append(part)
        value = value - part.astype(jnp.float32)
    return parts


def product(left, right):
    total = None
    for i, j in ((0, 2), (2, 0), (1, 1), (0, 1), (1, 0), (0, 0)):
        term = jnp.dot(left[i], right[j], preferred_element_type=jnp.float32)
        total = term if total is None else total + term
    return total


def spectral_part(
    tiles,
    modes,
    planes,
    plane,
    axial,
    cycle,
    left,
    spectrum,
    fetch_axial,
    fetch_cycle,
    send_sem,
    recv_sem,
    out_send_sem,
    out_recv_sem,
    own_sem,
):
    row, column = lax.axis_index("theta"), lax.axis_index("gz")
    me = row * GZ_COUNT + column

    def send_tile(i, carry):
        target = lax.rem(me + i, DEVICES)
        pltpu.make_async_remote_copy(
            src_ref=tiles.at[target],
            dst_ref=planes.at[me],
            send_sem=send_sem,
            recv_sem=recv_sem,
            device_id={"theta": target // GZ_COUNT, "gz": lax.rem(target, GZ_COUNT)},
            device_id_type=MESH_ID,
        ).start()
        return carry

    lax.fori_loop(1, DEVICES, send_tile, 0)
    planes[me] = tiles[me]
    wait_bytes(planes.at[pl.ds(0, DEVICES - 1)], recv_sem)
    wait_bytes(planes.at[pl.ds(0, DEVICES - 1)], send_sem)

    group = lax.broadcasted_iota(jnp.int32, (8, 128), 1) // LOCAL_T

    def gather_lines(c, carry):
        for quad in range(THETA_COUNT // 4):
            parts = [planes[(4 * quad + b) * GZ_COUNT + c] for b in range(4)]
            for z in range(4):
                turned = [
                    parts[b] if b == z else pltpu.roll(parts[b], ((b - z) * LOCAL_T) % 128, 1)
                    for b in range(4)
                ]
                value = jnp.where(
                    group < 2,
                    jnp.where(group == 0, turned[0], turned[1]),
                    jnp.where(group == 2, turned[2], turned[3]),
                )
                start = pl.multiple_of(c * LOCAL_Z + 8 * z, 8)
                plane[pl.ds(start, 8), 128 * quad : 128 * quad + 128] = value
        return carry

    lax.fori_loop(0, GZ_COUNT, gather_lines, 0)
    fetch_axial.wait()
    lines = product(axial, split_value(plane[...]))
    for n, part in enumerate(split_value(lines)):
        left[n, :, :NTH] = part[:NZ]
        left[n, :, NTH:] = part[NZ:]
    fetch_cycle.wait()

    def transform(step, carry):
        pair = lax.rem(column // 2 + step, GZ_COUNT // 2)
        both = product(left, cycle.at[:, pair])
        spectrum[2 * pair] = both[:, :128]
        spectrum[2 * pair + 1] = both[:, 128:]

        def send_modes(i, inner):
            target_column = 2 * pair + lax.rem(column + i // THETA_COUNT, 2)
            target_row = lax.rem(row + i, THETA_COUNT)
            rows = pl.ds(pl.multiple_of(target_row * LOCAL_K, LOCAL_K), LOCAL_K)

            @pl.when(jnp.logical_or(target_row != row, target_column != column))
            def _():
                pltpu.make_async_remote_copy(
                    src_ref=spectrum.at[target_column, rows],
                    dst_ref=modes.at[me],
                    send_sem=out_send_sem,
                    recv_sem=out_recv_sem,
                    device_id={"theta": target_row, "gz": target_column},
                    device_id_type=MESH_ID,
                ).start()

            return inner

        lax.fori_loop(0, 2 * THETA_COUNT, send_modes, 0)
        return carry

    lax.fori_loop(0, GZ_COUNT // 2, transform, 0)
    own_rows = pl.ds(pl.multiple_of(row * LOCAL_K, LOCAL_K), LOCAL_K)
    keep = pltpu.make_async_copy(spectrum.at[column, own_rows], modes.at[me], own_sem)
    keep.start()
    keep.wait()
    wait_bytes(modes.at[pl.ds(0, DEVICES - 1)], out_send_sem)
    wait_bytes(modes.at[pl.ds(0, DEVICES - 1)], out_recv_sem)


def step_kernel(
    velocity,
    radial_hbm,
    axial_hbm,
    cycle_hbm,
    ratio,
    modes,
    radial,
    flow,
    packed,
    landed,
    tensor,
    state,
    filtered,
    row_sums,
    all_sums,
    swirl,
    partial,
    source,
    tiles,
    planes,
    plane,
    axial,
    cycle,
    left,
    spectrum,
    load_sem,
    send_sem,
    recv_sem,
    sum_send_sem,
    sum_recv_sem,
    move_sem,
):
    fetches = [
        pltpu.make_async_copy(source_ref, target, load_sem.at[n])
        for n, (source_ref, target) in enumerate(
            ((radial_hbm, radial), (axial_hbm, axial), (cycle_hbm, cycle)), 1
        )
    ]
    barrier = pltpu.get_barrier_semaphore()
    exchange(velocity, flow, packed, landed, load_sem.at[0], send_sem, recv_sem, barrier, fetches)
    strain_rows(flow, tensor, radial)
    numer, denom = filter_rows(flow, tensor, state, filtered)
    numer, denom = sum_everywhere(numer, denom, row_sums, all_sums, sum_send_sem, sum_recv_sem)
    width = radial[4][0:1]
    numer = numer * (width * (2.0 / 256.0))
    denom = denom * (width * width * (4.0 / 256.0))
    coefficient = numer / (denom + epsilon_den)
    eddy = jnp.broadcast_to(coefficient * width, (8, NR))
    stress_rows(tensor, ratio, eddy)
    source_rows(flow, tensor, swirl, partial, source, radial)
    for s in range(8):
        tiles[:, s, :] = source[s].T
    spectral_part(
        tiles,
        modes,
        planes,
        plane,
        axial,
        cycle,
        left,
        spectrum,
        fetches[1],
        fetches[2],
        *(move_sem.at[n] for n in range(5)),
    )


def step(velocity):
    vmem = pl.BlockSpec(memory_space=pltpu.VMEM)
    hbm = pl.BlockSpec(memory_space=pltpu.HBM)
    return pl.pallas_call(
        step_kernel,
        out_shape=(
            jax.ShapeDtypeStruct((LOCAL_T, LOCAL_Z, NR), jnp.float32),
            jax.ShapeDtypeStruct((DEVICES, LOCAL_K, 128), jnp.float32),
        ),
        in_specs=[hbm, hbm, hbm, hbm],
        out_specs=(vmem, vmem),
        scratch_shapes=[
            pltpu.VMEM((6, 8, NR), jnp.float32),
            pltpu.VMEM((3, T_ROWS, Z_ROWS, NR), jnp.float32),
            pltpu.VMEM((2, 9, LOCAL_T, NR), jnp.float32),
            pltpu.VMEM((2, 9, LOCAL_T + 16, NR), jnp.float32),
            pltpu.VMEM((7, S_ROWS, S_COLS, 8, NR), jnp.float32),
            pltpu.VMEM((2, 21, Z_STEP, 8, NR), jnp.float32),
            pltpu.VMEM((21, 2 * Z_STEP, 8, NR), jnp.float32),
            pltpu.VMEM((THETA_COUNT, 8, NR), jnp.float32),
            pltpu.VMEM((GZ_COUNT, 8, NR), jnp.float32),
            pltpu.VMEM((LOCAL_T + 2, Z_STEP, 8, NR), jnp.float32),
            pltpu.VMEM((LOCAL_T, Z_STEP, 8, NR), jnp.float32),
            pltpu.VMEM((8, 4 * LOCAL_T, NR), jnp.float32),
            pltpu.VMEM((NR, 8, 4 * LOCAL_T), jnp.float32),
            pltpu.VMEM((DEVICES, 8, 128), jnp.float32),
            pltpu.VMEM((NZ, NTH), jnp.float32),
            pltpu.VMEM((3, 2 * NZ, NZ), jnp.bfloat16),
            pltpu.VMEM((3, GZ_COUNT // 2, 2 * NTH, 4 * LOCAL_M), jnp.bfloat16),
            pltpu.VMEM((3, NZ, 2 * NTH), jnp.bfloat16),
            pltpu.VMEM((GZ_COUNT, NZ, 128), jnp.float32),
            pltpu.SemaphoreType.DMA((4,)),
            pltpu.SemaphoreType.DMA((8,)),
            pltpu.SemaphoreType.DMA((8,)),
            pltpu.SemaphoreType.DMA((2,)),
            pltpu.SemaphoreType.DMA((2,)),
            pltpu.SemaphoreType.DMA((5,)),
        ],
        compiler_params=pltpu.CompilerParams(
            collective_id=0, has_side_effects=True, vmem_limit_bytes=48 << 20
        ),
        name="step",
    )(
        *(
            pltpu.with_memory_space_constraint(jnp.asarray(value), pltpu.HBM)
            for value in (velocity, radial_table(), axial_table(), cycle_table())
        )
    )


def solve_kernel(modes_ref, ratio_ref, out_ref, ratio_out, inverse, partial, pressure, ratio_sem):
    keep = pltpu.make_async_copy(ratio_ref, ratio_out, ratio_sem)
    keep.start()
    row, column = lax.axis_index("theta"), lax.axis_index("gz")
    shape = (LOCAL_K, 128)
    theta_mode = column * LOCAL_M + lax.broadcasted_iota(jnp.int32, shape, 1) % LOCAL_M
    axial_mode = row * LOCAL_K + lax.broadcasted_iota(jnp.int32, shape, 0)
    theta_wave = jnp.minimum(theta_mode, NTH - theta_mode).astype(jnp.float32)
    axial_wave = jnp.minimum(axial_mode, NZ - axial_mode).astype(jnp.float32) * (
        2.0 * math.pi / pipe_length
    )
    theta_sq = theta_wave * theta_wave
    axial_sq = axial_wave * axial_wave * (1.0 / (NR * NR))

    def diagonal(i):
        middle = i + 0.5
        extra = float(NR) if i == NR - 1 else 0.0
        return theta_sq * (1.0 / middle) + (axial_sq * middle + (2.0 * i + 1.0 + extra))

    def load(i):
        return modes_ref[i] * (-(i + 0.5) / (NR * NR))

    low_diag, low_value = diagonal(0), load(0)
    high_diag, high_value = diagonal(NR - 1), load(NR - 1)
    for step in range(1, HALF):
        i = step
        low_inverse = 1.0 / low_diag
        inverse[i - 1] = low_inverse
        partial[i - 1] = low_value
        low_value = load(i) + (low_inverse * float(i)) * low_value
        low_diag = diagonal(i) - low_inverse * float(i * i)
        j = NR - 1 - step
        high_inverse = 1.0 / high_diag
        inverse[j + 1] = high_inverse
        partial[j + 1] = high_value
        high_value = load(j) + (high_inverse * float(j + 1)) * high_value
        high_diag = diagonal(j) - high_inverse * float((j + 1) * (j + 1))
    scale = 1.0 / (low_diag * high_diag - float(HALF * HALF))
    low = (low_value * high_diag + float(HALF) * high_value) * scale
    high = (high_value * low_diag + float(HALF) * low_value) * scale
    pressure[HALF - 1] = low
    pressure[HALF] = high
    for step in range(1, HALF):
        i = HALF - 1 - step
        low = (partial[i] + float(i + 1) * low) * inverse[i]
        pressure[i] = low
        j = HALF + step
        high = (partial[j] + float(j) * high) * inverse[j]
        pressure[j] = high
    for k in range(LOCAL_K):
        out_ref[:, k, :] = pressure[:, k, :].T
    keep.wait()


def solve(modes, ratio):
    vmem = pl.BlockSpec(memory_space=pltpu.VMEM)
    anywhere = pl.BlockSpec(memory_space=pl.ANY)
    pressure, ratio = pl.pallas_call(
        solve_kernel,
        out_shape=(
            jax.ShapeDtypeStruct((2 * LOCAL_M, LOCAL_K, NR), jnp.float32),
            jax.ShapeDtypeStruct((LOCAL_T, LOCAL_Z, NR), jnp.float32),
        ),
        in_specs=[vmem, anywhere],
        out_specs=(vmem, pl.BlockSpec(memory_space=pltpu.HBM)),
        scratch_shapes=[pltpu.VMEM((NR, LOCAL_K, 128), jnp.float32)] * 3 + [pltpu.SemaphoreType.DMA],
        compiler_params=pltpu.CompilerParams(vmem_limit_bytes=32 << 20),
        name="solve",
    )(modes, ratio)
    return ratio, pressure.reshape(2, LOCAL_M, LOCAL_K, NR)


def body(velocity):
    ratio, modes = step(velocity)
    return solve(modes, ratio)


def solution(mesh):
    return jax.shard_map(
        body,
        mesh=mesh,
        in_specs=(P(None, "theta", "gz", None),),
        out_specs=(P("theta", "gz", None), P(None, "gz", "theta", None)),
        check_vma=False,
    )
```

```python
import functools
import math

import jax
import jax.numpy as jnp
import ml_dtypes
import numpy as np
from jax import lax
from jax.experimental import pallas as pl
from jax.experimental.pallas import tpu as pltpu
from jax.sharding import PartitionSpec as P

NTH = 512
NZ = 256
NR = 128


pipe_length = 4.0 * math.pi
nu_molecular = 5e-05
time_step = 2.0
filter_ratio = 4.0
epsilon_den = 1e-06
pair_first = (0, 1, 2, 0, 0, 1)
pair_second = (0, 1, 2, 1, 2, 2)


THETA_COUNT = 16
GZ_COUNT = 8
DEVICES = THETA_COUNT * GZ_COUNT
LOCAL_T = NTH // THETA_COUNT
LOCAL_Z = NZ // GZ_COUNT
LOCAL_M = NTH // GZ_COUNT
LOCAL_K = NZ // THETA_COUNT
MESH_ID = pl.DeviceIdType.MESH
HALF = NR // 2


def wait_bytes(ref, sem):
    pltpu.make_async_copy(ref, ref, sem).wait()


T_ROWS = LOCAL_T + 6
Z_BASE = 8
Z_ROWS = LOCAL_Z + 2 * Z_BASE
Z_STEP = LOCAL_Z // 8
S_ROWS = LOCAL_T + 4
S_COLS = Z_STEP + 4
DT = 0.5 * NTH / (2.0 * math.pi)
DZ = 0.5 * NZ / pipe_length


def radial_table():
    radius = (np.arange(NR) + 0.5) / NR
    width = np.cbrt((1.0 / NR) * radius * (2.0 * np.pi / NTH) * (pipe_length / NZ)) ** 2
    upper = np.full(NR, 0.5 * NR)
    lower = upper.copy()
    upper[-1] = 0.0
    lower[0] = 0.0
    rows = np.stack([1.0 / radius, DT / radius, upper, lower, width, radius])
    return np.broadcast_to(rows[:, None, :], (6, 8, NR)).astype(np.float32)


def along_radius(field, radial):
    return pltpu.roll(field, NR - 1, 1) * radial[2] - pltpu.roll(field, 1, 1) * radial[3]


def tensor_magnitude(t):
    diagonal = t[0] * t[0] + t[1] * t[1] + t[2] * t[2]
    mixed = t[3] * t[3] + t[4] * t[4] + t[5] * t[5]
    return jnp.sqrt(2.0 * diagonal + 4.0 * mixed)


def neighbours(row, column):
    below, above = lax.rem(row + THETA_COUNT - 1, THETA_COUNT), lax.rem(row + 1, THETA_COUNT)
    left, right = lax.rem(column + GZ_COUNT - 1, GZ_COUNT), lax.rem(column + 1, GZ_COUNT)
    return below, above, left, right


def device(row, column):
    return {"theta": row, "gz": column}


def exchange(velocity, flow, packed, landed, corners, load_sem, send_sem, recv_sem, fetches):
    row, column = lax.axis_index("theta"), lax.axis_index("gz")
    below, above, left, right = neighbours(row, column)
    barrier = pltpu.get_barrier_semaphore()

    def greet_row(i, carry):
        target = lax.rem(row + i, THETA_COUNT)
        pl.semaphore_signal(barrier, inc=1, device_id=device(target, column), device_id_type=MESH_ID)
        return carry

    def greet_column(i, carry):
        target = lax.rem(column + i, GZ_COUNT)
        pl.semaphore_signal(barrier, inc=1, device_id=device(row, target), device_id_type=MESH_ID)
        return carry

    load = pltpu.make_async_copy(
        velocity, flow.at[:, pl.ds(3, LOCAL_T), pl.ds(Z_BASE, LOCAL_Z), :], load_sem
    )
    load.start()
    fetches[0].start()
    lax.fori_loop(1, THETA_COUNT, greet_row, 0)
    lax.fori_loop(1, GZ_COUNT, greet_column, 0)
    for r in (below, above):
        for c in (left, right):
            pl.semaphore_signal(barrier, inc=1, device_id=device(r, c), device_id_type=MESH_ID)
    load.wait()
    for side, first in ((0, Z_BASE + LOCAL_Z - 3), (1, Z_BASE)):
        for comp in range(3):
            for z in range(3):
                packed[side, 3 * comp + z] = flow[comp, pl.ds(3, LOCAL_T), first + z, :]
    sublane = lax.broadcasted_iota(jnp.int32, (8, NR), 0)
    for side, near in ((0, 2), (1, 0)):
        for comp in range(3):
            for end, start, put, shift in ((0, LOCAL_T - 8, 5, 6), (1, 0, 2, 2)):
                tile = packed[side, 3 * comp + near, pl.ds(start, 8), :]
                other = packed[side, 3 * comp + 1, pl.ds(start, 8), :]
                corners[0, 2 * side + end, comp] = jnp.where(
                    sublane == put, pltpu.roll(other, shift, 0), tile
                )
    pl.semaphore_wait(barrier, THETA_COUNT + GZ_COUNT + 2)

    def copy(n, source, target, r, c):
        item = pltpu.make_async_remote_copy(
            src_ref=source,
            dst_ref=target,
            send_sem=send_sem.at[n],
            recv_sem=recv_sem.at[n],
            device_id=device(r, c),
            device_id_type=MESH_ID,
        )
        item.start()
        return item

    inner = pl.ds(Z_BASE, LOCAL_Z)
    axial = [
        copy(side, packed.at[side], landed.at[side], row, target)
        for side, target in ((0, right), (1, left))
    ]
    rest = [
        copy(2, velocity.at[:, pl.ds(LOCAL_T - 3, 3)], flow.at[:, pl.ds(0, 3), inner], above, column),
        copy(3, velocity.at[:, pl.ds(0, 3)], flow.at[:, pl.ds(LOCAL_T + 3, 3), inner], below, column),
    ]
    for side, target in ((0, right), (1, left)):
        for end, r in ((0, above), (1, below)):
            n = 2 * side + end
            rest.append(copy(4 + n, corners.at[0, n], corners.at[1, n], r, target))
    fetches[1].start()
    fetches[2].start()

    def finish_axial():
        for item in axial:
            item.wait()
        for side, first in ((0, Z_BASE - 3), (1, Z_BASE + LOCAL_Z)):
            for comp in range(3):
                for z in range(3):
                    flow[comp, pl.ds(3, LOCAL_T), first + z, :] = landed[side, 3 * comp + z]

    def finish_rest():
        for item in rest:
            item.wait()
        for side, near, far in ((0, Z_BASE - 1, Z_BASE - 2), (1, Z_BASE + LOCAL_Z, Z_BASE + LOCAL_Z + 1)):
            for comp in range(3):
                low, high = corners.at[1, 2 * side, comp], corners.at[1, 2 * side + 1, comp]
                for t, line, z in ((1, 6, near), (2, 7, near), (2, 5, far)):
                    flow[comp, t, pl.ds(z, 1), :] = low[pl.ds(line, 1), :]
                for t, line, z in ((0, 0, near), (1, 1, near), (0, 2, far)):
                    flow[comp, LOCAL_T + 3 + t, pl.ds(z, 1), :] = high[pl.ds(line, 1), :]

    return finish_axial, finish_rest


def read_flow(flow, comp, t, q):
    return flow[comp, t, pl.ds(Z_BASE + q, 8, stride=Z_STEP), :]


def strain_rows(flow, tensor, radial, inner):
    def strain_row(step, carry):
        n = step + 3 if inner else step + (LOCAL_T - 2) * (step // 3)
        centre = [[read_flow(flow, c, n + 1, q) for q in range(-3, Z_STEP + 3)] for c in range(3)]
        for i in range(S_COLS):
            u = [centre[c][i + 1] for c in range(3)]
            dz = [(centre[c][i + 2] - centre[c][i]) * DZ for c in range(3)]
            dt = [
                (read_flow(flow, c, n + 2, i - 2) - read_flow(flow, c, n, i - 2)) * radial[1]
                for c in range(3)
            ]
            dr = [along_radius(u[c], radial) for c in range(3)]
            parts = [
                dr[0],
                dt[1] + u[0] * radial[0],
                dz[2],
                0.5 * (dr[1] - u[1] * radial[0] + dt[0]),
                0.5 * (dz[0] + dr[2]),
                0.5 * (dt[2] + dz[1]),
            ]
            for k in range(6):
                tensor[k, n, i] = parts[k]
            tensor[6, n, i] = tensor_magnitude(parts)
        return carry

    lax.fori_loop(0, LOCAL_T - 2 if inner else 6, strain_row, 0, unroll=2)


def filter_rows(flow, tensor, state, filtered):
    span = range(-1, Z_STEP + 1)

    def across(n):
        flows = [[read_flow(flow, c, n + 1, q) for q in span] for c in range(3)]
        for c in range(3):
            yield flows[c]
        for a, b in zip(pair_first, pair_second):
            yield [x * y for x, y in zip(flows[a], flows[b])]
        for k in range(6):
            yield [tensor[k, n, q + 2] for q in span]
        for k in range(6):
            yield [tensor[k, n, q + 2] * tensor[6, n, q + 2] for q in span]

    def axial(values):
        pairs = [x + y for x, y in zip(values[:-1], values[1:])]
        return [x + y for x, y in zip(pairs[:-1], pairs[1:])]

    def first_rows():
        for f, (one, two) in enumerate(zip(across(1), across(2))):
            one, two = axial(one), axial(two)
            for q in range(Z_STEP):
                state[0, f, q] = two[q]
                state[1, f, q] = one[q] + two[q]

    def pair_rows(step, carry):
        n = 3 + 2 * step
        for f, (one, two) in enumerate(zip(across(n), across(n + 1))):
            one, two = axial(one), axial(two)
            for q in range(Z_STEP):
                before = state[0, f, q] + one[q]
                after = one[q] + two[q]
                filtered[f, q] = state[1, f, q] + before
                filtered[f, Z_STEP + q] = before + after
                state[0, f, q] = two[q]
                state[1, f, q] = after
        numer, denom = carry
        for q in range(2 * Z_STEP):
            means = [filtered[c, q] for c in range(3)]
            smooth = [filtered[9 + k, q] for k in range(6)]
            size = tensor_magnitude(smooth) * (filter_ratio / 16.0)
            lm, mm = [], []
            for k in range(6):
                leonard = filtered[3 + k, q] - means[pair_first[k]] * means[pair_second[k]] * (1.0 / 16.0)
                model = size * smooth[k] - filtered[15 + k, q]
                lm.append(leonard * model)
                mm.append(model * model)
            numer = numer + (lm[0] + lm[1] + lm[2]) + 2.0 * (lm[3] + lm[4] + lm[5])
            denom = denom + (mm[0] + mm[1] + mm[2]) + 2.0 * (mm[3] + mm[4] + mm[5])
        return numer, denom

    first_rows()
    zero = jnp.zeros((8, NR), jnp.float32)
    return lax.fori_loop(0, LOCAL_T // 2, pair_rows, (zero, zero))


def sum_everywhere(numer, denom, row_sums, all_sums, send_sem, recv_sem):
    row, column = lax.axis_index("theta"), lax.axis_index("gz")
    first = lax.broadcasted_iota(jnp.int32, (8, NR), 0) == 0
    tile = jnp.where(
        first, jnp.sum(numer, axis=0, keepdims=True), jnp.sum(denom, axis=0, keepdims=True)
    )

    def share(buffer, tile, place, count, target, step):
        buffer[place] = tile

        def send(i, carry):
            pltpu.make_async_remote_copy(
                src_ref=buffer.at[place],
                dst_ref=buffer.at[place],
                send_sem=send_sem.at[step],
                recv_sem=recv_sem.at[step],
                device_id=target(lax.rem(place + i, count)),
                device_id_type=MESH_ID,
            ).start()
            return carry

        lax.fori_loop(1, count, send, 0)
        others = buffer.at[pl.ds(0, count - 1)]
        wait_bytes(others, recv_sem.at[step])
        wait_bytes(others, send_sem.at[step])
        total = buffer[0]
        for i in range(1, count):
            total = total + buffer[i]
        return total

    tile = share(row_sums, tile, row, THETA_COUNT, lambda i: device(i, column), 0)
    tile = share(all_sums, tile, column, GZ_COUNT, lambda i: device(row, i), 1)
    return tile[0:1], tile[1:2]


def stress_rows(tensor, ratio, eddy):
    def stress_row(n, carry):
        for i in range(S_COLS):
            viscosity = eddy * tensor[6, n, i]
            scale = 2.0 * viscosity + 2.0 * nu_molecular
            for k in range(6):
                tensor[k, n, i] = tensor[k, n, i] * scale
        return carry

    def ratio_row(t, carry):
        for q in range(Z_STEP):
            value = eddy * tensor[6, t + 2, q + 2] * (1.0 / nu_molecular)
            ratio[t, pl.ds(q, 8, stride=Z_STEP), :] = value
        return carry

    lax.fori_loop(0, LOCAL_T, ratio_row, 0)
    lax.fori_loop(0, S_ROWS, stress_row, 0, unroll=2)


def source_rows(flow, tensor, swirl, partial, source, radial):
    def swirl_row(n, carry):
        for q in range(Z_STEP):
            i = q + 2
            shear = tensor[3, n, i]
            force = (
                along_radius(shear, radial)
                + (tensor[1, n + 1, i] - tensor[1, n - 1, i]) * radial[1]
                + (tensor[5, n, i + 1] - tensor[5, n, i - 1]) * DZ
                + 2.0 * shear * radial[0]
            )
            swirl[n - 1, q] = read_flow(flow, 1, n + 1, q) + time_step * force
        return carry

    def other_row(t, carry):
        n = t + 2
        axial = []
        for q in range(-1, Z_STEP + 1):
            i = q + 2
            shear = tensor[4, n, i]
            force = (
                along_radius(shear, radial)
                + (tensor[5, n + 1, i] - tensor[5, n - 1, i]) * radial[1]
                + (tensor[2, n, i + 1] - tensor[2, n, i - 1]) * DZ
                + shear * radial[0]
            )
            axial.append(read_flow(flow, 2, n + 1, q) + time_step * force)
        for q in range(Z_STEP):
            i = q + 2
            normal = tensor[0, n, i]
            force = (
                along_radius(normal, radial)
                + (tensor[3, n + 1, i] - tensor[3, n - 1, i]) * radial[1]
                + (tensor[4, n, i + 1] - tensor[4, n, i - 1]) * DZ
                + (normal - tensor[1, n, i]) * radial[0]
            )
            outward = (read_flow(flow, 0, n + 1, q) + time_step * force) * radial[5]
            partial[t, q] = along_radius(outward, radial) * radial[0] + (axial[q + 2] - axial[q]) * DZ
        return carry

    def join_row(t, carry):
        for q in range(Z_STEP):
            value = partial[t, q] + (swirl[t + 2, q] - swirl[t, q]) * radial[1]
            source[:, q * LOCAL_T + t, :] = value
        return carry

    lax.fori_loop(1, S_ROWS - 1, swirl_row, 0, unroll=2)
    lax.fori_loop(0, LOCAL_T, other_row, 0, unroll=4)
    lax.fori_loop(0, LOCAL_T, join_row, 0, unroll=2)


def split_table(table):
    parts, rest = [], table
    for _ in range(3):
        part = rest.astype(np.float32).astype(ml_dtypes.bfloat16)
        parts.append(part)
        rest = rest - part.astype(np.float64)
    return np.stack(parts)


def axial_table():
    order = np.arange(NZ)
    block, rest = order // LOCAL_Z, order % LOCAL_Z
    cells = block * LOCAL_Z + 4 * (rest % 8) + rest // 8
    angle = 2.0 * np.pi * ((np.arange(NZ)[:, None] * cells[None, :]) % NZ) / NZ
    return split_table(np.concatenate([np.cos(angle), np.sin(angle)], axis=0))


def cycle_table():
    angle = 2.0 * np.pi * ((np.arange(NTH)[:, None] * np.arange(NTH)[None, :]) % NTH) / NTH
    scale = 1.0 / math.sqrt(NTH * NZ)
    cosine = (np.cos(angle) * scale).reshape(NTH, GZ_COUNT, LOCAL_M)
    sine = (np.sin(angle) * scale).reshape(NTH, GZ_COUNT, LOCAL_M)
    upper = np.stack([cosine, -sine], axis=2)
    lower = np.stack([-sine, -cosine], axis=2)
    both = np.concatenate([upper, lower], axis=0)[:, [0, 2, 1, 3, 4, 6, 5, 7]]
    both = both.reshape(2 * NTH, GZ_COUNT // 2, 4 * LOCAL_M)
    return split_table(np.moveaxis(both, 1, 0))


def split_value(value):
    parts = []
    for _ in range(3):
        part = value.astype(jnp.bfloat16)
        parts.append(part)
        value = value - part.astype(jnp.float32)
    return parts


def product(left, right):
    total = None
    for i, j in ((0, 2), (2, 0), (1, 1), (0, 1), (1, 0), (0, 0)):
        term = jnp.dot(left[i], right[j], preferred_element_type=jnp.float32)
        total = term if total is None else total + term
    return total


def spectral_part(
    tiles,
    modes,
    planes,
    plane,
    axial,
    cycle,
    left,
    spectrum,
    fetch_axial,
    fetch_cycle,
    send_sem,
    recv_sem,
    out_send_sem,
    out_recv_sem,
    own_sem,
):
    row, column = lax.axis_index("theta"), lax.axis_index("gz")
    me = row * GZ_COUNT + column

    def send_tile(i, carry):
        target = lax.rem(me + i, DEVICES)
        pltpu.make_async_remote_copy(
            src_ref=tiles.at[target],
            dst_ref=planes.at[me],
            send_sem=send_sem,
            recv_sem=recv_sem,
            device_id={"theta": target // GZ_COUNT, "gz": lax.rem(target, GZ_COUNT)},
            device_id_type=MESH_ID,
        ).start()
        return carry

    lax.fori_loop(1, DEVICES, send_tile, 0)
    planes[me] = tiles[me]
    wait_bytes(planes.at[pl.ds(0, DEVICES - 1)], recv_sem)
    wait_bytes(planes.at[pl.ds(0, DEVICES - 1)], send_sem)

    group = lax.broadcasted_iota(jnp.int32, (8, 128), 1) // LOCAL_T

    def gather_lines(c, carry):
        for quad in range(THETA_COUNT // 4):
            parts = [planes[(4 * quad + b) * GZ_COUNT + c] for b in range(4)]
            for z in range(4):
                turned = [
                    parts[b] if b == z else pltpu.roll(parts[b], ((b - z) * LOCAL_T) % 128, 1)
                    for b in range(4)
                ]
                value = jnp.where(
                    group < 2,
                    jnp.where(group == 0, turned[0], turned[1]),
                    jnp.where(group == 2, turned[2], turned[3]),
                )
                start = pl.multiple_of(c * LOCAL_Z + 8 * z, 8)
                plane[pl.ds(start, 8), 128 * quad : 128 * quad + 128] = value
        return carry

    lax.fori_loop(0, GZ_COUNT, gather_lines, 0)
    fetch_axial.wait()
    lines = product(axial, split_value(plane[...]))
    for n, part in enumerate(split_value(lines)):
        left[n, :, :NTH] = part[:NZ]
        left[n, :, NTH:] = part[NZ:]
    fetch_cycle.wait()

    def transform(step, carry):
        chunk = lax.rem(2 * (column // 4) + lax.rem(column, 2) + step, GZ_COUNT // 2)
        first = 4 * (chunk // 2) + lax.rem(chunk, 2)
        both = product(left, cycle.at[:, chunk])
        spectrum[first] = both[:, :128]
        spectrum[first + 2] = both[:, 128:]

        def send_modes(i, inner):
            target_column = first + 2 * lax.rem(i, 2)
            target_row = lax.rem(row + i // 2, THETA_COUNT)
            rows = pl.ds(pl.multiple_of(target_row * LOCAL_K, LOCAL_K), LOCAL_K)

            @pl.when(jnp.logical_or(target_row != row, target_column != column))
            def _():
                pltpu.make_async_remote_copy(
                    src_ref=spectrum.at[target_column, rows],
                    dst_ref=modes.at[me],
                    send_sem=out_send_sem,
                    recv_sem=out_recv_sem,
                    device_id={"theta": target_row, "gz": target_column},
                    device_id_type=MESH_ID,
                ).start()

            return inner

        lax.fori_loop(0, 2 * THETA_COUNT, send_modes, 0)
        return carry

    lax.fori_loop(0, GZ_COUNT // 2, transform, 0)
    own_rows = pl.ds(pl.multiple_of(row * LOCAL_K, LOCAL_K), LOCAL_K)
    keep = pltpu.make_async_copy(spectrum.at[column, own_rows], modes.at[me], own_sem)
    keep.start()
    keep.wait()
    wait_bytes(modes.at[pl.ds(0, DEVICES - 1)], out_send_sem)
    wait_bytes(modes.at[pl.ds(0, DEVICES - 1)], out_recv_sem)


def step_kernel(
    velocity,
    radial_hbm,
    axial_hbm,
    cycle_hbm,
    ratio,
    modes,
    inverse,
    radial,
    flow,
    packed,
    landed,
    corners,
    tensor,
    state,
    filtered,
    row_sums,
    all_sums,
    swirl,
    partial,
    source,
    tiles,
    planes,
    plane,
    axial,
    cycle,
    left,
    spectrum,
    load_sem,
    send_sem,
    recv_sem,
    sum_send_sem,
    sum_recv_sem,
    move_sem,
):
    fetches = [
        pltpu.make_async_copy(source_ref, target, load_sem.at[n])
        for n, (source_ref, target) in enumerate(
            ((radial_hbm, radial), (axial_hbm, axial), (cycle_hbm, cycle)), 1
        )
    ]
    finish_axial, finish_rest = exchange(
        velocity, flow, packed, landed, corners, load_sem.at[0], send_sem, recv_sem, fetches
    )
    factor_rows(inverse)
    fetches[0].wait()
    finish_axial()
    strain_rows(flow, tensor, radial, True)
    finish_rest()
    strain_rows(flow, tensor, radial, False)
    numer, denom = filter_rows(flow, tensor, state, filtered)
    numer, denom = sum_everywhere(numer, denom, row_sums, all_sums, sum_send_sem, sum_recv_sem)
    width = radial[4][0:1]
    numer = numer * (width * (2.0 / 256.0))
    denom = denom * (width * width * (4.0 / 256.0))
    coefficient = numer / (denom + epsilon_den)
    eddy = jnp.broadcast_to(coefficient * width, (8, NR))
    stress_rows(tensor, ratio, eddy)
    source_rows(flow, tensor, swirl, partial, source, radial)
    for s in range(8):
        tiles[:, s, :] = source[s].T
    spectral_part(
        tiles,
        modes,
        planes,
        plane,
        axial,
        cycle,
        left,
        spectrum,
        fetches[1],
        fetches[2],
        *(move_sem.at[n] for n in range(5)),
    )


def step(velocity):
    vmem = pl.BlockSpec(memory_space=pltpu.VMEM)
    hbm = pl.BlockSpec(memory_space=pltpu.HBM)
    return pl.pallas_call(
        step_kernel,
        out_shape=(
            jax.ShapeDtypeStruct((LOCAL_T, LOCAL_Z, NR), jnp.float32),
            jax.ShapeDtypeStruct((DEVICES, LOCAL_K, 128), jnp.float32),
            jax.ShapeDtypeStruct((NR, LOCAL_K, 128), jnp.float32),
        ),
        in_specs=[hbm, hbm, hbm, hbm],
        out_specs=(vmem, vmem, vmem),
        scratch_shapes=[
            pltpu.VMEM((6, 8, NR), jnp.float32),
            pltpu.VMEM((3, T_ROWS, Z_ROWS, NR), jnp.float32),
            pltpu.VMEM((2, 9, LOCAL_T, NR), jnp.float32),
            pltpu.VMEM((2, 9, LOCAL_T, NR), jnp.float32),
            pltpu.VMEM((2, 4, 3, 8, NR), jnp.float32),
            pltpu.VMEM((7, S_ROWS, S_COLS, 8, NR), jnp.float32),
            pltpu.VMEM((2, 21, Z_STEP, 8, NR), jnp.float32),
            pltpu.VMEM((21, 2 * Z_STEP, 8, NR), jnp.float32),
            pltpu.VMEM((THETA_COUNT, 8, NR), jnp.float32),
            pltpu.VMEM((GZ_COUNT, 8, NR), jnp.float32),
            pltpu.VMEM((LOCAL_T + 2, Z_STEP, 8, NR), jnp.float32),
            pltpu.VMEM((LOCAL_T, Z_STEP, 8, NR), jnp.float32),
            pltpu.VMEM((8, 4 * LOCAL_T, NR), jnp.float32),
            pltpu.VMEM((NR, 8, 4 * LOCAL_T), jnp.float32),
            pltpu.VMEM((DEVICES, 8, 128), jnp.float32),
            pltpu.VMEM((NZ, NTH), jnp.float32),
            pltpu.VMEM((3, 2 * NZ, NZ), jnp.bfloat16),
            pltpu.VMEM((3, GZ_COUNT // 2, 2 * NTH, 4 * LOCAL_M), jnp.bfloat16),
            pltpu.VMEM((3, NZ, 2 * NTH), jnp.bfloat16),
            pltpu.VMEM((GZ_COUNT, NZ, 128), jnp.float32),
            pltpu.SemaphoreType.DMA((4,)),
            pltpu.SemaphoreType.DMA((8,)),
            pltpu.SemaphoreType.DMA((8,)),
            pltpu.SemaphoreType.DMA((2,)),
            pltpu.SemaphoreType.DMA((2,)),
            pltpu.SemaphoreType.DMA((5,)),
        ],
        compiler_params=pltpu.CompilerParams(
            collective_id=0, has_side_effects=True, vmem_limit_bytes=48 << 20
        ),
        name="step",
    )(
        *(
            pltpu.with_memory_space_constraint(jnp.asarray(value), pltpu.HBM)
            for value in (velocity, radial_table(), axial_table(), cycle_table())
        )
    )


def diagonals():
    row, column = lax.axis_index("theta"), lax.axis_index("gz")
    shape = (LOCAL_K, 128)
    theta_mode = column * LOCAL_M + lax.broadcasted_iota(jnp.int32, shape, 1) % LOCAL_M
    axial_mode = row * LOCAL_K + lax.broadcasted_iota(jnp.int32, shape, 0)
    theta_wave = jnp.minimum(theta_mode, NTH - theta_mode).astype(jnp.float32)
    axial_wave = jnp.minimum(axial_mode, NZ - axial_mode).astype(jnp.float32) * (
        2.0 * math.pi / pipe_length
    )
    theta_sq = theta_wave * theta_wave
    axial_sq = axial_wave * axial_wave * (1.0 / (NR * NR))

    def diagonal(i):
        middle = i + 0.5
        extra = float(NR) if i == NR - 1 else 0.0
        return theta_sq * (1.0 / middle) + (axial_sq * middle + (2.0 * i + 1.0 + extra))

    return diagonal


def factor_rows(inverse):
    diagonal = diagonals()
    low, high = diagonal(0), diagonal(NR - 1)
    for i in range(1, HALF):
        j = NR - 1 - i
        low_inverse, high_inverse = 1.0 / low, 1.0 / high
        inverse[i - 1] = low_inverse
        inverse[j + 1] = high_inverse
        low = diagonal(i) - low_inverse * float(i * i)
        high = diagonal(j) - high_inverse * float((j + 1) * (j + 1))
    inverse[HALF - 1] = low
    inverse[HALF] = high


def solve_kernel(modes, inverse, ratio_ref, out_ref, ratio_out, partial, pressure, ratio_sem):
    keep = pltpu.make_async_copy(ratio_ref, ratio_out, ratio_sem)
    keep.start()

    def load(i):
        return modes[i] * (-(i + 0.5) / (NR * NR))

    low, high = load(0), load(NR - 1)
    for i in range(1, HALF):
        j = NR - 1 - i
        partial[i - 1] = low
        partial[j + 1] = high
        low = load(i) + (inverse[i - 1] * float(i)) * low
        high = load(j) + (inverse[j + 1] * float(j + 1)) * high
    top, bottom = inverse[HALF - 1], inverse[HALF]
    scale = 1.0 / (top * bottom - float(HALF * HALF))
    low, high = (
        (low * bottom + float(HALF) * high) * scale,
        (high * top + float(HALF) * low) * scale,
    )
    pressure[HALF - 1] = low
    pressure[HALF] = high
    for step in range(1, HALF):
        i, j = HALF - 1 - step, HALF + step
        low = (partial[i] + float(i + 1) * low) * inverse[i]
        high = (partial[j] + float(j) * high) * inverse[j]
        pressure[i] = low
        pressure[j] = high
    for k in range(LOCAL_K):
        out_ref[:, k, :] = pressure[:, k, :].T
    keep.wait()


def solve(modes, inverse, ratio):
    vmem = pl.BlockSpec(memory_space=pltpu.VMEM)
    anywhere = pl.BlockSpec(memory_space=pl.ANY)
    pressure, ratio = pl.pallas_call(
        solve_kernel,
        out_shape=(
            jax.ShapeDtypeStruct((2 * LOCAL_M, LOCAL_K, NR), jnp.float32),
            jax.ShapeDtypeStruct((LOCAL_T, LOCAL_Z, NR), jnp.float32),
        ),
        in_specs=[vmem, vmem, anywhere],
        out_specs=(vmem, pl.BlockSpec(memory_space=pltpu.HBM)),
        scratch_shapes=[pltpu.VMEM((NR, LOCAL_K, 128), jnp.float32)] * 2 + [pltpu.SemaphoreType.DMA],
        compiler_params=pltpu.CompilerParams(vmem_limit_bytes=32 << 20),
        name="solve",
    )(modes, inverse, ratio)
    return ratio, pressure.reshape(2, LOCAL_M, LOCAL_K, NR)


def body(velocity):
    ratio, modes, inverse = step(velocity)
    return solve(modes, inverse, ratio)


def solution(mesh):
    return jax.shard_map(
        body,
        mesh=mesh,
        in_specs=(P(None, "theta", "gz", None),),
        out_specs=(P("theta", "gz", None), P(None, "gz", "theta", None)),
        check_vma=False,
    )
```

```python
import functools
import math

import jax
import jax.numpy as jnp
import ml_dtypes
import numpy as np
from jax import lax
from jax.experimental import pallas as pl
from jax.experimental.pallas import tpu as pltpu
from jax.sharding import PartitionSpec as P

NTH = 512
NZ = 256
NR = 128


pipe_length = 4.0 * math.pi
nu_molecular = 5e-05
time_step = 2.0
filter_ratio = 4.0
epsilon_den = 1e-06
pair_first = (0, 1, 2, 0, 0, 1)
pair_second = (0, 1, 2, 1, 2, 2)


THETA_COUNT = 16
GZ_COUNT = 8
DEVICES = THETA_COUNT * GZ_COUNT
LOCAL_T = NTH // THETA_COUNT
LOCAL_Z = NZ // GZ_COUNT
LOCAL_M = NTH // GZ_COUNT
LOCAL_K = NZ // THETA_COUNT
MESH_ID = pl.DeviceIdType.MESH
HALF = NR // 2


def wait_bytes(ref, sem):
    pltpu.make_async_copy(ref, ref, sem).wait()


T_ROWS = LOCAL_T + 6
Z_BASE = 8
Z_ROWS = LOCAL_Z + 2 * Z_BASE
Z_STEP = LOCAL_Z // 8
S_ROWS = LOCAL_T + 4
S_COLS = Z_STEP + 4
DT = 0.5 * NTH / (2.0 * math.pi)
DZ = 0.5 * NZ / pipe_length


def radial_table():
    radius = (np.arange(NR) + 0.5) / NR
    width = np.cbrt((1.0 / NR) * radius * (2.0 * np.pi / NTH) * (pipe_length / NZ)) ** 2
    upper = np.full(NR, 0.5 * NR)
    lower = upper.copy()
    upper[-1] = 0.0
    lower[0] = 0.0
    rows = np.stack(
        [
            1.0 / radius,
            DT / radius,
            upper,
            lower,
            width,
            radius,
            upper / radius,
            lower / radius,
            time_step * radius,
            2.0 * width,
            (filter_ratio / 8.0) * width,
            time_step * DT / radius,
        ]
    )
    return np.broadcast_to(rows[:, None, :], (12, 8, NR)).astype(np.float32)


def along_radius(field, radial):
    return pltpu.roll(field, NR - 1, 1) * radial[2] - pltpu.roll(field, 1, 1) * radial[3]


def tensor_magnitude(t):
    diagonal = t[0] * t[0] + t[1] * t[1] + t[2] * t[2]
    mixed = t[3] * t[3] + t[4] * t[4] + t[5] * t[5]
    return jnp.sqrt(2.0 * diagonal + 4.0 * mixed)


def neighbours(row, column):
    below, above = lax.rem(row + THETA_COUNT - 1, THETA_COUNT), lax.rem(row + 1, THETA_COUNT)
    left, right = lax.rem(column + GZ_COUNT - 1, GZ_COUNT), lax.rem(column + 1, GZ_COUNT)
    return below, above, left, right


def device(row, column):
    return {"theta": row, "gz": column}


def exchange(velocity, flow, packed, landed, corners, load_sem, send_sem, recv_sem, fetches):
    row, column = lax.axis_index("theta"), lax.axis_index("gz")
    below, above, left, right = neighbours(row, column)
    barrier = pltpu.get_barrier_semaphore()

    def greet_row(i, carry):
        target = lax.rem(row + i, THETA_COUNT)
        pl.semaphore_signal(barrier, inc=1, device_id=device(target, column), device_id_type=MESH_ID)
        return carry

    def greet_column(i, carry):
        target = lax.rem(column + i, GZ_COUNT)
        pl.semaphore_signal(barrier, inc=1, device_id=device(row, target), device_id_type=MESH_ID)
        return carry

    load = pltpu.make_async_copy(
        velocity, flow.at[:, pl.ds(3, LOCAL_T), pl.ds(Z_BASE, LOCAL_Z), :], load_sem
    )
    load.start()
    fetches[0].start()
    lax.fori_loop(1, THETA_COUNT, greet_row, 0)
    lax.fori_loop(1, GZ_COUNT, greet_column, 0)
    for r in (below, above):
        for c in (left, right):
            pl.semaphore_signal(barrier, inc=1, device_id=device(r, c), device_id_type=MESH_ID)
    load.wait()
    for side, first in ((0, Z_BASE + LOCAL_Z - 3), (1, Z_BASE)):
        for comp in range(3):
            for z in range(3):
                packed[side, 3 * comp + z] = flow[comp, pl.ds(3, LOCAL_T), first + z, :]
    sublane = lax.broadcasted_iota(jnp.int32, (8, NR), 0)
    for side, near in ((0, 2), (1, 0)):
        for comp in range(3):
            for end, start, put, shift in ((0, LOCAL_T - 8, 5, 6), (1, 0, 2, 2)):
                tile = packed[side, 3 * comp + near, pl.ds(start, 8), :]
                other = packed[side, 3 * comp + 1, pl.ds(start, 8), :]
                corners[0, 2 * side + end, comp] = jnp.where(
                    sublane == put, pltpu.roll(other, shift, 0), tile
                )
    pl.semaphore_wait(barrier, THETA_COUNT + GZ_COUNT + 2)

    def copy(n, source, target, r, c):
        item = pltpu.make_async_remote_copy(
            src_ref=source,
            dst_ref=target,
            send_sem=send_sem.at[n],
            recv_sem=recv_sem.at[n],
            device_id=device(r, c),
            device_id_type=MESH_ID,
        )
        item.start()
        return item

    inner = pl.ds(Z_BASE, LOCAL_Z)
    axial = [
        copy(side, packed.at[side], landed.at[side], row, target)
        for side, target in ((0, right), (1, left))
    ]
    rest = [
        copy(2, velocity.at[:, pl.ds(LOCAL_T - 3, 3)], flow.at[:, pl.ds(0, 3), inner], above, column),
        copy(3, velocity.at[:, pl.ds(0, 3)], flow.at[:, pl.ds(LOCAL_T + 3, 3), inner], below, column),
    ]
    for side, target in ((0, right), (1, left)):
        for end, r in ((0, above), (1, below)):
            n = 2 * side + end
            rest.append(copy(4 + n, corners.at[0, n], corners.at[1, n], r, target))
    fetches[1].start()
    fetches[2].start()

    def finish_axial():
        for item in axial:
            item.wait()
        for side, first in ((0, Z_BASE - 3), (1, Z_BASE + LOCAL_Z)):
            for comp in range(3):
                for z in range(3):
                    flow[comp, pl.ds(3, LOCAL_T), first + z, :] = landed[side, 3 * comp + z]

    def finish_rest():
        for item in rest:
            item.wait()
        for side, near, far in ((0, Z_BASE - 1, Z_BASE - 2), (1, Z_BASE + LOCAL_Z, Z_BASE + LOCAL_Z + 1)):
            for comp in range(3):
                low, high = corners.at[1, 2 * side, comp], corners.at[1, 2 * side + 1, comp]
                for t, line, z in ((1, 6, near), (2, 7, near), (2, 5, far)):
                    flow[comp, t, pl.ds(z, 1), :] = low[pl.ds(line, 1), :]
                for t, line, z in ((0, 0, near), (1, 1, near), (0, 2, far)):
                    flow[comp, LOCAL_T + 3 + t, pl.ds(z, 1), :] = high[pl.ds(line, 1), :]

    return finish_axial, finish_rest


def read_flow(flow, comp, t, q):
    return flow[comp, t, pl.ds(Z_BASE + q, 8, stride=Z_STEP), :]


def strain_rows(flow, tensor, radial, inner):
    def strain_row(step, carry):
        n = step + 3 if inner else step + (LOCAL_T - 2) * (step // 3)
        centre = [[read_flow(flow, c, n + 1, q) for q in range(-3, Z_STEP + 3)] for c in range(3)]
        for i in range(S_COLS):
            u = [centre[c][i + 1] for c in range(3)]
            dz = [(centre[c][i + 2] - centre[c][i]) * DZ for c in range(3)]
            dt = [
                (read_flow(flow, c, n + 2, i - 2) - read_flow(flow, c, n, i - 2)) * radial[1]
                for c in range(3)
            ]
            dr = [along_radius(u[c], radial) for c in range(3)]
            parts = [
                dr[0],
                dt[1] + u[0] * radial[0],
                dz[2],
                0.5 * (dr[1] - u[1] * radial[0] + dt[0]),
                0.5 * (dz[0] + dr[2]),
                0.5 * (dt[2] + dz[1]),
            ]
            size = tensor_magnitude(parts)
            scale = size * radial[9]
            tensor[6, n, i] = size
            for k in range(6):
                tensor[k, n, i] = parts[k]
                tensor[7 + k, n, i] = parts[k] * scale
        return carry

    lax.fori_loop(0, LOCAL_T - 2 if inner else 6, strain_row, 0, unroll=2)


def filter_rows(flow, tensor, state, filtered, radial):
    span = range(-1, Z_STEP + 1)

    def across(n):
        flows = [[read_flow(flow, c, n + 1, q) for q in span] for c in range(3)]
        for c in range(3):
            yield flows[c]
        for a, b in zip(pair_first, pair_second):
            yield [x * y for x, y in zip(flows[a], flows[b])]
        for k in range(6):
            yield [tensor[k, n, q + 2] for q in span]
        for k in range(6):
            yield [tensor[7 + k, n, q + 2] for q in span]

    def axial(values):
        pairs = [x + y for x, y in zip(values[:-1], values[1:])]
        return [x + y for x, y in zip(pairs[:-1], pairs[1:])]

    def first_rows():
        for f, (one, two) in enumerate(zip(across(1), across(2))):
            one, two = axial(one), axial(two)
            for q in range(Z_STEP):
                state[0, f, q] = two[q]
                state[1, f, q] = one[q] + two[q]

    def pair_rows(step, carry):
        n = 3 + 2 * step
        for f, (one, two) in enumerate(zip(across(n), across(n + 1))):
            one, two = axial(one), axial(two)
            for q in range(Z_STEP):
                before = state[0, f, q] + one[q]
                after = one[q] + two[q]
                filtered[f, q] = state[1, f, q] + before
                filtered[f, Z_STEP + q] = before + after
                state[0, f, q] = two[q]
                state[1, f, q] = after
        numer, denom = carry
        for q in range(2 * Z_STEP):
            means = [filtered[c, q] for c in range(3)]
            smooth = [filtered[9 + k, q] for k in range(6)]
            size = tensor_magnitude(smooth) * radial[10]
            lm, mm = [], []
            for k in range(6):
                leonard = filtered[3 + k, q] - means[pair_first[k]] * means[pair_second[k]] * (1.0 / 16.0)
                model = size * smooth[k] - filtered[15 + k, q]
                lm.append(leonard * model)
                mm.append(model * model)
            numer = numer + (lm[0] + lm[1] + lm[2]) + 2.0 * (lm[3] + lm[4] + lm[5])
            denom = denom + (mm[0] + mm[1] + mm[2]) + 2.0 * (mm[3] + mm[4] + mm[5])
        return numer, denom

    first_rows()
    zero = jnp.zeros((8, NR), jnp.float32)
    return lax.fori_loop(0, LOCAL_T // 2, pair_rows, (zero, zero))


def sum_everywhere(numer, denom, row_sums, all_sums, send_sem, recv_sem, meanwhile):
    row, column = lax.axis_index("theta"), lax.axis_index("gz")
    first = lax.broadcasted_iota(jnp.int32, (8, NR), 0) == 0
    tile = jnp.where(
        first, jnp.sum(numer, axis=0, keepdims=True), jnp.sum(denom, axis=0, keepdims=True)
    )

    def share(buffer, tile, place, count, target, step):
        buffer[place] = tile

        def send(i, carry):
            pltpu.make_async_remote_copy(
                src_ref=buffer.at[place],
                dst_ref=buffer.at[place],
                send_sem=send_sem.at[step],
                recv_sem=recv_sem.at[step],
                device_id=target(lax.rem(place + i, count)),
                device_id_type=MESH_ID,
            ).start()
            return carry

        lax.fori_loop(1, count, send, 0)
        meanwhile[step]()
        others = buffer.at[pl.ds(0, count - 1)]
        wait_bytes(others, recv_sem.at[step])
        wait_bytes(others, send_sem.at[step])
        total = buffer[0]
        for i in range(1, count):
            total = total + buffer[i]
        return total

    tile = share(row_sums, tile, row, THETA_COUNT, lambda i: device(i, column), 0)
    tile = share(all_sums, tile, column, GZ_COUNT, lambda i: device(row, i), 1)
    return tile[0:1], tile[1:2]


def force_parts(field, radial, cross):
    still, moved = field
    rest = along_radius(still, radial) + cross(0)
    outer = pltpu.roll(moved, NR - 1, 1) * radial[2]
    inner = pltpu.roll(moved, 1, 1) * radial[3]
    return rest * (2.0 * nu_molecular * time_step), cross(7), outer, inner


def swirl_rows(flow, tensor, swirl, radial):
    def swirl_row(n, carry):
        for q in range(Z_STEP):
            i = q + 2

            def cross(k):
                return (
                    (tensor[k + 1, n + 1, i] - tensor[k + 1, n - 1, i]) * radial[1]
                    + (tensor[k + 5, n, i + 1] - tensor[k + 5, n, i - 1]) * DZ
                    + 2.0 * tensor[k + 3, n, i] * radial[0]
                )

            rest, here, outer, inner = force_parts((tensor[3, n, i], tensor[10, n, i]), radial, cross)
            swirl[0, n - 1, q] = read_flow(flow, 1, n + 1, q) + rest
            swirl[1, n - 1, q] = here
            swirl[2, n - 1, q] = outer
            swirl[3, n - 1, q] = inner
        return carry

    lax.fori_loop(1, S_ROWS - 1, swirl_row, 0, unroll=2)


def form_rows(flow, tensor, form, radial, start, stop):
    def form_row(t, carry):
        n = t + 2
        axial = []
        for q in range(-1, Z_STEP + 1):
            i = q + 2

            def cross(k):
                return (
                    (tensor[k + 5, n + 1, i] - tensor[k + 5, n - 1, i]) * radial[1]
                    + (tensor[k + 2, n, i + 1] - tensor[k + 2, n, i - 1]) * DZ
                    + tensor[k + 4, n, i] * radial[0]
                )

            rest, here, outer, inner = force_parts((tensor[4, n, i], tensor[11, n, i]), radial, cross)
            axial.append((read_flow(flow, 2, n + 1, q) + rest, here, outer, inner))
        for q in range(Z_STEP):
            i = q + 2

            def cross(k):
                return (
                    (tensor[k + 3, n + 1, i] - tensor[k + 3, n - 1, i]) * radial[1]
                    + (tensor[k + 4, n, i + 1] - tensor[k + 4, n, i - 1]) * DZ
                    + (tensor[k, n, i] - tensor[k + 1, n, i]) * radial[0]
                )

            rest, here, outer, inner = force_parts((tensor[0, n, i], tensor[7, n, i]), radial, cross)
            rest = (read_flow(flow, 0, n + 1, q) + rest) * radial[5]
            here, outer, inner = (value * radial[8] for value in (here, outer, inner))

            def out(value):
                return pltpu.roll(value, NR - 1, 1) * radial[6]

            def back(value):
                return pltpu.roll(value, 1, 1) * radial[7]

            slope = [(high - low) * DZ for high, low in zip(axial[q + 2], axial[q])]
            form[0, t, q] = slope[0] + (out(rest) - back(rest))
            form[1, t, q] = slope[1] * time_step - (out(inner) + back(outer))
            form[2, t, q] = slope[2] * time_step + out(here)
            form[3, t, q] = slope[3] * time_step + back(here)
            form[4, t, q] = out(outer)
            form[5, t, q] = back(inner)
        return carry

    lax.fori_loop(start, stop, form_row, 0, unroll=2)


def join_rows(swirl, form, radial):
    def join_row(t, carry):
        for k in range(4):
            for q in range(Z_STEP):
                slope = (swirl[k, t + 2, q] - swirl[k, t, q]) * radial[11 if k else 1]
                form[k, t, q] = form[k, t, q] + slope
        return carry

    lax.fori_loop(0, LOCAL_T, join_row, 0, unroll=2)


def source_rows(form, source, coefficient):
    here = jnp.broadcast_to(coefficient, (8, NR))
    outer, inner = pltpu.roll(here, NR - 1, 1), pltpu.roll(here, 1, 1)
    outer_two, inner_two = pltpu.roll(here, NR - 2, 1), pltpu.roll(here, 2, 1)

    def source_row(t, carry):
        for q in range(Z_STEP):
            value = form[0, t, q] + here * form[1, t, q]
            value = value + (outer * form[2, t, q] - inner * form[3, t, q])
            value = value + (outer_two * form[4, t, q] + inner_two * form[5, t, q])
            source[:, q * LOCAL_T + t, :] = value
        return carry

    lax.fori_loop(0, LOCAL_T, source_row, 0, unroll=4)


def ratio_rows(tensor, ratio, radial, coefficient):
    scale = coefficient * (radial[4][0:1] * (1.0 / nu_molecular))
    scale = jnp.broadcast_to(scale, (8, NR))

    def ratio_row(t, carry):
        for q in range(Z_STEP):
            ratio[t, pl.ds(q, 8, stride=Z_STEP), :] = scale * tensor[6, t + 2, q + 2]
        return carry

    lax.fori_loop(0, LOCAL_T, ratio_row, 0, unroll=4)


def split_table(table):
    parts, rest = [], table
    for _ in range(3):
        part = rest.astype(np.float32).astype(ml_dtypes.bfloat16)
        parts.append(part)
        rest = rest - part.astype(np.float64)
    return np.stack(parts)


def axial_table():
    order = np.arange(NZ)
    block, rest = order // LOCAL_Z, order % LOCAL_Z
    cells = block * LOCAL_Z + 4 * (rest % 8) + rest // 8
    angle = 2.0 * np.pi * ((np.arange(NZ)[:, None] * cells[None, :]) % NZ) / NZ
    return split_table(np.concatenate([np.cos(angle), np.sin(angle)], axis=0))


def cycle_table():
    angle = 2.0 * np.pi * ((np.arange(NTH)[:, None] * np.arange(NTH)[None, :]) % NTH) / NTH
    scale = 1.0 / math.sqrt(NTH * NZ)
    cosine = (np.cos(angle) * scale).reshape(NTH, GZ_COUNT, LOCAL_M)
    sine = (np.sin(angle) * scale).reshape(NTH, GZ_COUNT, LOCAL_M)
    upper = np.stack([cosine, -sine], axis=2)
    lower = np.stack([-sine, -cosine], axis=2)
    both = np.concatenate([upper, lower], axis=0)[:, [0, 2, 1, 3, 4, 6, 5, 7]]
    both = both.reshape(2 * NTH, GZ_COUNT // 2, 4 * LOCAL_M)
    return split_table(np.moveaxis(both, 1, 0))


def split_value(value):
    parts = []
    for _ in range(3):
        part = value.astype(jnp.bfloat16)
        parts.append(part)
        value = value - part.astype(jnp.float32)
    return parts


def product(left, right):
    total = None
    for i, j in ((0, 2), (2, 0), (1, 1), (0, 1), (1, 0), (0, 0)):
        term = jnp.dot(left[i], right[j], preferred_element_type=jnp.float32)
        total = term if total is None else total + term
    return total


def spectral_part(
    tiles,
    modes,
    planes,
    plane,
    axial,
    cycle,
    left,
    spectrum,
    fetch_axial,
    fetch_cycle,
    send_sem,
    recv_sem,
    out_send_sem,
    out_recv_sem,
    own_sem,
    meanwhile,
):
    row, column = lax.axis_index("theta"), lax.axis_index("gz")
    me = row * GZ_COUNT + column

    def send_tile(i, carry):
        target = lax.rem(me + i, DEVICES)
        pltpu.make_async_remote_copy(
            src_ref=tiles.at[target],
            dst_ref=planes.at[me],
            send_sem=send_sem,
            recv_sem=recv_sem,
            device_id={"theta": target // GZ_COUNT, "gz": lax.rem(target, GZ_COUNT)},
            device_id_type=MESH_ID,
        ).start()
        return carry

    lax.fori_loop(1, DEVICES, send_tile, 0)
    planes[me] = tiles[me]
    meanwhile()
    wait_bytes(planes.at[pl.ds(0, DEVICES - 1)], recv_sem)
    wait_bytes(planes.at[pl.ds(0, DEVICES - 1)], send_sem)

    group = lax.broadcasted_iota(jnp.int32, (8, 128), 1) // LOCAL_T

    def gather_lines(c, carry):
        for quad in range(THETA_COUNT // 4):
            parts = [planes[(4 * quad + b) * GZ_COUNT + c] for b in range(4)]
            for z in range(4):
                turned = [
                    parts[b] if b == z else pltpu.roll(parts[b], ((b - z) * LOCAL_T) % 128, 1)
                    for b in range(4)
                ]
                value = jnp.where(
                    group < 2,
                    jnp.where(group == 0, turned[0], turned[1]),
                    jnp.where(group == 2, turned[2], turned[3]),
                )
                start = pl.multiple_of(c * LOCAL_Z + 8 * z, 8)
                plane[pl.ds(start, 8), 128 * quad : 128 * quad + 128] = value
        return carry

    lax.fori_loop(0, GZ_COUNT, gather_lines, 0)
    fetch_axial.wait()
    lines = product(axial, split_value(plane[...]))
    for n, part in enumerate(split_value(lines)):
        left[n, :, :NTH] = part[:NZ]
        left[n, :, NTH:] = part[NZ:]
    fetch_cycle.wait()

    def transform(step, carry):
        chunk = lax.rem(2 * (column // 4) + lax.rem(column, 2) + step, GZ_COUNT // 2)
        first = 4 * (chunk // 2) + lax.rem(chunk, 2)
        both = product(left, cycle.at[:, chunk])
        spectrum[first] = both[:, :128]
        spectrum[first + 2] = both[:, 128:]

        def send_modes(i, inner):
            target_column = first + 2 * lax.rem(i, 2)
            target_row = lax.rem(row + i // 2, THETA_COUNT)
            rows = pl.ds(pl.multiple_of(target_row * LOCAL_K, LOCAL_K), LOCAL_K)

            @pl.when(jnp.logical_or(target_row != row, target_column != column))
            def _():
                pltpu.make_async_remote_copy(
                    src_ref=spectrum.at[target_column, rows],
                    dst_ref=modes.at[me],
                    send_sem=out_send_sem,
                    recv_sem=out_recv_sem,
                    device_id={"theta": target_row, "gz": target_column},
                    device_id_type=MESH_ID,
                ).start()

            return inner

        lax.fori_loop(0, 2 * THETA_COUNT, send_modes, 0)
        return carry

    lax.fori_loop(0, GZ_COUNT // 2, transform, 0)
    own_rows = pl.ds(pl.multiple_of(row * LOCAL_K, LOCAL_K), LOCAL_K)
    keep = pltpu.make_async_copy(spectrum.at[column, own_rows], modes.at[me], own_sem)
    keep.start()
    keep.wait()
    wait_bytes(modes.at[pl.ds(0, DEVICES - 1)], out_send_sem)
    wait_bytes(modes.at[pl.ds(0, DEVICES - 1)], out_recv_sem)


def step_kernel(
    velocity,
    radial_hbm,
    axial_hbm,
    cycle_hbm,
    ratio,
    modes,
    inverse,
    radial,
    flow,
    packed,
    landed,
    corners,
    tensor,
    state,
    filtered,
    row_sums,
    all_sums,
    swirl,
    form,
    source,
    tiles,
    planes,
    plane,
    axial,
    cycle,
    left,
    spectrum,
    load_sem,
    send_sem,
    recv_sem,
    sum_send_sem,
    sum_recv_sem,
    move_sem,
):
    fetches = [
        pltpu.make_async_copy(source_ref, target, load_sem.at[n])
        for n, (source_ref, target) in enumerate(
            ((radial_hbm, radial), (axial_hbm, axial), (cycle_hbm, cycle)), 1
        )
    ]
    finish_axial, finish_rest = exchange(
        velocity, flow, packed, landed, corners, load_sem.at[0], send_sem, recv_sem, fetches
    )
    factor_rows(inverse)
    fetches[0].wait()
    finish_axial()
    strain_rows(flow, tensor, radial, True)
    finish_rest()
    strain_rows(flow, tensor, radial, False)
    numer, denom = filter_rows(flow, tensor, state, filtered, radial)

    def first_wait():
        swirl_rows(flow, tensor, swirl, radial)
        form_rows(flow, tensor, form, radial, 0, 10)

    def second_wait():
        form_rows(flow, tensor, form, radial, 10, LOCAL_T)
        join_rows(swirl, form, radial)

    numer, denom = sum_everywhere(
        numer,
        denom,
        row_sums,
        all_sums,
        sum_send_sem,
        sum_recv_sem,
        (first_wait, second_wait),
    )
    coefficient = (numer * (1.0 / 256.0)) / (denom * (1.0 / 256.0) + epsilon_den)
    source_rows(form, source, coefficient)
    for s in range(8):
        tiles[:, s, :] = source[s].T
    spectral_part(
        tiles,
        modes,
        planes,
        plane,
        axial,
        cycle,
        left,
        spectrum,
        fetches[1],
        fetches[2],
        *(move_sem.at[n] for n in range(5)),
        lambda: ratio_rows(tensor, ratio, radial, coefficient),
    )


def step(velocity):
    vmem = pl.BlockSpec(memory_space=pltpu.VMEM)
    hbm = pl.BlockSpec(memory_space=pltpu.HBM)
    return pl.pallas_call(
        step_kernel,
        out_shape=(
            jax.ShapeDtypeStruct((LOCAL_T, LOCAL_Z, NR), jnp.float32),
            jax.ShapeDtypeStruct((DEVICES, LOCAL_K, 128), jnp.float32),
            jax.ShapeDtypeStruct((NR, LOCAL_K, 128), jnp.float32),
        ),
        in_specs=[hbm, hbm, hbm, hbm],
        out_specs=(vmem, vmem, vmem),
        scratch_shapes=[
            pltpu.VMEM((12, 8, NR), jnp.float32),
            pltpu.VMEM((3, T_ROWS, Z_ROWS, NR), jnp.float32),
            pltpu.VMEM((2, 9, LOCAL_T, NR), jnp.float32),
            pltpu.VMEM((2, 9, LOCAL_T, NR), jnp.float32),
            pltpu.VMEM((2, 4, 3, 8, NR), jnp.float32),
            pltpu.VMEM((13, S_ROWS, S_COLS, 8, NR), jnp.float32),
            pltpu.VMEM((2, 21, Z_STEP, 8, NR), jnp.float32),
            pltpu.VMEM((21, 2 * Z_STEP, 8, NR), jnp.float32),
            pltpu.VMEM((THETA_COUNT, 8, NR), jnp.float32),
            pltpu.VMEM((GZ_COUNT, 8, NR), jnp.float32),
            pltpu.VMEM((4, LOCAL_T + 2, Z_STEP, 8, NR), jnp.float32),
            pltpu.VMEM((6, LOCAL_T, Z_STEP, 8, NR), jnp.float32),
            pltpu.VMEM((8, 4 * LOCAL_T, NR), jnp.float32),
            pltpu.VMEM((NR, 8, 4 * LOCAL_T), jnp.float32),
            pltpu.VMEM((DEVICES, 8, 128), jnp.float32),
            pltpu.VMEM((NZ, NTH), jnp.float32),
            pltpu.VMEM((3, 2 * NZ, NZ), jnp.bfloat16),
            pltpu.VMEM((3, GZ_COUNT // 2, 2 * NTH, 4 * LOCAL_M), jnp.bfloat16),
            pltpu.VMEM((3, NZ, 2 * NTH), jnp.bfloat16),
            pltpu.VMEM((GZ_COUNT, NZ, 128), jnp.float32),
            pltpu.SemaphoreType.DMA((4,)),
            pltpu.SemaphoreType.DMA((8,)),
            pltpu.SemaphoreType.DMA((8,)),
            pltpu.SemaphoreType.DMA((2,)),
            pltpu.SemaphoreType.DMA((2,)),
            pltpu.SemaphoreType.DMA((5,)),
        ],
        compiler_params=pltpu.CompilerParams(
            collective_id=0, has_side_effects=True, vmem_limit_bytes=48 << 20
        ),
        name="step",
    )(
        *(
            pltpu.with_memory_space_constraint(jnp.asarray(value), pltpu.HBM)
            for value in (velocity, radial_table(), axial_table(), cycle_table())
        )
    )


def diagonals():
    row, column = lax.axis_index("theta"), lax.axis_index("gz")
    shape = (LOCAL_K, 128)
    theta_mode = column * LOCAL_M + lax.broadcasted_iota(jnp.int32, shape, 1) % LOCAL_M
    axial_mode = row * LOCAL_K + lax.broadcasted_iota(jnp.int32, shape, 0)
    theta_wave = jnp.minimum(theta_mode, NTH - theta_mode).astype(jnp.float32)
    axial_wave = jnp.minimum(axial_mode, NZ - axial_mode).astype(jnp.float32) * (
        2.0 * math.pi / pipe_length
    )
    theta_sq = theta_wave * theta_wave
    axial_sq = axial_wave * axial_wave * (1.0 / (NR * NR))

    def diagonal(i):
        middle = i + 0.5
        extra = float(NR) if i == NR - 1 else 0.0
        return theta_sq * (1.0 / middle) + (axial_sq * middle + (2.0 * i + 1.0 + extra))

    return diagonal


def factor_rows(inverse):
    diagonal = diagonals()
    low, high = diagonal(0), diagonal(NR - 1)
    for i in range(1, HALF):
        j = NR - 1 - i
        low_inverse, high_inverse = 1.0 / low, 1.0 / high
        inverse[i - 1] = low_inverse
        inverse[j + 1] = high_inverse
        low = diagonal(i) - low_inverse * float(i * i)
        high = diagonal(j) - high_inverse * float((j + 1) * (j + 1))
    inverse[HALF - 1] = low
    inverse[HALF] = high


def solve_kernel(modes, inverse, ratio_ref, out_ref, ratio_out, partial, pressure, ratio_sem):
    keep = pltpu.make_async_copy(ratio_ref, ratio_out, ratio_sem)
    keep.start()

    def load(i):
        return modes[i] * (-(i + 0.5) / (NR * NR))

    low, high = load(0), load(NR - 1)
    for i in range(1, HALF):
        j = NR - 1 - i
        partial[i - 1] = low
        partial[j + 1] = high
        low = load(i) + (inverse[i - 1] * float(i)) * low
        high = load(j) + (inverse[j + 1] * float(j + 1)) * high
    top, bottom = inverse[HALF - 1], inverse[HALF]
    scale = 1.0 / (top * bottom - float(HALF * HALF))
    low, high = (
        (low * bottom + float(HALF) * high) * scale,
        (high * top + float(HALF) * low) * scale,
    )
    pressure[HALF - 1] = low
    pressure[HALF] = high
    for step in range(1, HALF):
        i, j = HALF - 1 - step, HALF + step
        low = (partial[i] + float(i + 1) * low) * inverse[i]
        high = (partial[j] + float(j) * high) * inverse[j]
        pressure[i] = low
        pressure[j] = high
    for k in range(LOCAL_K):
        out_ref[:, k, :] = pressure[:, k, :].T
    keep.wait()


def solve(modes, inverse, ratio):
    vmem = pl.BlockSpec(memory_space=pltpu.VMEM)
    anywhere = pl.BlockSpec(memory_space=pl.ANY)
    pressure, ratio = pl.pallas_call(
        solve_kernel,
        out_shape=(
            jax.ShapeDtypeStruct((2 * LOCAL_M, LOCAL_K, NR), jnp.float32),
            jax.ShapeDtypeStruct((LOCAL_T, LOCAL_Z, NR), jnp.float32),
        ),
        in_specs=[vmem, vmem, anywhere],
        out_specs=(vmem, pl.BlockSpec(memory_space=pltpu.HBM)),
        scratch_shapes=[pltpu.VMEM((NR, LOCAL_K, 128), jnp.float32)] * 2 + [pltpu.SemaphoreType.DMA],
        compiler_params=pltpu.CompilerParams(vmem_limit_bytes=32 << 20),
        name="solve",
    )(modes, inverse, ratio)
    return ratio, pressure.reshape(2, LOCAL_M, LOCAL_K, NR)


def body(velocity):
    ratio, modes, inverse = step(velocity)
    return solve(modes, inverse, ratio)


def solution(mesh):
    return jax.shard_map(
        body,
        mesh=mesh,
        in_specs=(P(None, "theta", "gz", None),),
        out_specs=(P("theta", "gz", None), P(None, "gz", "theta", None)),
        check_vma=False,
    )
```

```python
import functools
import math

import jax
import jax.numpy as jnp
import ml_dtypes
import numpy as np
from jax import lax
from jax.experimental import pallas as pl
from jax.experimental.pallas import tpu as pltpu
from jax.sharding import PartitionSpec as P

NTH = 512
NZ = 256
NR = 128


pipe_length = 4.0 * math.pi
nu_molecular = 5e-05
time_step = 2.0
filter_ratio = 4.0
epsilon_den = 1e-06
pair_first = (0, 1, 2, 0, 0, 1)
pair_second = (0, 1, 2, 1, 2, 2)


THETA_COUNT = 16
GZ_COUNT = 8
DEVICES = THETA_COUNT * GZ_COUNT
LOCAL_T = NTH // THETA_COUNT
LOCAL_Z = NZ // GZ_COUNT
LOCAL_M = NTH // GZ_COUNT
LOCAL_K = NZ // THETA_COUNT
MESH_ID = pl.DeviceIdType.MESH
HALF = NR // 2


def wait_bytes(ref, sem):
    pltpu.make_async_copy(ref, ref, sem).wait()


T_ROWS = LOCAL_T + 6
Z_BASE = 8
Z_ROWS = LOCAL_Z + 2 * Z_BASE
Z_STEP = LOCAL_Z // 8
S_ROWS = LOCAL_T + 4
S_COLS = Z_STEP + 4
DT = 0.5 * NTH / (2.0 * math.pi)
DZ = 0.5 * NZ / pipe_length


def radial_table():
    radius = (np.arange(NR) + 0.5) / NR
    width = np.cbrt((1.0 / NR) * radius * (2.0 * np.pi / NTH) * (pipe_length / NZ)) ** 2
    upper = np.full(NR, 0.5 * NR)
    lower = upper.copy()
    upper[-1] = 0.0
    lower[0] = 0.0
    rows = np.stack(
        [
            1.0 / radius,
            DT / radius,
            upper,
            lower,
            width,
            radius,
            upper / radius,
            lower / radius,
            time_step * radius,
            2.0 * width,
            (filter_ratio / 8.0) * width,
            time_step * DT / radius,
        ]
    )
    return np.broadcast_to(rows[:, None, :], (12, 8, NR)).astype(np.float32)


def along_radius(field, radial):
    return pltpu.roll(field, NR - 1, 1) * radial[2] - pltpu.roll(field, 1, 1) * radial[3]


def tensor_magnitude(t):
    diagonal = t[0] * t[0] + t[1] * t[1] + t[2] * t[2]
    mixed = t[3] * t[3] + t[4] * t[4] + t[5] * t[5]
    return jnp.sqrt(2.0 * diagonal + 4.0 * mixed)


def neighbours(row, column):
    below, above = lax.rem(row + THETA_COUNT - 1, THETA_COUNT), lax.rem(row + 1, THETA_COUNT)
    left, right = lax.rem(column + GZ_COUNT - 1, GZ_COUNT), lax.rem(column + 1, GZ_COUNT)
    return below, above, left, right


def device(row, column):
    return {"theta": row, "gz": column}


def exchange(velocity, flow, packed, landed, corners, load_sem, send_sem, recv_sem, fetches):
    row, column = lax.axis_index("theta"), lax.axis_index("gz")
    below, above, left, right = neighbours(row, column)
    barrier = pltpu.get_barrier_semaphore()

    def greet_row(i, carry):
        target = lax.rem(row + i, THETA_COUNT)
        pl.semaphore_signal(barrier, inc=1, device_id=device(target, column), device_id_type=MESH_ID)
        return carry

    def greet_column(i, carry):
        target = lax.rem(column + i, GZ_COUNT)
        pl.semaphore_signal(barrier, inc=1, device_id=device(row, target), device_id_type=MESH_ID)
        return carry

    load = pltpu.make_async_copy(
        velocity, flow.at[:, pl.ds(3, LOCAL_T), pl.ds(Z_BASE, LOCAL_Z), :], load_sem
    )
    load.start()
    fetches[0].start()
    lax.fori_loop(1, THETA_COUNT, greet_row, 0)
    lax.fori_loop(1, GZ_COUNT, greet_column, 0)
    for r in (below, above):
        for c in (left, right):
            pl.semaphore_signal(barrier, inc=1, device_id=device(r, c), device_id_type=MESH_ID)
    load.wait()
    for side, first in ((0, Z_BASE + LOCAL_Z - 2), (1, Z_BASE)):
        for comp in range(3):
            for z in range(2):
                packed[side, 2 * comp + z] = flow[comp, pl.ds(3, LOCAL_T), first + z, :]
    sublane = lax.broadcasted_iota(jnp.int32, (8, NR), 0)
    for side, near in ((0, 1), (1, 0)):
        for comp in range(3):
            for end, start, put, shift in ((0, LOCAL_T - 8, 5, 6), (1, 0, 2, 2)):
                tile = packed[side, 2 * comp + near, pl.ds(start, 8), :]
                other = packed[side, 2 * comp + 1 - near, pl.ds(start, 8), :]
                corners[0, 2 * side + end, comp] = jnp.where(
                    sublane == put, pltpu.roll(other, shift, 0), tile
                )
    pl.semaphore_wait(barrier, THETA_COUNT + GZ_COUNT + 2)

    def copy(n, source, target, r, c):
        item = pltpu.make_async_remote_copy(
            src_ref=source,
            dst_ref=target,
            send_sem=send_sem.at[n],
            recv_sem=recv_sem.at[n],
            device_id=device(r, c),
            device_id_type=MESH_ID,
        )
        item.start()
        return item

    inner = pl.ds(Z_BASE, LOCAL_Z)
    axial = [
        copy(side, packed.at[side], landed.at[side], row, target)
        for side, target in ((0, right), (1, left))
    ]
    rest = [
        copy(2, velocity.at[:, pl.ds(LOCAL_T - 2, 2)], flow.at[:, pl.ds(1, 2), inner], above, column),
        copy(3, velocity.at[:, pl.ds(0, 2)], flow.at[:, pl.ds(LOCAL_T + 3, 2), inner], below, column),
    ]
    for side, target in ((0, right), (1, left)):
        for end, r in ((0, above), (1, below)):
            n = 2 * side + end
            rest.append(copy(4 + n, corners.at[0, n], corners.at[1, n], r, target))
    fetches[1].start()
    fetches[2].start()

    def finish_axial():
        for item in axial:
            item.wait()
        for side, first in ((0, Z_BASE - 2), (1, Z_BASE + LOCAL_Z)):
            for comp in range(3):
                for z in range(2):
                    flow[comp, pl.ds(3, LOCAL_T), first + z, :] = landed[side, 2 * comp + z]

    def finish_rest():
        for item in rest:
            item.wait()
        for side, near, far in ((0, Z_BASE - 1, Z_BASE - 2), (1, Z_BASE + LOCAL_Z, Z_BASE + LOCAL_Z + 1)):
            for comp in range(3):
                low, high = corners.at[1, 2 * side, comp], corners.at[1, 2 * side + 1, comp]
                for t, line, z in ((1, 6, near), (2, 7, near), (2, 5, far)):
                    flow[comp, t, pl.ds(z, 1), :] = low[pl.ds(line, 1), :]
                for t, line, z in ((0, 0, near), (1, 1, near), (0, 2, far)):
                    flow[comp, LOCAL_T + 3 + t, pl.ds(z, 1), :] = high[pl.ds(line, 1), :]

    return finish_axial, finish_rest


def read_flow(flow, comp, t, q):
    return flow[comp, t, pl.ds(Z_BASE + q, 8, stride=Z_STEP), :]


def strain_rows(flow, tensor, radial, inner):
    def strain_row(step, carry):
        n = step + 3 if inner else step + 1 + (LOCAL_T - 2) * (step // 2)
        centre = [[read_flow(flow, c, n + 1, q) for q in range(-2, Z_STEP + 2)] for c in range(3)]
        for i in range(1, S_COLS - 1):
            u = [centre[c][i] for c in range(3)]
            dz = [(centre[c][i + 1] - centre[c][i - 1]) * DZ for c in range(3)]
            dt = [
                (read_flow(flow, c, n + 2, i - 2) - read_flow(flow, c, n, i - 2)) * radial[1]
                for c in range(3)
            ]
            dr = [along_radius(u[c], radial) for c in range(3)]
            parts = [
                dr[0],
                dt[1] + u[0] * radial[0],
                dz[2],
                0.5 * (dr[1] - u[1] * radial[0] + dt[0]),
                0.5 * (dz[0] + dr[2]),
                0.5 * (dt[2] + dz[1]),
            ]
            size = tensor_magnitude(parts)
            scale = size * radial[9]
            tensor[6, n, i] = size
            for k in range(6):
                tensor[k, n, i] = parts[k]
                tensor[7 + k, n, i] = parts[k] * scale
        return carry

    lax.fori_loop(0, LOCAL_T - 2 if inner else 4, strain_row, 0, unroll=2)


def filter_rows(flow, tensor, state, filtered, radial):
    span = range(-1, Z_STEP + 1)

    def across(n):
        flows = [[read_flow(flow, c, n + 1, q) for q in span] for c in range(3)]
        for c in range(3):
            yield flows[c]
        for a, b in zip(pair_first, pair_second):
            yield [x * y for x, y in zip(flows[a], flows[b])]
        for k in range(6):
            yield [tensor[k, n, q + 2] for q in span]
        for k in range(6):
            yield [tensor[7 + k, n, q + 2] for q in span]

    def axial(values):
        pairs = [x + y for x, y in zip(values[:-1], values[1:])]
        return [x + y for x, y in zip(pairs[:-1], pairs[1:])]

    def first_rows():
        for f, (one, two) in enumerate(zip(across(1), across(2))):
            one, two = axial(one), axial(two)
            for q in range(Z_STEP):
                state[0, f, q] = two[q]
                state[1, f, q] = one[q] + two[q]

    def pair_rows(step, carry):
        n = 3 + 2 * step
        for f, (one, two) in enumerate(zip(across(n), across(n + 1))):
            one, two = axial(one), axial(two)
            for q in range(Z_STEP):
                before = state[0, f, q] + one[q]
                after = one[q] + two[q]
                filtered[f, q] = state[1, f, q] + before
                filtered[f, Z_STEP + q] = before + after
                state[0, f, q] = two[q]
                state[1, f, q] = after
        numer, denom = carry
        for q in range(2 * Z_STEP):
            means = [filtered[c, q] for c in range(3)]
            smooth = [filtered[9 + k, q] for k in range(6)]
            size = tensor_magnitude(smooth) * radial[10]
            lm, mm = [], []
            for k in range(6):
                leonard = filtered[3 + k, q] - means[pair_first[k]] * means[pair_second[k]] * (1.0 / 16.0)
                model = size * smooth[k] - filtered[15 + k, q]
                lm.append(leonard * model)
                mm.append(model * model)
            numer = numer + (lm[0] + lm[1] + lm[2]) + 2.0 * (lm[3] + lm[4] + lm[5])
            denom = denom + (mm[0] + mm[1] + mm[2]) + 2.0 * (mm[3] + mm[4] + mm[5])
        return numer, denom

    first_rows()
    zero = jnp.zeros((8, NR), jnp.float32)
    return lax.fori_loop(0, LOCAL_T // 2, pair_rows, (zero, zero))


def sum_everywhere(numer, denom, row_sums, all_sums, send_sem, recv_sem, meanwhile):
    row, column = lax.axis_index("theta"), lax.axis_index("gz")
    first = lax.broadcasted_iota(jnp.int32, (8, NR), 0) == 0
    tile = jnp.where(
        first, jnp.sum(numer, axis=0, keepdims=True), jnp.sum(denom, axis=0, keepdims=True)
    )

    def share(buffer, tile, place, count, target, step):
        buffer[place] = tile

        def send(i, carry):
            pltpu.make_async_remote_copy(
                src_ref=buffer.at[place],
                dst_ref=buffer.at[place],
                send_sem=send_sem.at[step],
                recv_sem=recv_sem.at[step],
                device_id=target(lax.rem(place + i, count)),
                device_id_type=MESH_ID,
            ).start()
            return carry

        lax.fori_loop(1, count, send, 0)
        meanwhile[step]()
        others = buffer.at[pl.ds(0, count - 1)]
        wait_bytes(others, recv_sem.at[step])
        wait_bytes(others, send_sem.at[step])
        total = buffer[0]
        for i in range(1, count):
            total = total + buffer[i]
        return total

    tile = share(row_sums, tile, row, THETA_COUNT, lambda i: device(i, column), 0)
    tile = share(all_sums, tile, column, GZ_COUNT, lambda i: device(row, i), 1)
    return tile[0:1], tile[1:2]


def force_parts(field, radial, cross):
    still, moved = field
    rest = along_radius(still, radial) + cross(0)
    outer = pltpu.roll(moved, NR - 1, 1) * radial[2]
    inner = pltpu.roll(moved, 1, 1) * radial[3]
    return rest * (2.0 * nu_molecular * time_step), cross(7), outer, inner


def face_rows(flow, tensor, swirl, drift, radial):
    def face_row(t, carry):
        n = t + 2
        for q in range(Z_STEP):
            i = q + 2

            def swirl_cross(k):
                return (
                    (tensor[k + 1, n + 1, i] - tensor[k + 1, n - 1, i]) * radial[1]
                    + (tensor[k + 5, n, i + 1] - tensor[k + 5, n, i - 1]) * DZ
                    + 2.0 * tensor[k + 3, n, i] * radial[0]
                )

            def drift_cross(k):
                return (
                    (tensor[k + 5, n + 1, i] - tensor[k + 5, n - 1, i]) * radial[1]
                    + (tensor[k + 2, n, i + 1] - tensor[k + 2, n, i - 1]) * DZ
                    + tensor[k + 4, n, i] * radial[0]
                )

            for comp, k, cross, target in ((1, 3, swirl_cross, swirl), (2, 4, drift_cross, drift)):
                field = (tensor[k, n, i], tensor[k + 7, n, i])
                rest, here, outer, inner = force_parts(field, radial, cross)
                target[0, t + 1, q] = read_flow(flow, comp, n + 1, q) + rest
                target[1, t + 1, q] = here
                target[2, t + 1, q] = outer
                target[3, t + 1, q] = inner
        return carry

    lax.fori_loop(0, LOCAL_T, face_row, 0, unroll=2)


def send_faces(swirl, drift, edges, send_sem, recv_sem):
    row, column = lax.axis_index("theta"), lax.axis_index("gz")
    below, above, left, right = neighbours(row, column)
    for k in range(4):
        edges[0, 0, k] = drift[k, pl.ds(1, LOCAL_T), Z_STEP - 1, 7, :]
        edges[0, 1, k] = drift[k, pl.ds(1, LOCAL_T), 0, 0, :]
    copies = []
    for n, (source, target, r, c) in enumerate(
        (
            (swirl.at[:, LOCAL_T], swirl.at[:, 0], above, column),
            (swirl.at[:, 1], swirl.at[:, LOCAL_T + 1], below, column),
            (edges.at[0, 0], edges.at[1, 0], row, right),
            (edges.at[0, 1], edges.at[1, 1], row, left),
        )
    ):
        item = pltpu.make_async_remote_copy(
            src_ref=source,
            dst_ref=target,
            send_sem=send_sem.at[n],
            recv_sem=recv_sem.at[n],
            device_id=device(r, c),
            device_id_type=MESH_ID,
        )
        item.start()
        copies.append(item)
    return copies


def form_rows(flow, tensor, form, radial):
    def form_row(t, carry):
        n = t + 2
        for q in range(Z_STEP):
            i = q + 2

            def cross(k):
                return (
                    (tensor[k + 3, n + 1, i] - tensor[k + 3, n - 1, i]) * radial[1]
                    + (tensor[k + 4, n, i + 1] - tensor[k + 4, n, i - 1]) * DZ
                    + (tensor[k, n, i] - tensor[k + 1, n, i]) * radial[0]
                )

            rest, here, outer, inner = force_parts((tensor[0, n, i], tensor[7, n, i]), radial, cross)
            rest = (read_flow(flow, 0, n + 1, q) + rest) * radial[5]
            here, outer, inner = (value * radial[8] for value in (here, outer, inner))

            def out(value):
                return pltpu.roll(value, NR - 1, 1) * radial[6]

            def back(value):
                return pltpu.roll(value, 1, 1) * radial[7]

            form[0, t, q] = out(rest) - back(rest)
            form[1, t, q] = -(out(inner) + back(outer))
            form[2, t, q] = out(here)
            form[3, t, q] = back(here)
            form[4, t, q] = out(outer)
            form[5, t, q] = back(inner)
        return carry

    lax.fori_loop(0, LOCAL_T, form_row, 0, unroll=2)


def join_rows(swirl, drift, edges, form, radial):
    sublane = lax.broadcasted_iota(jnp.int32, (8, NR), 0)

    def join_row(t, carry):
        for k in range(4):
            inside = [drift[k, t + 1, q] for q in range(Z_STEP)]
            low = jnp.broadcast_to(edges[1, 0, k, pl.ds(t, 1), :], (8, NR))
            high = jnp.broadcast_to(edges[1, 1, k, pl.ds(t, 1), :], (8, NR))
            low = jnp.where(sublane == 0, low, pltpu.roll(inside[-1], 1, 0))
            high = jnp.where(sublane == 7, high, pltpu.roll(inside[0], 7, 0))
            line = [low] + inside + [high]
            for q in range(Z_STEP):
                around = (swirl[k, t + 2, q] - swirl[k, t, q]) * radial[11 if k else 1]
                along = (line[q + 2] - line[q]) * (DZ * time_step if k else DZ)
                form[k, t, q] = form[k, t, q] + (around + along)
        return carry

    lax.fori_loop(0, LOCAL_T, join_row, 0, unroll=2)


def source_rows(form, source, coefficient):
    here = jnp.broadcast_to(coefficient, (8, NR))
    outer, inner = pltpu.roll(here, NR - 1, 1), pltpu.roll(here, 1, 1)
    outer_two, inner_two = pltpu.roll(here, NR - 2, 1), pltpu.roll(here, 2, 1)

    def source_row(t, carry):
        for q in range(Z_STEP):
            value = form[0, t, q] + here * form[1, t, q]
            value = value + (outer * form[2, t, q] - inner * form[3, t, q])
            value = value + (outer_two * form[4, t, q] + inner_two * form[5, t, q])
            source[:, q * LOCAL_T + t, :] = value
        return carry

    lax.fori_loop(0, LOCAL_T, source_row, 0, unroll=4)


def ratio_rows(tensor, ratio, radial, coefficient):
    scale = coefficient * (radial[4][0:1] * (1.0 / nu_molecular))
    scale = jnp.broadcast_to(scale, (8, NR))

    def ratio_row(t, carry):
        for q in range(Z_STEP):
            ratio[t, pl.ds(q, 8, stride=Z_STEP), :] = scale * tensor[6, t + 2, q + 2]
        return carry

    lax.fori_loop(0, LOCAL_T, ratio_row, 0, unroll=4)


def split_table(table):
    parts, rest = [], table
    for _ in range(3):
        part = rest.astype(np.float32).astype(ml_dtypes.bfloat16)
        parts.append(part)
        rest = rest - part.astype(np.float64)
    return np.stack(parts)


def axial_table():
    order = np.arange(NZ)
    block, rest = order // LOCAL_Z, order % LOCAL_Z
    cells = block * LOCAL_Z + 4 * (rest % 8) + rest // 8
    angle = 2.0 * np.pi * ((np.arange(NZ)[:, None] * cells[None, :]) % NZ) / NZ
    return split_table(np.concatenate([np.cos(angle), np.sin(angle)], axis=0))


def cycle_table():
    angle = 2.0 * np.pi * ((np.arange(NTH)[:, None] * np.arange(NTH)[None, :]) % NTH) / NTH
    scale = 1.0 / math.sqrt(NTH * NZ)
    cosine = (np.cos(angle) * scale).reshape(NTH, GZ_COUNT, LOCAL_M)
    sine = (np.sin(angle) * scale).reshape(NTH, GZ_COUNT, LOCAL_M)
    upper = np.stack([cosine, -sine], axis=2)
    lower = np.stack([-sine, -cosine], axis=2)
    both = np.concatenate([upper, lower], axis=0)[:, [0, 2, 1, 3, 4, 6, 5, 7]]
    both = both.reshape(2 * NTH, GZ_COUNT // 2, 4 * LOCAL_M)
    return split_table(np.moveaxis(both, 1, 0))


def split_value(value):
    parts = []
    for _ in range(3):
        part = value.astype(jnp.bfloat16)
        parts.append(part)
        value = value - part.astype(jnp.float32)
    return parts


def product(left, right):
    total = None
    for i, j in ((0, 2), (2, 0), (1, 1), (0, 1), (1, 0), (0, 0)):
        term = jnp.dot(left[i], right[j], preferred_element_type=jnp.float32)
        total = term if total is None else total + term
    return total


def spectral_part(
    tiles,
    modes,
    planes,
    plane,
    axial,
    cycle,
    left,
    spectrum,
    fetch_axial,
    fetch_cycle,
    send_sem,
    recv_sem,
    out_send_sem,
    out_recv_sem,
    own_sem,
    meanwhile,
):
    row, column = lax.axis_index("theta"), lax.axis_index("gz")
    me = row * GZ_COUNT + column

    def send_tile(i, carry):
        target = lax.rem(me + i, DEVICES)
        pltpu.make_async_remote_copy(
            src_ref=tiles.at[target],
            dst_ref=planes.at[me],
            send_sem=send_sem,
            recv_sem=recv_sem,
            device_id={"theta": target // GZ_COUNT, "gz": lax.rem(target, GZ_COUNT)},
            device_id_type=MESH_ID,
        ).start()
        return carry

    lax.fori_loop(1, DEVICES, send_tile, 0)
    planes[me] = tiles[me]
    meanwhile()
    wait_bytes(planes.at[pl.ds(0, DEVICES - 1)], recv_sem)
    wait_bytes(planes.at[pl.ds(0, DEVICES - 1)], send_sem)

    group = lax.broadcasted_iota(jnp.int32, (8, 128), 1) // LOCAL_T

    def gather_lines(c, carry):
        for quad in range(THETA_COUNT // 4):
            parts = [planes[(4 * quad + b) * GZ_COUNT + c] for b in range(4)]
            for z in range(4):
                turned = [
                    parts[b] if b == z else pltpu.roll(parts[b], ((b - z) * LOCAL_T) % 128, 1)
                    for b in range(4)
                ]
                value = jnp.where(
                    group < 2,
                    jnp.where(group == 0, turned[0], turned[1]),
                    jnp.where(group == 2, turned[2], turned[3]),
                )
                start = pl.multiple_of(c * LOCAL_Z + 8 * z, 8)
                plane[pl.ds(start, 8), 128 * quad : 128 * quad + 128] = value
        return carry

    lax.fori_loop(0, GZ_COUNT, gather_lines, 0)
    fetch_axial.wait()
    lines = product(axial, split_value(plane[...]))
    for n, part in enumerate(split_value(lines)):
        left[n, :, :NTH] = part[:NZ]
        left[n, :, NTH:] = part[NZ:]
    fetch_cycle.wait()

    def transform(step, carry):
        chunk = lax.rem(2 * (column // 4) + lax.rem(column, 2) + step, GZ_COUNT // 2)
        first = 4 * (chunk // 2) + lax.rem(chunk, 2)
        both = product(left, cycle.at[:, chunk])
        spectrum[first] = both[:, :128]
        spectrum[first + 2] = both[:, 128:]

        def send_modes(i, inner):
            target_column = first + 2 * lax.rem(i, 2)
            target_row = lax.rem(row + i // 2, THETA_COUNT)
            rows = pl.ds(pl.multiple_of(target_row * LOCAL_K, LOCAL_K), LOCAL_K)

            @pl.when(jnp.logical_or(target_row != row, target_column != column))
            def _():
                pltpu.make_async_remote_copy(
                    src_ref=spectrum.at[target_column, rows],
                    dst_ref=modes.at[me],
                    send_sem=out_send_sem,
                    recv_sem=out_recv_sem,
                    device_id={"theta": target_row, "gz": target_column},
                    device_id_type=MESH_ID,
                ).start()

            return inner

        lax.fori_loop(0, 2 * THETA_COUNT, send_modes, 0)
        return carry

    lax.fori_loop(0, GZ_COUNT // 2, transform, 0)
    own_rows = pl.ds(pl.multiple_of(row * LOCAL_K, LOCAL_K), LOCAL_K)
    keep = pltpu.make_async_copy(spectrum.at[column, own_rows], modes.at[me], own_sem)
    keep.start()
    keep.wait()
    wait_bytes(modes.at[pl.ds(0, DEVICES - 1)], out_send_sem)
    wait_bytes(modes.at[pl.ds(0, DEVICES - 1)], out_recv_sem)


def step_kernel(
    velocity,
    radial_hbm,
    axial_hbm,
    cycle_hbm,
    ratio,
    modes,
    inverse,
    radial,
    flow,
    packed,
    landed,
    corners,
    tensor,
    state,
    filtered,
    row_sums,
    all_sums,
    swirl,
    drift,
    edges,
    form,
    source,
    tiles,
    planes,
    plane,
    axial,
    cycle,
    left,
    spectrum,
    load_sem,
    send_sem,
    recv_sem,
    sum_send_sem,
    sum_recv_sem,
    face_send_sem,
    face_recv_sem,
    move_sem,
):
    fetches = [
        pltpu.make_async_copy(source_ref, target, load_sem.at[n])
        for n, (source_ref, target) in enumerate(
            ((radial_hbm, radial), (axial_hbm, axial), (cycle_hbm, cycle)), 1
        )
    ]
    finish_axial, finish_rest = exchange(
        velocity, flow, packed, landed, corners, load_sem.at[0], send_sem, recv_sem, fetches
    )
    factor_rows(inverse)
    fetches[0].wait()
    finish_axial()
    strain_rows(flow, tensor, radial, True)
    finish_rest()
    strain_rows(flow, tensor, radial, False)
    numer, denom = filter_rows(flow, tensor, state, filtered, radial)

    faces = []

    def first_wait():
        face_rows(flow, tensor, swirl, drift, radial)
        faces.extend(send_faces(swirl, drift, edges, face_send_sem, face_recv_sem))

    def second_wait():
        form_rows(flow, tensor, form, radial)
        for item in faces:
            item.wait()
        join_rows(swirl, drift, edges, form, radial)

    numer, denom = sum_everywhere(
        numer,
        denom,
        row_sums,
        all_sums,
        sum_send_sem,
        sum_recv_sem,
        (first_wait, second_wait),
    )
    coefficient = (numer * (1.0 / 256.0)) / (denom * (1.0 / 256.0) + epsilon_den)
    source_rows(form, source, coefficient)
    for s in range(8):
        tiles[:, s, :] = source[s].T
    spectral_part(
        tiles,
        modes,
        planes,
        plane,
        axial,
        cycle,
        left,
        spectrum,
        fetches[1],
        fetches[2],
        *(move_sem.at[n] for n in range(5)),
        lambda: ratio_rows(tensor, ratio, radial, coefficient),
    )


def step(velocity):
    vmem = pl.BlockSpec(memory_space=pltpu.VMEM)
    hbm = pl.BlockSpec(memory_space=pltpu.HBM)
    return pl.pallas_call(
        step_kernel,
        out_shape=(
            jax.ShapeDtypeStruct((LOCAL_T, LOCAL_Z, NR), jnp.float32),
            jax.ShapeDtypeStruct((DEVICES, LOCAL_K, 128), jnp.float32),
            jax.ShapeDtypeStruct((NR, LOCAL_K, 128), jnp.float32),
        ),
        in_specs=[hbm, hbm, hbm, hbm],
        out_specs=(vmem, vmem, vmem),
        scratch_shapes=[
            pltpu.VMEM((12, 8, NR), jnp.float32),
            pltpu.VMEM((3, T_ROWS, Z_ROWS, NR), jnp.float32),
            pltpu.VMEM((2, 6, LOCAL_T, NR), jnp.float32),
            pltpu.VMEM((2, 6, LOCAL_T, NR), jnp.float32),
            pltpu.VMEM((2, 4, 3, 8, NR), jnp.float32),
            pltpu.VMEM((13, S_ROWS, S_COLS, 8, NR), jnp.float32),
            pltpu.VMEM((2, 21, Z_STEP, 8, NR), jnp.float32),
            pltpu.VMEM((21, 2 * Z_STEP, 8, NR), jnp.float32),
            pltpu.VMEM((THETA_COUNT, 8, NR), jnp.float32),
            pltpu.VMEM((GZ_COUNT, 8, NR), jnp.float32),
            pltpu.VMEM((4, LOCAL_T + 2, Z_STEP, 8, NR), jnp.float32),
            pltpu.VMEM((4, LOCAL_T + 2, Z_STEP, 8, NR), jnp.float32),
            pltpu.VMEM((2, 2, 4, LOCAL_T, NR), jnp.float32),
            pltpu.VMEM((6, LOCAL_T, Z_STEP, 8, NR), jnp.float32),
            pltpu.VMEM((8, 4 * LOCAL_T, NR), jnp.float32),
            pltpu.VMEM((NR, 8, 4 * LOCAL_T), jnp.float32),
            pltpu.VMEM((DEVICES, 8, 128), jnp.float32),
            pltpu.VMEM((NZ, NTH), jnp.float32),
            pltpu.VMEM((3, 2 * NZ, NZ), jnp.bfloat16),
            pltpu.VMEM((3, GZ_COUNT // 2, 2 * NTH, 4 * LOCAL_M), jnp.bfloat16),
            pltpu.VMEM((3, NZ, 2 * NTH), jnp.bfloat16),
            pltpu.VMEM((GZ_COUNT, NZ, 128), jnp.float32),
            pltpu.SemaphoreType.DMA((4,)),
            pltpu.SemaphoreType.DMA((8,)),
            pltpu.SemaphoreType.DMA((8,)),
            pltpu.SemaphoreType.DMA((2,)),
            pltpu.SemaphoreType.DMA((2,)),
            pltpu.SemaphoreType.DMA((4,)),
            pltpu.SemaphoreType.DMA((4,)),
            pltpu.SemaphoreType.DMA((5,)),
        ],
        compiler_params=pltpu.CompilerParams(
            collective_id=0, has_side_effects=True, vmem_limit_bytes=48 << 20
        ),
        name="step",
    )(
        *(
            pltpu.with_memory_space_constraint(jnp.asarray(value), pltpu.HBM)
            for value in (velocity, radial_table(), axial_table(), cycle_table())
        )
    )


def diagonals():
    row, column = lax.axis_index("theta"), lax.axis_index("gz")
    shape = (LOCAL_K, 128)
    theta_mode = column * LOCAL_M + lax.broadcasted_iota(jnp.int32, shape, 1) % LOCAL_M
    axial_mode = row * LOCAL_K + lax.broadcasted_iota(jnp.int32, shape, 0)
    theta_wave = jnp.minimum(theta_mode, NTH - theta_mode).astype(jnp.float32)
    axial_wave = jnp.minimum(axial_mode, NZ - axial_mode).astype(jnp.float32) * (
        2.0 * math.pi / pipe_length
    )
    theta_sq = theta_wave * theta_wave
    axial_sq = axial_wave * axial_wave * (1.0 / (NR * NR))

    def diagonal(i):
        middle = i + 0.5
        extra = float(NR) if i == NR - 1 else 0.0
        return theta_sq * (1.0 / middle) + (axial_sq * middle + (2.0 * i + 1.0 + extra))

    return diagonal


def factor_rows(inverse):
    diagonal = diagonals()
    low, high = diagonal(0), diagonal(NR - 1)
    for i in range(1, HALF):
        j = NR - 1 - i
        low_inverse, high_inverse = 1.0 / low, 1.0 / high
        inverse[i - 1] = low_inverse
        inverse[j + 1] = high_inverse
        low = diagonal(i) - low_inverse * float(i * i)
        high = diagonal(j) - high_inverse * float((j + 1) * (j + 1))
    inverse[HALF - 1] = low
    inverse[HALF] = high


def solve_kernel(modes, inverse, ratio_ref, out_ref, ratio_out, partial, pressure, ratio_sem):
    keep = pltpu.make_async_copy(ratio_ref, ratio_out, ratio_sem)
    keep.start()

    def load(i):
        return modes[i] * (-(i + 0.5) / (NR * NR))

    low, high = load(0), load(NR - 1)
    for i in range(1, HALF):
        j = NR - 1 - i
        partial[i - 1] = low
        partial[j + 1] = high
        low = load(i) + (inverse[i - 1] * float(i)) * low
        high = load(j) + (inverse[j + 1] * float(j + 1)) * high
    top, bottom = inverse[HALF - 1], inverse[HALF]
    scale = 1.0 / (top * bottom - float(HALF * HALF))
    low, high = (
        (low * bottom + float(HALF) * high) * scale,
        (high * top + float(HALF) * low) * scale,
    )
    pressure[HALF - 1] = low
    pressure[HALF] = high
    for step in range(1, HALF):
        i, j = HALF - 1 - step, HALF + step
        low = (partial[i] + float(i + 1) * low) * inverse[i]
        high = (partial[j] + float(j) * high) * inverse[j]
        pressure[i] = low
        pressure[j] = high
    for k in range(LOCAL_K):
        out_ref[:, k, :] = pressure[:, k, :].T
    keep.wait()


def solve(modes, inverse, ratio):
    vmem = pl.BlockSpec(memory_space=pltpu.VMEM)
    anywhere = pl.BlockSpec(memory_space=pl.ANY)
    pressure, ratio = pl.pallas_call(
        solve_kernel,
        out_shape=(
            jax.ShapeDtypeStruct((2 * LOCAL_M, LOCAL_K, NR), jnp.float32),
            jax.ShapeDtypeStruct((LOCAL_T, LOCAL_Z, NR), jnp.float32),
        ),
        in_specs=[vmem, vmem, anywhere],
        out_specs=(vmem, pl.BlockSpec(memory_space=pltpu.HBM)),
        scratch_shapes=[pltpu.VMEM((NR, LOCAL_K, 128), jnp.float32)] * 2 + [pltpu.SemaphoreType.DMA],
        compiler_params=pltpu.CompilerParams(vmem_limit_bytes=32 << 20),
        name="solve",
    )(modes, inverse, ratio)
    return ratio, pressure.reshape(2, LOCAL_M, LOCAL_K, NR)


def body(velocity):
    ratio, modes, inverse = step(velocity)
    return solve(modes, inverse, ratio)


def solution(mesh):
    return jax.shard_map(
        body,
        mesh=mesh,
        in_specs=(P(None, "theta", "gz", None),),
        out_specs=(P("theta", "gz", None), P(None, "gz", "theta", None)),
        check_vma=False,
    )
```

```python
import functools
import math

import jax
import jax.numpy as jnp
import ml_dtypes
import numpy as np
from jax import lax
from jax.experimental import pallas as pl
from jax.experimental.pallas import tpu as pltpu
from jax.sharding import PartitionSpec as P

NTH = 512
NZ = 256
NR = 128


pipe_length = 4.0 * math.pi
nu_molecular = 5e-05
time_step = 2.0
filter_ratio = 4.0
epsilon_den = 1e-06
pair_first = (0, 1, 2, 0, 0, 1)
pair_second = (0, 1, 2, 1, 2, 2)


THETA_COUNT = 16
GZ_COUNT = 8
DEVICES = THETA_COUNT * GZ_COUNT
LOCAL_T = NTH // THETA_COUNT
LOCAL_Z = NZ // GZ_COUNT
LOCAL_M = NTH // GZ_COUNT
LOCAL_K = NZ // THETA_COUNT
MESH_ID = pl.DeviceIdType.MESH
HALF = NR // 2


def wait_bytes(ref, sem):
    pltpu.make_async_copy(ref, ref, sem).wait()


T_ROWS = LOCAL_T + 6
Z_BASE = 8
Z_ROWS = LOCAL_Z + 2 * Z_BASE
Z_STEP = LOCAL_Z // 8
S_ROWS = LOCAL_T + 4
S_COLS = Z_STEP + 4
DT = 0.5 * NTH / (2.0 * math.pi)
DZ = 0.5 * NZ / pipe_length


def radial_table():
    radius = (np.arange(NR) + 0.5) / NR
    width = np.cbrt((1.0 / NR) * radius * (2.0 * np.pi / NTH) * (pipe_length / NZ)) ** 2
    upper = np.full(NR, 0.5 * NR)
    lower = upper.copy()
    upper[-1] = 0.0
    lower[0] = 0.0
    out, back = upper / radius, lower / radius
    outward, inward = time_step * radius * upper, time_step * radius * lower
    centre = -(out * np.roll(inward, -1) + back * np.roll(outward, 1))
    rows = np.stack(
        [
            1.0 / radius,
            DT / radius,
            upper,
            lower,
            width,
            radius,
            out,
            back,
            time_step * radius,
            2.0 * width,
            (filter_ratio / 8.0) * width,
            time_step * DT / radius,
            out * np.roll(outward, -1),
            centre,
            back * np.roll(inward, 1),
        ]
    )
    return np.broadcast_to(rows[:, None, :], (15, 8, NR)).astype(np.float32)


def along_radius(field, radial):
    return pltpu.roll(field, NR - 1, 1) * radial[2] - pltpu.roll(field, 1, 1) * radial[3]


def tensor_magnitude(t):
    diagonal = t[0] * t[0] + t[1] * t[1] + t[2] * t[2]
    mixed = t[3] * t[3] + t[4] * t[4] + t[5] * t[5]
    return jnp.sqrt(2.0 * diagonal + 4.0 * mixed)


def neighbours(row, column):
    below, above = lax.rem(row + THETA_COUNT - 1, THETA_COUNT), lax.rem(row + 1, THETA_COUNT)
    left, right = lax.rem(column + GZ_COUNT - 1, GZ_COUNT), lax.rem(column + 1, GZ_COUNT)
    return below, above, left, right


def device(row, column):
    return {"theta": row, "gz": column}


def exchange(velocity, flow, packed, landed, corners, load_sem, send_sem, recv_sem, fetches):
    row, column = lax.axis_index("theta"), lax.axis_index("gz")
    below, above, left, right = neighbours(row, column)
    barrier = pltpu.get_barrier_semaphore()

    def greet_row(i, carry):
        target = lax.rem(row + i, THETA_COUNT)
        pl.semaphore_signal(barrier, inc=1, device_id=device(target, column), device_id_type=MESH_ID)
        return carry

    def greet_column(i, carry):
        target = lax.rem(column + i, GZ_COUNT)
        pl.semaphore_signal(barrier, inc=1, device_id=device(row, target), device_id_type=MESH_ID)
        return carry

    load = pltpu.make_async_copy(
        velocity, flow.at[:, pl.ds(3, LOCAL_T), pl.ds(Z_BASE, LOCAL_Z), :], load_sem
    )
    load.start()
    fetches[0].start()
    lax.fori_loop(1, THETA_COUNT, greet_row, 0)
    lax.fori_loop(1, GZ_COUNT, greet_column, 0)
    for r in (below, above):
        for c in (left, right):
            pl.semaphore_signal(barrier, inc=1, device_id=device(r, c), device_id_type=MESH_ID)
    load.wait()
    for side, first in ((0, Z_BASE + LOCAL_Z - 2), (1, Z_BASE)):
        for comp in range(3):
            for z in range(2):
                packed[side, 2 * comp + z] = flow[comp, pl.ds(3, LOCAL_T), first + z, :]
    sublane = lax.broadcasted_iota(jnp.int32, (8, NR), 0)
    for side, near in ((0, 1), (1, 0)):
        for comp in range(3):
            for end, start, put, shift in ((0, LOCAL_T - 8, 5, 6), (1, 0, 2, 2)):
                tile = packed[side, 2 * comp + near, pl.ds(start, 8), :]
                other = packed[side, 2 * comp + 1 - near, pl.ds(start, 8), :]
                corners[0, 2 * side + end, comp] = jnp.where(
                    sublane == put, pltpu.roll(other, shift, 0), tile
                )
    pl.semaphore_wait(barrier, THETA_COUNT + GZ_COUNT + 2)

    def copy(n, source, target, r, c):
        item = pltpu.make_async_remote_copy(
            src_ref=source,
            dst_ref=target,
            send_sem=send_sem.at[n],
            recv_sem=recv_sem.at[n],
            device_id=device(r, c),
            device_id_type=MESH_ID,
        )
        item.start()
        return item

    inner = pl.ds(Z_BASE, LOCAL_Z)
    axial = [
        copy(side, packed.at[side], landed.at[side], row, target)
        for side, target in ((0, right), (1, left))
    ]
    rest = []

    def start_rest():
        low, high = pl.ds(0, 2), pl.ds(LOCAL_T - 2, 2)
        rest.append(copy(2, velocity.at[:, high], flow.at[:, pl.ds(1, 2), inner], above, column))
        rest.append(copy(3, velocity.at[:, low], flow.at[:, pl.ds(LOCAL_T + 3, 2), inner], below, column))
        for side, target in ((0, right), (1, left)):
            for end, r in ((0, above), (1, below)):
                n = 2 * side + end
                rest.append(copy(4 + n, corners.at[0, n], corners.at[1, n], r, target))
        fetches[1].start()
        fetches[2].start()

    def finish_axial():
        for item in axial:
            item.wait()
        for side, first in ((0, Z_BASE - 2), (1, Z_BASE + LOCAL_Z)):
            for comp in range(3):
                for z in range(2):
                    flow[comp, pl.ds(3, LOCAL_T), first + z, :] = landed[side, 2 * comp + z]

    def finish_rest():
        for item in rest:
            item.wait()
        for side, near, far in ((0, Z_BASE - 1, Z_BASE - 2), (1, Z_BASE + LOCAL_Z, Z_BASE + LOCAL_Z + 1)):
            for comp in range(3):
                low, high = corners.at[1, 2 * side, comp], corners.at[1, 2 * side + 1, comp]
                for t, line, z in ((1, 6, near), (2, 7, near), (2, 5, far)):
                    flow[comp, t, pl.ds(z, 1), :] = low[pl.ds(line, 1), :]
                for t, line, z in ((0, 0, near), (1, 1, near), (0, 2, far)):
                    flow[comp, LOCAL_T + 3 + t, pl.ds(z, 1), :] = high[pl.ds(line, 1), :]

    return start_rest, finish_axial, finish_rest


def read_flow(flow, comp, t, q):
    return flow[comp, t, pl.ds(Z_BASE + q, 8, stride=Z_STEP), :]


def strain_rows(flow, tensor, radial, inner, columns):
    def strain_row(step, carry):
        n = step + 3 if inner else step + 1 + (LOCAL_T - 2) * (step // 2)
        needed = {i + d for i in columns for d in (-1, 0, 1)}
        centre = [{i: read_flow(flow, c, n + 1, i - 2) for i in sorted(needed)} for c in range(3)]
        for i in columns:
            u = [centre[c][i] for c in range(3)]
            dz = [(centre[c][i + 1] - centre[c][i - 1]) * DZ for c in range(3)]
            dt = [
                (read_flow(flow, c, n + 2, i - 2) - read_flow(flow, c, n, i - 2)) * radial[1]
                for c in range(3)
            ]
            dr = [along_radius(u[c], radial) for c in range(3)]
            parts = [
                dr[0],
                dt[1] + u[0] * radial[0],
                dz[2],
                0.5 * (dr[1] - u[1] * radial[0] + dt[0]),
                0.5 * (dz[0] + dr[2]),
                0.5 * (dt[2] + dz[1]),
            ]
            size = tensor_magnitude(parts)
            scale = size * radial[9]
            tensor[6, n, i] = size
            for k in range(6):
                tensor[k, n, i] = parts[k]
                tensor[7 + k, n, i] = parts[k] * scale
        return carry

    lax.fori_loop(0, LOCAL_T - 2 if inner else 4, strain_row, 0, unroll=2)


def filter_rows(flow, tensor, state, filtered, radial):
    span = range(-1, Z_STEP + 1)

    def across(n):
        flows = [[read_flow(flow, c, n + 1, q) for q in span] for c in range(3)]
        for c in range(3):
            yield flows[c]
        for a, b in zip(pair_first, pair_second):
            yield [x * y for x, y in zip(flows[a], flows[b])]
        for k in range(6):
            yield [tensor[k, n, q + 2] for q in span]
        for k in range(6):
            yield [tensor[7 + k, n, q + 2] for q in span]

    def axial(values):
        pairs = [x + y for x, y in zip(values[:-1], values[1:])]
        return [x + y for x, y in zip(pairs[:-1], pairs[1:])]

    def first_rows():
        for f, (one, two) in enumerate(zip(across(1), across(2))):
            one, two = axial(one), axial(two)
            for q in range(Z_STEP):
                state[0, f, q] = two[q]
                state[1, f, q] = one[q] + two[q]

    def pair_rows(step, carry):
        n = 3 + 2 * step
        for f, (one, two) in enumerate(zip(across(n), across(n + 1))):
            one, two = axial(one), axial(two)
            for q in range(Z_STEP):
                before = state[0, f, q] + one[q]
                after = one[q] + two[q]
                filtered[f, q] = state[1, f, q] + before
                filtered[f, Z_STEP + q] = before + after
                state[0, f, q] = two[q]
                state[1, f, q] = after
        numer, denom = carry
        for q in range(2 * Z_STEP):
            means = [filtered[c, q] for c in range(3)]
            smooth = [filtered[9 + k, q] for k in range(6)]
            size = tensor_magnitude(smooth) * radial[10]
            lm, mm = [], []
            for k in range(6):
                leonard = filtered[3 + k, q] - means[pair_first[k]] * means[pair_second[k]] * (1.0 / 16.0)
                model = size * smooth[k] - filtered[15 + k, q]
                lm.append(leonard * model)
                mm.append(model * model)
            numer = numer + (lm[0] + lm[1] + lm[2]) + 2.0 * (lm[3] + lm[4] + lm[5])
            denom = denom + (mm[0] + mm[1] + mm[2]) + 2.0 * (mm[3] + mm[4] + mm[5])
        return numer, denom

    first_rows()
    zero = jnp.zeros((8, NR), jnp.float32)
    return lax.fori_loop(0, LOCAL_T // 2, pair_rows, (zero, zero))


def sum_everywhere(numer, denom, row_sums, all_sums, send_sem, recv_sem, meanwhile):
    row, column = lax.axis_index("theta"), lax.axis_index("gz")
    first = lax.broadcasted_iota(jnp.int32, (8, NR), 0) == 0
    tile = jnp.where(
        first, jnp.sum(numer, axis=0, keepdims=True), jnp.sum(denom, axis=0, keepdims=True)
    )

    def share(buffer, tile, place, count, target, step):
        buffer[place] = tile

        def send(i, carry):
            pltpu.make_async_remote_copy(
                src_ref=buffer.at[place],
                dst_ref=buffer.at[place],
                send_sem=send_sem.at[step],
                recv_sem=recv_sem.at[step],
                device_id=target(lax.rem(place + i, count)),
                device_id_type=MESH_ID,
            ).start()
            return carry

        lax.fori_loop(1, count, send, 0)
        meanwhile[step]()
        others = buffer.at[pl.ds(0, count - 1)]
        wait_bytes(others, recv_sem.at[step])
        wait_bytes(others, send_sem.at[step])
        total = buffer[0]
        for i in range(1, count):
            total = total + buffer[i]
        return total

    tile = share(row_sums, tile, row, THETA_COUNT, lambda i: device(i, column), 0)
    tile = share(all_sums, tile, column, GZ_COUNT, lambda i: device(row, i), 1)
    return tile[0:1], tile[1:2]


still_scale = 2.0 * nu_molecular * time_step


def face_rows(flow, tensor, swirl, drift, radial):
    def face_row(t, carry):
        n = t + 2
        for q in range(Z_STEP):
            i = q + 2

            def swirl_cross(k):
                return (
                    (tensor[k + 1, n + 1, i] - tensor[k + 1, n - 1, i]) * radial[1]
                    + (tensor[k + 5, n, i + 1] - tensor[k + 5, n, i - 1]) * DZ
                    + 2.0 * tensor[k + 3, n, i] * radial[0]
                )

            def drift_cross(k):
                return (
                    (tensor[k + 5, n + 1, i] - tensor[k + 5, n - 1, i]) * radial[1]
                    + (tensor[k + 2, n, i + 1] - tensor[k + 2, n, i - 1]) * DZ
                    + tensor[k + 4, n, i] * radial[0]
                )

            size = tensor[6, n, i] * radial[9]
            size_out, size_in = pltpu.roll(size, NR - 1, 1), pltpu.roll(size, 1, 1)
            for comp, k, cross, target in ((1, 3, swirl_cross, swirl), (2, 4, drift_cross, drift)):
                outer = pltpu.roll(tensor[k, n, i], NR - 1, 1) * radial[2]
                inner = pltpu.roll(tensor[k, n, i], 1, 1) * radial[3]
                rest = (outer - inner) + cross(0)
                target[0, t + 1, q] = read_flow(flow, comp, n + 1, q) + rest * still_scale
                target[1, t + 1, q] = cross(7)
                target[2, t + 1, q] = size_out * outer
                target[3, t + 1, q] = size_in * inner
        return carry

    lax.fori_loop(0, LOCAL_T, face_row, 0, unroll=4)


def send_faces(swirl, drift, edges, send_sem, recv_sem):
    row, column = lax.axis_index("theta"), lax.axis_index("gz")
    below, above, left, right = neighbours(row, column)
    for k in range(4):
        edges[0, 0, k] = drift[k, pl.ds(1, LOCAL_T), Z_STEP - 1, 7, :]
        edges[0, 1, k] = drift[k, pl.ds(1, LOCAL_T), 0, 0, :]
    copies = []
    for n, (source, target, r, c) in enumerate(
        (
            (swirl.at[:, LOCAL_T], swirl.at[:, 0], above, column),
            (swirl.at[:, 1], swirl.at[:, LOCAL_T + 1], below, column),
            (edges.at[0, 0], edges.at[1, 0], row, right),
            (edges.at[0, 1], edges.at[1, 1], row, left),
        )
    ):
        item = pltpu.make_async_remote_copy(
            src_ref=source,
            dst_ref=target,
            send_sem=send_sem.at[n],
            recv_sem=recv_sem.at[n],
            device_id=device(r, c),
            device_id_type=MESH_ID,
        )
        item.start()
        copies.append(item)
    return copies


def form_rows(flow, tensor, form, radial):
    def form_row(t, carry):
        n = t + 2
        for q in range(Z_STEP):
            i = q + 2

            def cross(k):
                return (
                    (tensor[k + 3, n + 1, i] - tensor[k + 3, n - 1, i]) * radial[1]
                    + (tensor[k + 4, n, i + 1] - tensor[k + 4, n, i - 1]) * DZ
                    + (tensor[k, n, i] - tensor[k + 1, n, i]) * radial[0]
                )

            still, moved = tensor[0, n, i], tensor[7, n, i]
            rest = (read_flow(flow, 0, n + 1, q) + cross(0) * still_scale) * radial[5]
            here = cross(7) * radial[8]
            twice = (
                pltpu.roll(still, NR - 2, 1) * radial[12]
                + pltpu.roll(still, 2, 1) * radial[14]
                + still * radial[13]
            )
            slope = pltpu.roll(rest, NR - 1, 1) * radial[6] - pltpu.roll(rest, 1, 1) * radial[7]
            form[0, t, q] = slope + twice * (2.0 * nu_molecular)
            form[1, t, q] = moved * radial[13]
            form[2, t, q] = pltpu.roll(here, NR - 1, 1) * radial[6]
            form[3, t, q] = pltpu.roll(here, 1, 1) * radial[7]
            form[4, t, q] = pltpu.roll(moved, NR - 2, 1) * radial[12]
            form[5, t, q] = pltpu.roll(moved, 2, 1) * radial[14]
        return carry

    lax.fori_loop(0, LOCAL_T, form_row, 0, unroll=4)


def join_rows(swirl, drift, edges, form, radial):
    sublane = lax.broadcasted_iota(jnp.int32, (8, NR), 0)

    def join_row(t, carry):
        for k in range(4):
            inside = [drift[k, t + 1, q] for q in range(Z_STEP)]
            low = jnp.broadcast_to(edges[1, 0, k, pl.ds(t, 1), :], (8, NR))
            high = jnp.broadcast_to(edges[1, 1, k, pl.ds(t, 1), :], (8, NR))
            low = jnp.where(sublane == 0, low, pltpu.roll(inside[-1], 1, 0))
            high = jnp.where(sublane == 7, high, pltpu.roll(inside[0], 7, 0))
            line = [low] + inside + [high]
            for q in range(Z_STEP):
                around = (swirl[k, t + 2, q] - swirl[k, t, q]) * radial[11 if k else 1]
                along = (line[q + 2] - line[q]) * (DZ * time_step if k else DZ)
                form[k, t, q] = form[k, t, q] + (around + along)
        return carry

    lax.fori_loop(0, LOCAL_T, join_row, 0, unroll=4)


def source_rows(form, source, coefficient):
    here = jnp.broadcast_to(coefficient, (8, NR))
    outer, inner = pltpu.roll(here, NR - 1, 1), pltpu.roll(here, 1, 1)
    outer_two, inner_two = pltpu.roll(here, NR - 2, 1), pltpu.roll(here, 2, 1)

    def source_row(t, carry):
        for q in range(Z_STEP):
            value = form[0, t, q] + here * form[1, t, q]
            value = value + (outer * form[2, t, q] - inner * form[3, t, q])
            value = value + (outer_two * form[4, t, q] + inner_two * form[5, t, q])
            source[:, q * LOCAL_T + t, :] = value
        return carry

    lax.fori_loop(0, LOCAL_T, source_row, 0, unroll=4)


def ratio_rows(tensor, ratio, radial, coefficient):
    scale = coefficient * (radial[4][0:1] * (1.0 / nu_molecular))
    scale = jnp.broadcast_to(scale, (8, NR))

    def ratio_row(t, carry):
        for q in range(Z_STEP):
            ratio[t, pl.ds(q, 8, stride=Z_STEP), :] = scale * tensor[6, t + 2, q + 2]
        return carry

    lax.fori_loop(0, LOCAL_T, ratio_row, 0, unroll=4)


def split_table(table):
    parts, rest = [], table
    for _ in range(3):
        part = rest.astype(np.float32).astype(ml_dtypes.bfloat16)
        parts.append(part)
        rest = rest - part.astype(np.float64)
    return np.stack(parts)


def axial_table():
    order = np.arange(NZ)
    block, rest = order // LOCAL_Z, order % LOCAL_Z
    cells = block * LOCAL_Z + 4 * (rest % 8) + rest // 8
    angle = 2.0 * np.pi * ((np.arange(NZ)[:, None] * cells[None, :]) % NZ) / NZ
    return split_table(np.concatenate([np.cos(angle), np.sin(angle)], axis=0))


def cycle_table():
    angle = 2.0 * np.pi * ((np.arange(NTH)[:, None] * np.arange(NTH)[None, :]) % NTH) / NTH
    scale = 1.0 / math.sqrt(NTH * NZ)
    cosine = (np.cos(angle) * scale).reshape(NTH, GZ_COUNT, LOCAL_M)
    sine = (np.sin(angle) * scale).reshape(NTH, GZ_COUNT, LOCAL_M)
    upper = np.stack([cosine, -sine], axis=2)
    lower = np.stack([-sine, -cosine], axis=2)
    both = np.concatenate([upper, lower], axis=0)[:, [0, 2, 1, 3, 4, 6, 5, 7]]
    both = both.reshape(2 * NTH, GZ_COUNT // 2, 4 * LOCAL_M)
    return split_table(np.moveaxis(both, 1, 0))


def split_value(value):
    parts = []
    for _ in range(3):
        part = value.astype(jnp.bfloat16)
        parts.append(part)
        value = value - part.astype(jnp.float32)
    return parts


def product(left, right):
    total = None
    for i, j in ((0, 2), (2, 0), (1, 1), (0, 1), (1, 0), (0, 0)):
        term = jnp.dot(left[i], right[j], preferred_element_type=jnp.float32)
        total = term if total is None else total + term
    return total


def spectral_part(
    tiles,
    modes,
    planes,
    plane,
    axial,
    cycle,
    left,
    spectrum,
    fetch_axial,
    fetch_cycle,
    send_sem,
    recv_sem,
    out_send_sem,
    out_recv_sem,
    own_sem,
    meanwhile,
):
    row, column = lax.axis_index("theta"), lax.axis_index("gz")
    me = row * GZ_COUNT + column

    def send_tile(i, carry):
        target = lax.rem(me + i, DEVICES)
        pltpu.make_async_remote_copy(
            src_ref=tiles.at[target],
            dst_ref=planes.at[me],
            send_sem=send_sem,
            recv_sem=recv_sem,
            device_id={"theta": target // GZ_COUNT, "gz": lax.rem(target, GZ_COUNT)},
            device_id_type=MESH_ID,
        ).start()
        return carry

    lax.fori_loop(1, DEVICES, send_tile, 0)
    planes[me] = tiles[me]
    meanwhile()
    wait_bytes(planes.at[pl.ds(0, DEVICES - 1)], recv_sem)
    wait_bytes(planes.at[pl.ds(0, DEVICES - 1)], send_sem)

    group = lax.broadcasted_iota(jnp.int32, (8, 128), 1) // LOCAL_T

    def gather_lines(c, carry):
        for quad in range(THETA_COUNT // 4):
            parts = [planes[(4 * quad + b) * GZ_COUNT + c] for b in range(4)]
            for z in range(4):
                turned = [
                    parts[b] if b == z else pltpu.roll(parts[b], ((b - z) * LOCAL_T) % 128, 1)
                    for b in range(4)
                ]
                value = jnp.where(
                    group < 2,
                    jnp.where(group == 0, turned[0], turned[1]),
                    jnp.where(group == 2, turned[2], turned[3]),
                )
                start = pl.multiple_of(c * LOCAL_Z + 8 * z, 8)
                plane[pl.ds(start, 8), 128 * quad : 128 * quad + 128] = value
        return carry

    lax.fori_loop(0, GZ_COUNT, gather_lines, 0)
    fetch_axial.wait()
    lines = product(axial, split_value(plane[...]))
    for n, part in enumerate(split_value(lines)):
        left[n, :, :NTH] = part[:NZ]
        left[n, :, NTH:] = part[NZ:]
    fetch_cycle.wait()

    def transform(step, carry):
        chunk = lax.rem(2 * (column // 4) + lax.rem(column, 2) + step, GZ_COUNT // 2)
        first = 4 * (chunk // 2) + lax.rem(chunk, 2)
        both = product(left, cycle.at[:, chunk])
        spectrum[first] = both[:, :128]
        spectrum[first + 2] = both[:, 128:]

        def send_modes(i, inner):
            target_column = first + 2 * lax.rem(i, 2)
            target_row = lax.rem(row + i // 2, THETA_COUNT)
            rows = pl.ds(pl.multiple_of(target_row * LOCAL_K, LOCAL_K), LOCAL_K)

            @pl.when(jnp.logical_or(target_row != row, target_column != column))
            def _():
                pltpu.make_async_remote_copy(
                    src_ref=spectrum.at[target_column, rows],
                    dst_ref=modes.at[me],
                    send_sem=out_send_sem,
                    recv_sem=out_recv_sem,
                    device_id={"theta": target_row, "gz": target_column},
                    device_id_type=MESH_ID,
                ).start()

            return inner

        lax.fori_loop(0, 2 * THETA_COUNT, send_modes, 0)
        return carry

    lax.fori_loop(0, GZ_COUNT // 2, transform, 0)
    own_rows = pl.ds(pl.multiple_of(row * LOCAL_K, LOCAL_K), LOCAL_K)
    keep = pltpu.make_async_copy(spectrum.at[column, own_rows], modes.at[me], own_sem)
    keep.start()
    keep.wait()
    wait_bytes(modes.at[pl.ds(0, DEVICES - 1)], out_send_sem)
    wait_bytes(modes.at[pl.ds(0, DEVICES - 1)], out_recv_sem)


def step_kernel(
    velocity,
    radial_hbm,
    axial_hbm,
    cycle_hbm,
    ratio,
    modes,
    inverse,
    radial,
    flow,
    packed,
    landed,
    corners,
    tensor,
    state,
    filtered,
    row_sums,
    all_sums,
    swirl,
    drift,
    edges,
    form,
    source,
    tiles,
    planes,
    plane,
    axial,
    cycle,
    left,
    spectrum,
    load_sem,
    send_sem,
    recv_sem,
    sum_send_sem,
    sum_recv_sem,
    face_send_sem,
    face_recv_sem,
    move_sem,
):
    fetches = [
        pltpu.make_async_copy(source_ref, target, load_sem.at[n])
        for n, (source_ref, target) in enumerate(
            ((radial_hbm, radial), (axial_hbm, axial), (cycle_hbm, cycle)), 1
        )
    ]
    start_rest, finish_axial, finish_rest = exchange(
        velocity, flow, packed, landed, corners, load_sem.at[0], send_sem, recv_sem, fetches
    )
    start_rest()
    factor_rows(inverse)
    fetches[0].wait()
    strain_rows(flow, tensor, radial, True, (3, 4))
    finish_axial()
    strain_rows(flow, tensor, radial, True, (1, 2, 5, 6))
    finish_rest()
    strain_rows(flow, tensor, radial, False, range(1, S_COLS - 1))
    numer, denom = filter_rows(flow, tensor, state, filtered, radial)

    faces = []

    def first_wait():
        face_rows(flow, tensor, swirl, drift, radial)
        faces.extend(send_faces(swirl, drift, edges, face_send_sem, face_recv_sem))

    def second_wait():
        form_rows(flow, tensor, form, radial)
        for item in faces:
            item.wait()
        join_rows(swirl, drift, edges, form, radial)

    numer, denom = sum_everywhere(
        numer,
        denom,
        row_sums,
        all_sums,
        sum_send_sem,
        sum_recv_sem,
        (first_wait, second_wait),
    )
    coefficient = (numer * (1.0 / 256.0)) / (denom * (1.0 / 256.0) + epsilon_den)
    source_rows(form, source, coefficient)
    for s in range(8):
        tiles[:, s, :] = source[s].T
    spectral_part(
        tiles,
        modes,
        planes,
        plane,
        axial,
        cycle,
        left,
        spectrum,
        fetches[1],
        fetches[2],
        *(move_sem.at[n] for n in range(5)),
        lambda: ratio_rows(tensor, ratio, radial, coefficient),
    )


def step(velocity):
    vmem = pl.BlockSpec(memory_space=pltpu.VMEM)
    hbm = pl.BlockSpec(memory_space=pltpu.HBM)
    return pl.pallas_call(
        step_kernel,
        out_shape=(
            jax.ShapeDtypeStruct((LOCAL_T, LOCAL_Z, NR), jnp.float32),
            jax.ShapeDtypeStruct((DEVICES, LOCAL_K, 128), jnp.float32),
            jax.ShapeDtypeStruct((NR, LOCAL_K, 128), jnp.float32),
        ),
        in_specs=[hbm, hbm, hbm, hbm],
        out_specs=(vmem, vmem, vmem),
        scratch_shapes=[
            pltpu.VMEM((15, 8, NR), jnp.float32),
            pltpu.VMEM((3, T_ROWS, Z_ROWS, NR), jnp.float32),
            pltpu.VMEM((2, 6, LOCAL_T, NR), jnp.float32),
            pltpu.VMEM((2, 6, LOCAL_T, NR), jnp.float32),
            pltpu.VMEM((2, 4, 3, 8, NR), jnp.float32),
            pltpu.VMEM((13, S_ROWS, S_COLS, 8, NR), jnp.float32),
            pltpu.VMEM((2, 21, Z_STEP, 8, NR), jnp.float32),
            pltpu.VMEM((21, 2 * Z_STEP, 8, NR), jnp.float32),
            pltpu.VMEM((THETA_COUNT, 8, NR), jnp.float32),
            pltpu.VMEM((GZ_COUNT, 8, NR), jnp.float32),
            pltpu.VMEM((4, LOCAL_T + 2, Z_STEP, 8, NR), jnp.float32),
            pltpu.VMEM((4, LOCAL_T + 2, Z_STEP, 8, NR), jnp.float32),
            pltpu.VMEM((2, 2, 4, LOCAL_T, NR), jnp.float32),
            pltpu.VMEM((6, LOCAL_T, Z_STEP, 8, NR), jnp.float32),
            pltpu.VMEM((8, 4 * LOCAL_T, NR), jnp.float32),
            pltpu.VMEM((NR, 8, 4 * LOCAL_T), jnp.float32),
            pltpu.VMEM((DEVICES, 8, 128), jnp.float32),
            pltpu.VMEM((NZ, NTH), jnp.float32),
            pltpu.VMEM((3, 2 * NZ, NZ), jnp.bfloat16),
            pltpu.VMEM((3, GZ_COUNT // 2, 2 * NTH, 4 * LOCAL_M), jnp.bfloat16),
            pltpu.VMEM((3, NZ, 2 * NTH), jnp.bfloat16),
            pltpu.VMEM((GZ_COUNT, NZ, 128), jnp.float32),
            pltpu.SemaphoreType.DMA((4,)),
            pltpu.SemaphoreType.DMA((8,)),
            pltpu.SemaphoreType.DMA((8,)),
            pltpu.SemaphoreType.DMA((2,)),
            pltpu.SemaphoreType.DMA((2,)),
            pltpu.SemaphoreType.DMA((4,)),
            pltpu.SemaphoreType.DMA((4,)),
            pltpu.SemaphoreType.DMA((5,)),
        ],
        compiler_params=pltpu.CompilerParams(
            collective_id=0, has_side_effects=True, vmem_limit_bytes=48 << 20
        ),
        name="step",
    )(
        *(
            pltpu.with_memory_space_constraint(jnp.asarray(value), pltpu.HBM)
            for value in (velocity, radial_table(), axial_table(), cycle_table())
        )
    )


def diagonals():
    row, column = lax.axis_index("theta"), lax.axis_index("gz")
    shape = (LOCAL_K, 128)
    theta_mode = column * LOCAL_M + lax.broadcasted_iota(jnp.int32, shape, 1) % LOCAL_M
    axial_mode = row * LOCAL_K + lax.broadcasted_iota(jnp.int32, shape, 0)
    theta_wave = jnp.minimum(theta_mode, NTH - theta_mode).astype(jnp.float32)
    axial_wave = jnp.minimum(axial_mode, NZ - axial_mode).astype(jnp.float32) * (
        2.0 * math.pi / pipe_length
    )
    theta_sq = theta_wave * theta_wave
    axial_sq = axial_wave * axial_wave * (1.0 / (NR * NR))

    def diagonal(i):
        middle = i + 0.5
        extra = float(NR) if i == NR - 1 else 0.0
        return theta_sq * (1.0 / middle) + (axial_sq * middle + (2.0 * i + 1.0 + extra))

    return diagonal


def factor_rows(inverse):
    diagonal = diagonals()
    low, high = diagonal(0), diagonal(NR - 1)
    for i in range(1, HALF):
        j = NR - 1 - i
        low_inverse, high_inverse = 1.0 / low, 1.0 / high
        inverse[i - 1] = low_inverse
        inverse[j + 1] = high_inverse
        low = diagonal(i) - low_inverse * float(i * i)
        high = diagonal(j) - high_inverse * float((j + 1) * (j + 1))
    inverse[HALF - 1] = low
    inverse[HALF] = high


def solve_kernel(modes, inverse, ratio_ref, out_ref, ratio_out, partial, pressure, ratio_sem):
    keep = pltpu.make_async_copy(ratio_ref, ratio_out, ratio_sem)
    keep.start()

    def load(i):
        return modes[i] * (-(i + 0.5) / (NR * NR))

    low, high = load(0), load(NR - 1)
    for i in range(1, HALF):
        j = NR - 1 - i
        partial[i - 1] = low
        partial[j + 1] = high
        low = load(i) + (inverse[i - 1] * float(i)) * low
        high = load(j) + (inverse[j + 1] * float(j + 1)) * high
    top, bottom = inverse[HALF - 1], inverse[HALF]
    scale = 1.0 / (top * bottom - float(HALF * HALF))
    low, high = (
        (low * bottom + float(HALF) * high) * scale,
        (high * top + float(HALF) * low) * scale,
    )
    pressure[HALF - 1] = low
    pressure[HALF] = high
    for step in range(1, HALF):
        i, j = HALF - 1 - step, HALF + step
        low = (partial[i] + float(i + 1) * low) * inverse[i]
        high = (partial[j] + float(j) * high) * inverse[j]
        pressure[i] = low
        pressure[j] = high
    for k in range(LOCAL_K):
        out_ref[:, k, :] = pressure[:, k, :].T
    keep.wait()


def solve(modes, inverse, ratio):
    vmem = pl.BlockSpec(memory_space=pltpu.VMEM)
    anywhere = pl.BlockSpec(memory_space=pl.ANY)
    pressure, ratio = pl.pallas_call(
        solve_kernel,
        out_shape=(
            jax.ShapeDtypeStruct((2 * LOCAL_M, LOCAL_K, NR), jnp.float32),
            jax.ShapeDtypeStruct((LOCAL_T, LOCAL_Z, NR), jnp.float32),
        ),
        in_specs=[vmem, vmem, anywhere],
        out_specs=(vmem, pl.BlockSpec(memory_space=pltpu.HBM)),
        scratch_shapes=[pltpu.VMEM((NR, LOCAL_K, 128), jnp.float32)] * 2 + [pltpu.SemaphoreType.DMA],
        compiler_params=pltpu.CompilerParams(vmem_limit_bytes=32 << 20),
        name="solve",
    )(modes, inverse, ratio)
    return ratio, pressure.reshape(2, LOCAL_M, LOCAL_K, NR)


def body(velocity):
    ratio, modes, inverse = step(velocity)
    return solve(modes, inverse, ratio)


def solution(mesh):
    return jax.shard_map(
        body,
        mesh=mesh,
        in_specs=(P(None, "theta", "gz", None),),
        out_specs=(P("theta", "gz", None), P(None, "gz", "theta", None)),
        check_vma=False,
    )
```

```python
import functools
import math

import jax
import jax.numpy as jnp
import ml_dtypes
import numpy as np
from jax import lax
from jax.experimental import pallas as pl
from jax.experimental.pallas import tpu as pltpu
from jax.sharding import PartitionSpec as P

NTH = 512
NZ = 256
NR = 128


pipe_length = 4.0 * math.pi
nu_molecular = 5e-05
time_step = 2.0
filter_ratio = 4.0
epsilon_den = 1e-06
pair_first = (0, 1, 2, 0, 0, 1)
pair_second = (0, 1, 2, 1, 2, 2)


THETA_COUNT = 16
GZ_COUNT = 8
DEVICES = THETA_COUNT * GZ_COUNT
LOCAL_T = NTH // THETA_COUNT
LOCAL_Z = NZ // GZ_COUNT
LOCAL_M = NTH // GZ_COUNT
LOCAL_K = NZ // THETA_COUNT
MESH_ID = pl.DeviceIdType.MESH
HALF = NR // 2


def wait_bytes(ref, sem):
    pltpu.make_async_copy(ref, ref, sem).wait()


T_ROWS = LOCAL_T + 6
Z_BASE = 8
Z_ROWS = LOCAL_Z + 2 * Z_BASE
Z_STEP = LOCAL_Z // 8
S_ROWS = LOCAL_T + 4
S_COLS = Z_STEP + 4
DT = 0.5 * NTH / (2.0 * math.pi)
DZ = 0.5 * NZ / pipe_length


def radial_table():
    radius = (np.arange(NR) + 0.5) / NR
    width = np.cbrt((1.0 / NR) * radius * (2.0 * np.pi / NTH) * (pipe_length / NZ)) ** 2
    upper = np.full(NR, 0.5 * NR)
    lower = upper.copy()
    upper[-1] = 0.0
    lower[0] = 0.0
    out, back = upper / radius, lower / radius
    outward, inward = time_step * radius * upper, time_step * radius * lower
    centre = -(out * np.roll(inward, -1) + back * np.roll(outward, 1))
    rows = np.stack(
        [
            1.0 / radius,
            DT / radius,
            upper,
            lower,
            width,
            radius,
            out,
            back,
            time_step * radius,
            2.0 * width,
            (filter_ratio / 8.0) * width,
            time_step * DT / radius,
            out * np.roll(outward, -1),
            centre,
            back * np.roll(inward, 1),
        ]
    )
    return np.broadcast_to(rows[:, None, :], (15, 8, NR)).astype(np.float32)


def along_radius(field, radial):
    return pltpu.roll(field, NR - 1, 1) * radial[2] - pltpu.roll(field, 1, 1) * radial[3]


def tensor_magnitude(t):
    diagonal = t[0] * t[0] + t[1] * t[1] + t[2] * t[2]
    mixed = t[3] * t[3] + t[4] * t[4] + t[5] * t[5]
    return jnp.sqrt(2.0 * diagonal + 4.0 * mixed)


def neighbours(row, column):
    below, above = lax.rem(row + THETA_COUNT - 1, THETA_COUNT), lax.rem(row + 1, THETA_COUNT)
    left, right = lax.rem(column + GZ_COUNT - 1, GZ_COUNT), lax.rem(column + 1, GZ_COUNT)
    return below, above, left, right


def device(row, column):
    return {"theta": row, "gz": column}


def exchange(velocity, flow, packed, landed, corners, load_sem, send_sem, recv_sem, fetches):
    row, column = lax.axis_index("theta"), lax.axis_index("gz")
    below, above, left, right = neighbours(row, column)
    barrier = pltpu.get_barrier_semaphore()

    def greet_row(i, carry):
        target = lax.rem(row + i, THETA_COUNT)
        pl.semaphore_signal(barrier, inc=1, device_id=device(target, column), device_id_type=MESH_ID)
        return carry

    def greet_column(i, carry):
        target = lax.rem(column + i, GZ_COUNT)
        pl.semaphore_signal(barrier, inc=1, device_id=device(row, target), device_id_type=MESH_ID)
        return carry

    load = pltpu.make_async_copy(
        velocity, flow.at[:, pl.ds(3, LOCAL_T), pl.ds(Z_BASE, LOCAL_Z), :], load_sem
    )
    load.start()
    fetches[0].start()
    lax.fori_loop(1, THETA_COUNT, greet_row, 0)
    lax.fori_loop(1, GZ_COUNT, greet_column, 0)
    for r in (below, above):
        for c in (left, right):
            pl.semaphore_signal(barrier, inc=1, device_id=device(r, c), device_id_type=MESH_ID)
    load.wait()
    for side, first in ((0, Z_BASE + LOCAL_Z - 2), (1, Z_BASE)):
        for comp in range(3):
            for z in range(2):
                packed[side, 2 * comp + z] = flow[comp, pl.ds(3, LOCAL_T), first + z, :]
    sublane = lax.broadcasted_iota(jnp.int32, (8, NR), 0)
    for side, near in ((0, 1), (1, 0)):
        for comp in range(3):
            for end, start, put, shift in ((0, LOCAL_T - 8, 5, 6), (1, 0, 2, 2)):
                tile = packed[side, 2 * comp + near, pl.ds(start, 8), :]
                other = packed[side, 2 * comp + 1 - near, pl.ds(start, 8), :]
                corners[0, 2 * side + end, comp] = jnp.where(
                    sublane == put, pltpu.roll(other, shift, 0), tile
                )
    pl.semaphore_wait(barrier, THETA_COUNT + GZ_COUNT + 2)

    def copy(n, source, target, r, c):
        item = pltpu.make_async_remote_copy(
            src_ref=source,
            dst_ref=target,
            send_sem=send_sem.at[n],
            recv_sem=recv_sem.at[n],
            device_id=device(r, c),
            device_id_type=MESH_ID,
        )
        item.start()
        return item

    inner = pl.ds(Z_BASE, LOCAL_Z)
    axial = [
        copy(side, packed.at[side], landed.at[side], row, target)
        for side, target in ((0, right), (1, left))
    ]
    rest = []

    def start_rest():
        low, high = pl.ds(0, 2), pl.ds(LOCAL_T - 2, 2)
        rest.append(copy(2, velocity.at[:, high], flow.at[:, pl.ds(1, 2), inner], above, column))
        rest.append(copy(3, velocity.at[:, low], flow.at[:, pl.ds(LOCAL_T + 3, 2), inner], below, column))
        for side, target in ((0, right), (1, left)):
            for end, r in ((0, above), (1, below)):
                n = 2 * side + end
                rest.append(copy(4 + n, corners.at[0, n], corners.at[1, n], r, target))
        fetches[1].start()
        fetches[2].start()

    def finish_axial():
        for item in axial:
            item.wait()
        for side, first in ((0, Z_BASE - 2), (1, Z_BASE + LOCAL_Z)):
            for comp in range(3):
                for z in range(2):
                    flow[comp, pl.ds(3, LOCAL_T), first + z, :] = landed[side, 2 * comp + z]

    def finish_rest():
        for item in rest:
            item.wait()
        for side, near, far in ((0, Z_BASE - 1, Z_BASE - 2), (1, Z_BASE + LOCAL_Z, Z_BASE + LOCAL_Z + 1)):
            for comp in range(3):
                low, high = corners.at[1, 2 * side, comp], corners.at[1, 2 * side + 1, comp]
                for t, line, z in ((1, 6, near), (2, 7, near), (2, 5, far)):
                    flow[comp, t, pl.ds(z, 1), :] = low[pl.ds(line, 1), :]
                for t, line, z in ((0, 0, near), (1, 1, near), (0, 2, far)):
                    flow[comp, LOCAL_T + 3 + t, pl.ds(z, 1), :] = high[pl.ds(line, 1), :]

    return start_rest, finish_axial, finish_rest


def read_flow(flow, comp, t, q):
    return flow[comp, t, pl.ds(Z_BASE + q, 8, stride=Z_STEP), :]


def strain_rows(flow, tensor, radial, inner, columns):
    def strain_row(step, carry):
        n = step + 3 if inner else step + 1 + (LOCAL_T - 2) * (step // 2)
        needed = {i + d for i in columns for d in (-1, 0, 1)}
        centre = [{i: read_flow(flow, c, n + 1, i - 2) for i in sorted(needed)} for c in range(3)]
        for i in columns:
            u = [centre[c][i] for c in range(3)]
            dz = [(centre[c][i + 1] - centre[c][i - 1]) * DZ for c in range(3)]
            dt = [
                (read_flow(flow, c, n + 2, i - 2) - read_flow(flow, c, n, i - 2)) * radial[1]
                for c in range(3)
            ]
            dr = [along_radius(u[c], radial) for c in range(3)]
            parts = [
                dr[0],
                dt[1] + u[0] * radial[0],
                dz[2],
                0.5 * (dr[1] - u[1] * radial[0] + dt[0]),
                0.5 * (dz[0] + dr[2]),
                0.5 * (dt[2] + dz[1]),
            ]
            size = tensor_magnitude(parts)
            scale = size * radial[9]
            tensor[6, n, i] = size
            for k in range(6):
                tensor[k, n, i] = parts[k]
                tensor[7 + k, n, i] = parts[k] * scale
        return carry

    lax.fori_loop(0, LOCAL_T - 2 if inner else 4, strain_row, 0, unroll=2)


def filter_rows(flow, tensor, state, filtered, radial):
    span = range(-1, Z_STEP + 1)

    def across(n):
        flows = [[read_flow(flow, c, n + 1, q) for q in span] for c in range(3)]
        for c in range(3):
            yield flows[c]
        for a, b in zip(pair_first, pair_second):
            yield [x * y for x, y in zip(flows[a], flows[b])]
        for k in range(6):
            yield [tensor[k, n, q + 2] for q in span]
        for k in range(6):
            yield [tensor[7 + k, n, q + 2] for q in span]

    def axial(values):
        pairs = [x + y for x, y in zip(values[:-1], values[1:])]
        return [x + y for x, y in zip(pairs[:-1], pairs[1:])]

    def first_rows():
        for f, (one, two) in enumerate(zip(across(1), across(2))):
            one, two = axial(one), axial(two)
            for q in range(Z_STEP):
                state[0, f, q] = two[q]
                state[1, f, q] = one[q] + two[q]

    def pair_rows(step, carry):
        n = 3 + 2 * step
        for f, (one, two) in enumerate(zip(across(n), across(n + 1))):
            one, two = axial(one), axial(two)
            for q in range(Z_STEP):
                before = state[0, f, q] + one[q]
                after = one[q] + two[q]
                filtered[f, q] = state[1, f, q] + before
                filtered[f, Z_STEP + q] = before + after
                state[0, f, q] = two[q]
                state[1, f, q] = after
        numer, denom = carry
        for q in range(2 * Z_STEP):
            means = [filtered[c, q] for c in range(3)]
            smooth = [filtered[9 + k, q] for k in range(6)]
            size = tensor_magnitude(smooth) * radial[10]
            lm, mm = [], []
            for k in range(6):
                leonard = filtered[3 + k, q] - means[pair_first[k]] * means[pair_second[k]] * (1.0 / 16.0)
                model = size * smooth[k] - filtered[15 + k, q]
                lm.append(leonard * model)
                mm.append(model * model)
            numer = numer + (lm[0] + lm[1] + lm[2]) + 2.0 * (lm[3] + lm[4] + lm[5])
            denom = denom + (mm[0] + mm[1] + mm[2]) + 2.0 * (mm[3] + mm[4] + mm[5])
        return numer, denom

    first_rows()
    zero = jnp.zeros((8, NR), jnp.float32)
    return lax.fori_loop(0, LOCAL_T // 2, pair_rows, (zero, zero))


def sum_everywhere(numer, denom, row_sums, all_sums, send_sem, recv_sem, meanwhile):
    row, column = lax.axis_index("theta"), lax.axis_index("gz")
    first = lax.broadcasted_iota(jnp.int32, (8, NR), 0) == 0
    tile = jnp.where(
        first, jnp.sum(numer, axis=0, keepdims=True), jnp.sum(denom, axis=0, keepdims=True)
    )

    def share(buffer, tile, place, count, target, step):
        buffer[place] = tile

        def send(i, carry):
            pltpu.make_async_remote_copy(
                src_ref=buffer.at[place],
                dst_ref=buffer.at[place],
                send_sem=send_sem.at[step],
                recv_sem=recv_sem.at[step],
                device_id=target(lax.rem(place + i, count)),
                device_id_type=MESH_ID,
            ).start()
            return carry

        lax.fori_loop(1, count, send, 0)
        meanwhile[step]()
        others = buffer.at[pl.ds(0, count - 1)]
        wait_bytes(others, recv_sem.at[step])
        wait_bytes(others, send_sem.at[step])
        total = buffer[0]
        for i in range(1, count):
            total = total + buffer[i]
        return total

    tile = share(row_sums, tile, row, THETA_COUNT, lambda i: device(i, column), 0)
    tile = share(all_sums, tile, column, GZ_COUNT, lambda i: device(row, i), 1)
    return tile[0:1], tile[1:2]


still_scale = 2.0 * nu_molecular * time_step


def face_rows(flow, tensor, swirl, drift, radial):
    def face_row(t, carry):
        n = t + 2
        for q in range(Z_STEP):
            i = q + 2

            def swirl_cross(k):
                return (
                    (tensor[k + 1, n + 1, i] - tensor[k + 1, n - 1, i]) * radial[1]
                    + (tensor[k + 5, n, i + 1] - tensor[k + 5, n, i - 1]) * DZ
                    + 2.0 * tensor[k + 3, n, i] * radial[0]
                )

            def drift_cross(k):
                return (
                    (tensor[k + 5, n + 1, i] - tensor[k + 5, n - 1, i]) * radial[1]
                    + (tensor[k + 2, n, i + 1] - tensor[k + 2, n, i - 1]) * DZ
                    + tensor[k + 4, n, i] * radial[0]
                )

            size = tensor[6, n, i] * radial[9]
            size_out, size_in = pltpu.roll(size, NR - 1, 1), pltpu.roll(size, 1, 1)
            for comp, k, cross, target in ((1, 3, swirl_cross, swirl), (2, 4, drift_cross, drift)):
                outer = pltpu.roll(tensor[k, n, i], NR - 1, 1) * radial[2]
                inner = pltpu.roll(tensor[k, n, i], 1, 1) * radial[3]
                rest = (outer - inner) + cross(0)
                target[0, t + 1, q] = read_flow(flow, comp, n + 1, q) + rest * still_scale
                target[1, t + 1, q] = cross(7)
                target[2, t + 1, q] = size_out * outer
                target[3, t + 1, q] = size_in * inner
        return carry

    lax.fori_loop(0, LOCAL_T, face_row, 0, unroll=4)


def send_faces(swirl, drift, edges, send_sem, recv_sem):
    row, column = lax.axis_index("theta"), lax.axis_index("gz")
    below, above, left, right = neighbours(row, column)
    for k in range(4):
        edges[0, 0, k] = drift[k, pl.ds(1, LOCAL_T), Z_STEP - 1, 7, :]
        edges[0, 1, k] = drift[k, pl.ds(1, LOCAL_T), 0, 0, :]
    copies = []
    for n, (source, target, r, c) in enumerate(
        (
            (swirl.at[:, LOCAL_T], swirl.at[:, 0], above, column),
            (swirl.at[:, 1], swirl.at[:, LOCAL_T + 1], below, column),
            (edges.at[0, 0], edges.at[1, 0], row, right),
            (edges.at[0, 1], edges.at[1, 1], row, left),
        )
    ):
        item = pltpu.make_async_remote_copy(
            src_ref=source,
            dst_ref=target,
            send_sem=send_sem.at[n],
            recv_sem=recv_sem.at[n],
            device_id=device(r, c),
            device_id_type=MESH_ID,
        )
        item.start()
        copies.append(item)
    return copies


def form_rows(flow, tensor, form, radial):
    def form_row(t, carry):
        n = t + 2
        for q in range(Z_STEP):
            i = q + 2

            def cross(k):
                return (
                    (tensor[k + 3, n + 1, i] - tensor[k + 3, n - 1, i]) * radial[1]
                    + (tensor[k + 4, n, i + 1] - tensor[k + 4, n, i - 1]) * DZ
                    + (tensor[k, n, i] - tensor[k + 1, n, i]) * radial[0]
                )

            still, moved = tensor[0, n, i], tensor[7, n, i]
            rest = (read_flow(flow, 0, n + 1, q) + cross(0) * still_scale) * radial[5]
            here = cross(7) * radial[8]
            twice = (
                pltpu.roll(still, NR - 2, 1) * radial[12]
                + pltpu.roll(still, 2, 1) * radial[14]
                + still * radial[13]
            )
            slope = pltpu.roll(rest, NR - 1, 1) * radial[6] - pltpu.roll(rest, 1, 1) * radial[7]
            form[0, t, q] = slope + twice * (2.0 * nu_molecular)
            form[1, t, q] = moved * radial[13]
            form[2, t, q] = pltpu.roll(here, NR - 1, 1) * radial[6]
            form[3, t, q] = pltpu.roll(here, 1, 1) * radial[7]
            form[4, t, q] = pltpu.roll(moved, NR - 2, 1) * radial[12]
            form[5, t, q] = pltpu.roll(moved, 2, 1) * radial[14]
        return carry

    lax.fori_loop(0, LOCAL_T, form_row, 0, unroll=4)


def join_rows(swirl, drift, edges, form, radial):
    sublane = lax.broadcasted_iota(jnp.int32, (8, NR), 0)

    def join_row(t, carry):
        for k in range(4):
            inside = [drift[k, t + 1, q] for q in range(Z_STEP)]
            low = jnp.broadcast_to(edges[1, 0, k, pl.ds(t, 1), :], (8, NR))
            high = jnp.broadcast_to(edges[1, 1, k, pl.ds(t, 1), :], (8, NR))
            low = jnp.where(sublane == 0, low, pltpu.roll(inside[-1], 1, 0))
            high = jnp.where(sublane == 7, high, pltpu.roll(inside[0], 7, 0))
            line = [low] + inside + [high]
            for q in range(Z_STEP):
                around = (swirl[k, t + 2, q] - swirl[k, t, q]) * radial[11 if k else 1]
                along = (line[q + 2] - line[q]) * (DZ * time_step if k else DZ)
                form[k, t, q] = form[k, t, q] + (around + along)
        return carry

    lax.fori_loop(0, LOCAL_T, join_row, 0, unroll=4)


def source_rows(form, source, coefficient):
    here = jnp.broadcast_to(coefficient, (8, NR))
    outer, inner = pltpu.roll(here, NR - 1, 1), pltpu.roll(here, 1, 1)
    outer_two, inner_two = pltpu.roll(here, NR - 2, 1), pltpu.roll(here, 2, 1)

    def source_row(t, carry):
        for q in range(Z_STEP):
            value = form[0, t, q] + here * form[1, t, q]
            value = value + (outer * form[2, t, q] - inner * form[3, t, q])
            value = value + (outer_two * form[4, t, q] + inner_two * form[5, t, q])
            source[:, q * LOCAL_T + t, :] = value
        return carry

    lax.fori_loop(0, LOCAL_T, source_row, 0, unroll=4)


def ratio_rows(tensor, ratio, radial, coefficient):
    scale = coefficient * (radial[4][0:1] * (1.0 / nu_molecular))
    scale = jnp.broadcast_to(scale, (8, NR))

    def ratio_row(t, carry):
        for q in range(Z_STEP):
            ratio[t, pl.ds(q, 8, stride=Z_STEP), :] = scale * tensor[6, t + 2, q + 2]
        return carry

    lax.fori_loop(0, LOCAL_T, ratio_row, 0, unroll=4)


def split_table(table):
    parts, rest = [], table
    for _ in range(3):
        part = rest.astype(np.float32).astype(ml_dtypes.bfloat16)
        parts.append(part)
        rest = rest - part.astype(np.float64)
    return np.stack(parts)


def axial_table():
    order = np.arange(NZ)
    block, rest = order // LOCAL_Z, order % LOCAL_Z
    cells = block * LOCAL_Z + 4 * (rest % 8) + rest // 8
    angle = 2.0 * np.pi * ((np.arange(NZ)[:, None] * cells[None, :]) % NZ) / NZ
    return split_table(np.concatenate([np.cos(angle), np.sin(angle)], axis=0))


def cycle_table():
    angle = 2.0 * np.pi * ((np.arange(NTH)[:, None] * np.arange(NTH)[None, :]) % NTH) / NTH
    scale = 1.0 / math.sqrt(NTH * NZ)
    cosine = (np.cos(angle) * scale).reshape(NTH, GZ_COUNT, LOCAL_M)
    sine = (np.sin(angle) * scale).reshape(NTH, GZ_COUNT, LOCAL_M)
    upper = np.stack([cosine, -sine], axis=2)
    lower = np.stack([-sine, -cosine], axis=2)
    both = np.concatenate([upper, lower], axis=0)[:, [0, 2, 1, 3, 4, 6, 5, 7]]
    both = both.reshape(2 * NTH, GZ_COUNT // 2, 4 * LOCAL_M)
    return split_table(np.moveaxis(both, 1, 0))


def split_value(value):
    parts = []
    for _ in range(3):
        part = value.astype(jnp.bfloat16)
        parts.append(part)
        value = value - part.astype(jnp.float32)
    return parts


def product(left, right):
    total = None
    for i, j in ((0, 2), (2, 0), (1, 1), (0, 1), (1, 0), (0, 0)):
        term = jnp.dot(left[i], right[j], preferred_element_type=jnp.float32)
        total = term if total is None else total + term
    return total


def spectral_part(
    tiles,
    modes,
    planes,
    plane,
    axial,
    cycle,
    left,
    spectrum,
    fetch_axial,
    fetch_cycle,
    send_sem,
    recv_sem,
    out_send_sem,
    out_recv_sem,
    own_sem,
    meanwhile,
):
    row, column = lax.axis_index("theta"), lax.axis_index("gz")
    me = row * GZ_COUNT + column

    def send_tile(i, carry):
        target = lax.rem(me + i, DEVICES)
        pltpu.make_async_remote_copy(
            src_ref=tiles.at[target],
            dst_ref=planes.at[me],
            send_sem=send_sem,
            recv_sem=recv_sem,
            device_id={"theta": target // GZ_COUNT, "gz": lax.rem(target, GZ_COUNT)},
            device_id_type=MESH_ID,
        ).start()
        return carry

    lax.fori_loop(1, DEVICES, send_tile, 0)
    planes[me] = tiles[me]
    meanwhile()
    wait_bytes(planes.at[pl.ds(0, DEVICES - 1)], recv_sem)
    wait_bytes(planes.at[pl.ds(0, DEVICES - 1)], send_sem)

    group = lax.broadcasted_iota(jnp.int32, (8, 128), 1) // LOCAL_T

    def gather_lines(c, carry):
        for quad in range(THETA_COUNT // 4):
            parts = [planes[(4 * quad + b) * GZ_COUNT + c] for b in range(4)]
            for z in range(4):
                turned = [
                    parts[b] if b == z else pltpu.roll(parts[b], ((b - z) * LOCAL_T) % 128, 1)
                    for b in range(4)
                ]
                value = jnp.where(
                    group < 2,
                    jnp.where(group == 0, turned[0], turned[1]),
                    jnp.where(group == 2, turned[2], turned[3]),
                )
                start = pl.multiple_of(c * LOCAL_Z + 8 * z, 8)
                plane[pl.ds(start, 8), 128 * quad : 128 * quad + 128] = value
        return carry

    lax.fori_loop(0, GZ_COUNT, gather_lines, 0)
    fetch_axial.wait()
    lines = product(axial, split_value(plane[...]))
    for n, part in enumerate(split_value(lines)):
        left[n, :, :NTH] = part[:NZ]
        left[n, :, NTH:] = part[NZ:]
    fetch_cycle.wait()

    def transform(step, carry):
        chunk = lax.rem(2 * (column // 4) + lax.rem(column, 2) + step, GZ_COUNT // 2)
        first = 4 * (chunk // 2) + lax.rem(chunk, 2)
        both = product(left, cycle.at[:, chunk])
        spectrum[first] = both[:, :128]
        spectrum[first + 2] = both[:, 128:]

        def send_modes(i, inner):
            target_column = first + 2 * lax.rem(i, 2)
            target_row = lax.rem(row + i // 2, THETA_COUNT)
            rows = pl.ds(pl.multiple_of(target_row * LOCAL_K, LOCAL_K), LOCAL_K)

            @pl.when(jnp.logical_or(target_row != row, target_column != column))
            def _():
                pltpu.make_async_remote_copy(
                    src_ref=spectrum.at[target_column, rows],
                    dst_ref=modes.at[me],
                    send_sem=out_send_sem,
                    recv_sem=out_recv_sem,
                    device_id={"theta": target_row, "gz": target_column},
                    device_id_type=MESH_ID,
                ).start()

            return inner

        lax.fori_loop(0, 2 * THETA_COUNT, send_modes, 0)
        return carry

    lax.fori_loop(0, GZ_COUNT // 2, transform, 0)
    own_rows = pl.ds(pl.multiple_of(row * LOCAL_K, LOCAL_K), LOCAL_K)
    keep = pltpu.make_async_copy(spectrum.at[column, own_rows], modes.at[me], own_sem)
    keep.start()
    keep.wait()
    wait_bytes(modes.at[pl.ds(0, DEVICES - 1)], out_send_sem)
    wait_bytes(modes.at[pl.ds(0, DEVICES - 1)], out_recv_sem)


def step_kernel(
    velocity,
    radial_hbm,
    axial_hbm,
    cycle_hbm,
    ratio,
    modes,
    inverse,
    radial,
    flow,
    packed,
    landed,
    corners,
    tensor,
    state,
    filtered,
    row_sums,
    all_sums,
    swirl,
    drift,
    edges,
    form,
    source,
    tiles,
    planes,
    plane,
    axial,
    cycle,
    left,
    spectrum,
    load_sem,
    send_sem,
    recv_sem,
    sum_send_sem,
    sum_recv_sem,
    face_send_sem,
    face_recv_sem,
    move_sem,
):
    fetches = [
        pltpu.make_async_copy(source_ref, target, load_sem.at[n])
        for n, (source_ref, target) in enumerate(
            ((radial_hbm, radial), (axial_hbm, axial), (cycle_hbm, cycle)), 1
        )
    ]
    start_rest, finish_axial, finish_rest = exchange(
        velocity, flow, packed, landed, corners, load_sem.at[0], send_sem, recv_sem, fetches
    )
    start_rest()
    factor_rows(inverse)
    fetches[0].wait()
    strain_rows(flow, tensor, radial, True, (3, 4))
    finish_axial()
    strain_rows(flow, tensor, radial, True, (1, 2, 5, 6))
    finish_rest()
    strain_rows(flow, tensor, radial, False, range(1, S_COLS - 1))
    numer, denom = filter_rows(flow, tensor, state, filtered, radial)

    faces = []

    def first_wait():
        face_rows(flow, tensor, swirl, drift, radial)
        faces.extend(send_faces(swirl, drift, edges, face_send_sem, face_recv_sem))

    def second_wait():
        form_rows(flow, tensor, form, radial)
        for item in faces:
            item.wait()
        join_rows(swirl, drift, edges, form, radial)

    numer, denom = sum_everywhere(
        numer,
        denom,
        row_sums,
        all_sums,
        sum_send_sem,
        sum_recv_sem,
        (first_wait, second_wait),
    )
    coefficient = (numer * (1.0 / 256.0)) / (denom * (1.0 / 256.0) + epsilon_den)
    source_rows(form, source, coefficient)
    for s in range(8):
        tiles[:, s, :] = source[s].T
    spectral_part(
        tiles,
        modes,
        planes,
        plane,
        axial,
        cycle,
        left,
        spectrum,
        fetches[1],
        fetches[2],
        *(move_sem.at[n] for n in range(5)),
        lambda: ratio_rows(tensor, ratio, radial, coefficient),
    )


def step(velocity):
    vmem = pl.BlockSpec(memory_space=pltpu.VMEM)
    hbm = pl.BlockSpec(memory_space=pltpu.HBM)
    return pl.pallas_call(
        step_kernel,
        out_shape=(
            jax.ShapeDtypeStruct((LOCAL_T, LOCAL_Z, NR), jnp.float32),
            jax.ShapeDtypeStruct((DEVICES, LOCAL_K, 128), jnp.float32),
            jax.ShapeDtypeStruct((NR, LOCAL_K, 128), jnp.float32),
        ),
        in_specs=[hbm, hbm, hbm, hbm],
        out_specs=(vmem, vmem, vmem),
        scratch_shapes=[
            pltpu.VMEM((15, 8, NR), jnp.float32),
            pltpu.VMEM((3, T_ROWS, Z_ROWS, NR), jnp.float32),
            pltpu.VMEM((2, 6, LOCAL_T, NR), jnp.float32),
            pltpu.VMEM((2, 6, LOCAL_T, NR), jnp.float32),
            pltpu.VMEM((2, 4, 3, 8, NR), jnp.float32),
            pltpu.VMEM((13, S_ROWS, S_COLS, 8, NR), jnp.float32),
            pltpu.VMEM((2, 21, Z_STEP, 8, NR), jnp.float32),
            pltpu.VMEM((21, 2 * Z_STEP, 8, NR), jnp.float32),
            pltpu.VMEM((THETA_COUNT, 8, NR), jnp.float32),
            pltpu.VMEM((GZ_COUNT, 8, NR), jnp.float32),
            pltpu.VMEM((4, LOCAL_T + 2, Z_STEP, 8, NR), jnp.float32),
            pltpu.VMEM((4, LOCAL_T + 2, Z_STEP, 8, NR), jnp.float32),
            pltpu.VMEM((2, 2, 4, LOCAL_T, NR), jnp.float32),
            pltpu.VMEM((6, LOCAL_T, Z_STEP, 8, NR), jnp.float32),
            pltpu.VMEM((8, 4 * LOCAL_T, NR), jnp.float32),
            pltpu.VMEM((NR, 8, 4 * LOCAL_T), jnp.float32),
            pltpu.VMEM((DEVICES, 8, 128), jnp.float32),
            pltpu.VMEM((NZ, NTH), jnp.float32),
            pltpu.VMEM((3, 2 * NZ, NZ), jnp.bfloat16),
            pltpu.VMEM((3, GZ_COUNT // 2, 2 * NTH, 4 * LOCAL_M), jnp.bfloat16),
            pltpu.VMEM((3, NZ, 2 * NTH), jnp.bfloat16),
            pltpu.VMEM((GZ_COUNT, NZ, 128), jnp.float32),
            pltpu.SemaphoreType.DMA((4,)),
            pltpu.SemaphoreType.DMA((8,)),
            pltpu.SemaphoreType.DMA((8,)),
            pltpu.SemaphoreType.DMA((2,)),
            pltpu.SemaphoreType.DMA((2,)),
            pltpu.SemaphoreType.DMA((4,)),
            pltpu.SemaphoreType.DMA((4,)),
            pltpu.SemaphoreType.DMA((5,)),
        ],
        compiler_params=pltpu.CompilerParams(
            collective_id=0, has_side_effects=True, vmem_limit_bytes=48 << 20
        ),
        name="step",
    )(
        *(
            pltpu.with_memory_space_constraint(jnp.asarray(value), pltpu.HBM)
            for value in (velocity, radial_table(), axial_table(), cycle_table())
        )
    )


def diagonals():
    row, column = lax.axis_index("theta"), lax.axis_index("gz")
    shape = (LOCAL_K, 128)
    theta_mode = column * LOCAL_M + lax.broadcasted_iota(jnp.int32, shape, 1) % LOCAL_M
    axial_mode = row * LOCAL_K + lax.broadcasted_iota(jnp.int32, shape, 0)
    theta_wave = jnp.minimum(theta_mode, NTH - theta_mode).astype(jnp.float32)
    axial_wave = jnp.minimum(axial_mode, NZ - axial_mode).astype(jnp.float32) * (
        2.0 * math.pi / pipe_length
    )
    theta_sq = theta_wave * theta_wave
    axial_sq = axial_wave * axial_wave * (1.0 / (NR * NR))

    def diagonal(i):
        middle = i + 0.5
        extra = float(NR) if i == NR - 1 else 0.0
        return theta_sq * (1.0 / middle) + (axial_sq * middle + (2.0 * i + 1.0 + extra))

    return diagonal


def factor_rows(inverse):
    diagonal = diagonals()
    low, high = diagonal(0), diagonal(NR - 1)
    for i in range(1, HALF):
        j = NR - 1 - i
        low_inverse, high_inverse = 1.0 / low, 1.0 / high
        inverse[i - 1] = low_inverse
        inverse[j + 1] = high_inverse
        low = diagonal(i) - low_inverse * float(i * i)
        high = diagonal(j) - high_inverse * float((j + 1) * (j + 1))
    inverse[HALF - 1] = low
    inverse[HALF] = high


def solve_kernel(
    modes, inverse, ratio_ref, out_hbm, ratio_out, partial, pressure, turned, ratio_sem, out_sem
):
    keep = pltpu.make_async_copy(ratio_ref, ratio_out, ratio_sem)
    keep.start()

    def load(i):
        return modes[i] * (-(i + 0.5) / (NR * NR))

    low, high = load(0), load(NR - 1)
    for i in range(1, HALF):
        j = NR - 1 - i
        partial[i - 1] = low
        partial[j + 1] = high
        low = load(i) + (inverse[i - 1] * float(i)) * low
        high = load(j) + (inverse[j + 1] * float(j + 1)) * high
    top, bottom = inverse[HALF - 1], inverse[HALF]
    scale = 1.0 / (top * bottom - float(HALF * HALF))
    low, high = (
        (low * bottom + float(HALF) * high) * scale,
        (high * top + float(HALF) * low) * scale,
    )
    pressure[HALF - 1] = low
    pressure[HALF] = high
    for step in range(1, HALF):
        i, j = HALF - 1 - step, HALF + step
        low = (partial[i] + float(i + 1) * low) * inverse[i]
        high = (partial[j] + float(j) * high) * inverse[j]
        pressure[i] = low
        pressure[j] = high
    copies = [keep]
    for half in range(LOCAL_K // 8):
        rows = pl.ds(8 * half, 8)
        for k in range(8 * half, 8 * half + 8):
            turned[:, k, :] = pressure[:, k, :].T
        item = pltpu.make_async_copy(turned.at[:, rows], out_hbm.at[:, rows], out_sem.at[half])
        item.start()
        copies.append(item)
    for item in copies:
        item.wait()


def solve(modes, inverse, ratio):
    vmem = pl.BlockSpec(memory_space=pltpu.VMEM)
    anywhere = pl.BlockSpec(memory_space=pl.ANY)
    pressure, ratio = pl.pallas_call(
        solve_kernel,
        out_shape=(
            jax.ShapeDtypeStruct((2 * LOCAL_M, LOCAL_K, NR), jnp.float32),
            jax.ShapeDtypeStruct((LOCAL_T, LOCAL_Z, NR), jnp.float32),
        ),
        in_specs=[vmem, vmem, anywhere],
        out_specs=(pl.BlockSpec(memory_space=pltpu.HBM), pl.BlockSpec(memory_space=pltpu.HBM)),
        scratch_shapes=[pltpu.VMEM((NR, LOCAL_K, 128), jnp.float32)] * 2
        + [
            pltpu.VMEM((2 * LOCAL_M, LOCAL_K, NR), jnp.float32),
            pltpu.SemaphoreType.DMA,
            pltpu.SemaphoreType.DMA((LOCAL_K // 8,)),
        ],
        compiler_params=pltpu.CompilerParams(vmem_limit_bytes=32 << 20),
        name="solve",
    )(modes, inverse, ratio)
    return ratio, pressure.reshape(2, LOCAL_M, LOCAL_K, NR)


def body(velocity):
    ratio, modes, inverse = step(velocity)
    return solve(modes, inverse, ratio)


def solution(mesh):
    return jax.shard_map(
        body,
        mesh=mesh,
        in_specs=(P(None, "theta", "gz", None),),
        out_specs=(P("theta", "gz", None), P(None, "gz", "theta", None)),
        check_vma=False,
    )
```
